32 devices in a mesh: dp: 4 (over z), expert: 8 (over y, x, core).
Axes of the slice: x: 2, y: 2, z: 4, core: 2. Of those that a mesh axis runs over, the one named last changes fastest.
Arguments:
- tokens: bfloat16 [32768, 768], P(('dp', 'expert')), may hold values from -6 to 6
- lengths: int32 [32], P(('dp', 'expert')), may hold values from 128 to 1024, as said below
- expert_index: int32 [32768], P(('dp', 'expert')), may hold values from 0 to 7, as said below
- centroids: float32 [8, 768], replicated, may hold values from -0.15625 to 0.15625
- input_weight: bfloat16 [768, 2304], replicated, may hold values from -0.3125 to 0.3125
- output_weight: bfloat16 [768, 768], replicated, may hold values from -0.875 to 0.875
- first_gain: float32 [768], replicated, may hold values from 0.5 to 1.5
- first_shift: float32 [768], replicated, may hold values from -1 to 1
- second_gain: float32 [768], replicated, may hold values from 0.5 to 1.5
- second_shift: float32 [768], replicated, may hold values from -1 to 1
- up_weight: bfloat16 [8, 768, 3072], P('expert'), may hold values from -0.21875 to 0.21875
- down_weight: bfloat16 [8, 3072, 768], P('expert'), may hold values from -0.3125 to 0.3125
- cotangent: bfloat16 [32768, 768], P(('dp', 'expert')), may hold values from -6 to 6
Outputs:
- layer_output: bfloat16 [32768, 768], P(('dp', 'expert'))
- input_gradient: bfloat16 [32768, 768], P(('dp', 'expert'))
- input_weight_gradient: float32 [768, 2304], P('dp')
- output_weight_gradient: float32 [768, 768], P('dp')
- first_gain_gradient: float32 [768], P('dp')
- first_shift_gradient: float32 [768], P('dp')
- second_gain_gradient: float32 [768], P('dp')
- second_shift_gradient: float32 [768], P('dp')
- up_weight_gradient: float32 [8, 768, 3072], P('expert', 'dp')
- down_weight_gradient: float32 [8, 3072, 768], P('expert', 'dp')
The draws below stay inside these ranges and needn't reach their ends.
Inputs may be any that keep to these rules, and one draw needn't show every extreme that they name: `lengths`: some sequence has exactly 1024 live positions. `expert_index`: in each aligned block of 1024 rows (the sequences of one device), at most 128 rows inside their sequence's length name any one expert, and one expert, the same in every block, is named by exactly 128 of them.
All inputs are finite; a program needn't handle non-finite values.
Results may differ from the reference program's by a relative error of at most 0.015.
Values may be sent and summed in bfloat16 or wider, within the bound.
No kernel may reach another device: no remote copies, remote signals or barrier semaphores. Data moves between devices by JAX's collectives and lax.ppermute only.
A program may use at most 256 MiB of HBM per device.

```python
import jax
import jax.numpy as jnp
from jax import lax

D = 768
HEADS = 12
HD = 64
FF = 3072
SPECIALIST_COUNT = 8
LEN = 1024
MIN_LEN = 128
SEQ_DEV = 1
DEVICE_WORD_CAP = 1024
SEQS = 32
TOKENS = 32768
CAP = 128


def shared_lengths(key):
    starting_shift = jax.random.fold_in(key, 11)
    drawn = jax.random.randint(jax.random.fold_in(starting_shift, 1), (SEQS,), MIN_LEN, LEN + 1)
    longest = jax.random.randint(jax.random.fold_in(starting_shift, 2), (), 0, SEQS)
    return drawn.at[longest].set(LEN).astype(jnp.int32)


def draw_lengths(key, part):
    return shared_lengths(key)


def draw_expert_index(key, part):
    lengths = shared_lengths(key)
    blocks = SEQS // SEQ_DEV
    starting_shift = jax.random.fold_in(key, 23)
    hottest = jax.random.randint(jax.random.fold_in(starting_shift, 1), (), 0, SPECIALIST_COUNT)
    additional_reward = jax.random.randint(jax.random.fold_in(starting_shift, 2), (SPECIALIST_COUNT,), 1, 3 * DEVICE_WORD_CAP)
    position_within_bucket = jnp.arange(DEVICE_WORD_CAP, dtype=jnp.int32)
    assigned_specialist = position_within_bucket // CAP
    damping_multiplier = (assigned_specialist != hottest).astype(jnp.int32)
    stochastic_jitter = jax.random.randint(jax.random.fold_in(starting_shift, 3), (blocks, DEVICE_WORD_CAP), 0, DEVICE_WORD_CAP)
    ordering_criteria = damping_multiplier[None, :] * (additional_reward[assigned_specialist][None, :] + stochastic_jitter) * DEVICE_WORD_CAP + position_within_bucket[None, :]
    order = jnp.argsort(ordering_criteria, axis=1)
    sorted_owner = assigned_specialist[order]
    inside = (position_within_bucket % LEN)[None, :] < lengths.reshape(blocks, SEQ_DEV)[:, position_within_bucket // LEN]
    shuffle = jax.random.randint(jax.random.fold_in(starting_shift, 4), (blocks, DEVICE_WORD_CAP), 0, DEVICE_WORD_CAP) * DEVICE_WORD_CAP + position_within_bucket[None, :]
    rank_keys = (1 - inside.astype(jnp.int32)) * (DEVICE_WORD_CAP * DEVICE_WORD_CAP) + shuffle
    ranks = jnp.argsort(jnp.argsort(rank_keys, axis=1), axis=1)
    return jnp.take_along_axis(sorted_owner, ranks, axis=1).reshape(-1).astype(jnp.int32)


def shard_levels(stream_key, dims, cuts, least, largest):
    level, own = 1.0, jax.random.fold_in(stream_key, 6)
    for axis_at, parts in cuts:
        steps = jnp.exp(jax.random.uniform(jax.random.fold_in(own, axis_at), (parts,), jnp.float32, least / len(cuts), largest / len(cuts)))
        level = level * jnp.repeat(steps, dims[axis_at] // parts).reshape([-1 if axis == axis_at else 1 for axis in range(len(dims))])
    return level


def scatter_about(key, shape, width, most, shards=(), kind=jnp.bfloat16):
    values = width * jax.random.normal(key, shape, jnp.float32)
    if shards:
        values = values * shard_levels(key, shape, shards, -0.22, 0.18)
    return jnp.clip(values, -most, most).astype(kind)


def setup_inputs(seed: int = 0) -> dict:
    arg_keys = jax.random.split(jax.random.key(seed), 14)
    tokens = scatter_about(arg_keys[0], (TOKENS, D), 1.0, 6.0, ((0, 32),))
    lengths = draw_lengths(jax.random.fold_in(arg_keys[13], 71), 0)
    expert_index = draw_expert_index(jax.random.fold_in(arg_keys[13], 71), 0)
    centroids = scatter_about(arg_keys[3], (SPECIALIST_COUNT, D), (2 * D) ** -0.5, 0.15625, (), jnp.float32)
    input_weight = scatter_about(arg_keys[4], (D, 3 * D), (D // 2) ** -0.5, 0.3125)
    output_weight = scatter_about(arg_keys[5], (D, D), (D // 16) ** -0.5, 0.875)
    first_gain = jnp.clip(1.0 + 0.1 * jax.random.normal(arg_keys[6], (D,), jnp.float32), 0.5, 1.5)
    first_shift = scatter_about(arg_keys[7], (D,), 0.2, 1.0, (), jnp.float32)
    second_gain = jnp.clip(1.0 + 0.1 * jax.random.normal(arg_keys[8], (D,), jnp.float32), 0.5, 1.5)
    second_shift = scatter_about(arg_keys[9], (D,), 0.2, 1.0, (), jnp.float32)
    up_weight = scatter_about(arg_keys[10], (SPECIALIST_COUNT, D, FF), D ** -0.5, 0.21875, ((0, 8),))
    down_weight = scatter_about(arg_keys[11], (SPECIALIST_COUNT, FF, D), (FF // 8) ** -0.5, 0.3125, ((0, 8),))
    cotangent = scatter_about(arg_keys[12], (TOKENS, D), 1.0, 6.0, ((0, 32),))
    return {"tokens": tokens, "lengths": lengths, "expert_index": expert_index, "centroids": centroids, "input_weight": input_weight, "output_weight": output_weight, "first_gain": first_gain, "first_shift": first_shift, "second_gain": second_gain, "second_shift": second_shift, "up_weight": up_weight, "down_weight": down_weight, "cotangent": cotangent}


@jax.custom_vjp
def low(v):
    return lax.optimization_barrier(v.astype(jnp.bfloat16)).astype(jnp.float32)

@jax.custom_vjp
def low_back(v):
    return v

def low_keep(v):
    return (low(v), None)

def low_pass(kept, grad):
    return (grad,)

def back_keep(v):
    return (v, None)

def back_low(kept, grad):
    return (low(grad),)
low.defvjp(low_keep, low_pass)
low_back.defvjp(back_keep, back_low)
highest = lax.Precision.HIGHEST
epsilon = 1e-05

def matmul(left, right):
    return jnp.dot(left, right, precision=highest, preferred_element_type=jnp.float32)

def both_ways(values):
    return low_back(low(values))

def layer_norm(values, norm_gain, norm_shift):
    average = lax.optimization_barrier(jnp.mean(values, axis=-1, keepdims=True))
    centred = values - average
    variance = lax.optimization_barrier(jnp.mean(centred * centred, axis=-1, keepdims=True))
    return centred * lax.rsqrt(variance + epsilon) * norm_gain + norm_shift

def routing(lengths, expert_index):
    blocks = TOKENS // DEVICE_WORD_CAP
    positions = jnp.arange(TOKENS, dtype=jnp.int32)
    present = positions % LEN < lengths[positions // LEN]
    onehot = (expert_index[:, None] == jnp.arange(SPECIALIST_COUNT, dtype=jnp.int32)[None, :]) & present[:, None]
    counts = jnp.cumsum(onehot.reshape(blocks, DEVICE_WORD_CAP, SPECIALIST_COUNT).astype(jnp.int32), axis=1).reshape(TOKENS, SPECIALIST_COUNT)
    slot = lax.optimization_barrier(jnp.sum(jnp.where(onehot, counts - 1, 0), axis=1)).astype(jnp.int32)
    per_expert = blocks * CAP
    sink = SPECIALIST_COUNT * per_expert
    target = jnp.where(present, expert_index * per_expert + positions // DEVICE_WORD_CAP * CAP + slot, sink).astype(jnp.int32)
    table = jnp.full((sink + 1,), TOKENS, jnp.int32).at[target].set(positions)
    return (present, target, table[:sink].reshape(SPECIALIST_COUNT, per_expert))

def attend(pieces):
    query, key_rows, value_rows, length = pieces
    rows = jnp.arange(LEN, dtype=jnp.int32)
    allowed = (rows[None, :] <= rows[:, None]) & (rows[None, :] < length)
    scores = low_back(jnp.einsum('qhd,khd->hqk', query, key_rows, precision=highest) * HD ** (-0.5))
    scores = jnp.where(allowed[None], scores, -1e+30)
    top = lax.optimization_barrier(jnp.max(scores, axis=-1, keepdims=True))
    weights = jnp.exp(scores - top)
    probs = weights / lax.optimization_barrier(jnp.sum(weights, axis=-1, keepdims=True))
    return jnp.einsum('hqk,khd->qhd', low(probs), value_rows, precision=highest)

def forward(present, target, table, lengths, expert_index, centroids, tokens, input_weight, output_weight, first_gain, first_shift, second_gain, second_shift, up_weight, down_weight):
    sequences = TOKENS // LEN
    row_mask = present.astype(jnp.float32)[:, None]
    normed = low(layer_norm(tokens, first_gain, first_shift))
    projected = matmul(normed, input_weight)
    queries = both_ways(projected[:, :D]).reshape(sequences, LEN, HEADS, HD)
    keys = both_ways(projected[:, D:2 * D]).reshape(sequences, LEN, HEADS, HD)
    values = both_ways(projected[:, 2 * D:]).reshape(sequences, LEN, HEADS, HD)
    mixed = lax.map(jax.checkpoint(attend), (queries, keys, values, lengths))
    mixed = both_ways(mixed.reshape(TOKENS, D))
    branch = low_back(matmul(mixed, output_weight))
    residual = tokens + row_mask * branch
    hidden = layer_norm(residual, second_gain, second_shift)
    routed = both_ways(hidden)
    gate = jax.nn.sigmoid(lax.optimization_barrier(jnp.sum(hidden * centroids[expert_index], axis=-1)))[:, None]
    padded = jnp.concatenate([routed, jnp.zeros((1, D), jnp.float32)], axis=0)

    def expert_rows(pieces):
        rows_index, up_matrix, down_matrix = pieces
        upper = low_back(matmul(padded[rows_index], up_matrix))
        active = low(jax.nn.gelu(upper, approximate=False))
        return both_ways(matmul(active, down_matrix))
    produced = lax.map(jax.checkpoint(expert_rows), (table, up_weight, down_weight))
    produced = jnp.concatenate([produced.reshape(-1, D), jnp.zeros((1, D), jnp.float32)], axis=0)[target]
    return residual + row_mask * gate * produced

def reference(tokens, lengths, expert_index, centroids, input_weight, output_weight, first_gain, first_shift, second_gain, second_shift, up_weight, down_weight, cotangent):
    present, target, table = routing(lengths, expert_index)

    def layer(*weights):
        return forward(present, target, table, lengths, expert_index, centroids, *weights)
    result, pullback = jax.vjp(layer, tokens.astype(jnp.float32), input_weight.astype(jnp.float32), output_weight.astype(jnp.float32), first_gain, first_shift, second_gain, second_shift, up_weight.astype(jnp.float32), down_weight.astype(jnp.float32))
    gradients = pullback(cotangent.astype(jnp.float32))
    return (result.astype(jnp.bfloat16), gradients[0].astype(jnp.bfloat16), gradients[1], gradients[2], gradients[3], gradients[4], gradients[5], gradients[6], gradients[7], gradients[8])
```

```python
import functools

import jax
import jax.numpy as jnp
from jax import lax
from jax.experimental import pallas as pl
from jax.experimental.pallas import tpu as pltpu
from jax.sharding import PartitionSpec as P

HEADS = 12
EPS = 1e-05
EXCLUDED = -1e30
BF = jnp.bfloat16
F32 = jnp.float32
QUERY_ROWS = 256
GAIN_ROWS = 64


def dot(left, right, left_axis=1, right_axis=0):
    return lax.dot_general(
        left,
        right,
        (((left_axis,), (right_axis,)), ((), ())),
        preferred_element_type=F32,
    )


def params(limit=60):
    return pltpu.CompilerParams(vmem_limit_bytes=limit << 20)


def cost(flops, bytes_accessed, transcendentals=0):
    return pl.CostEstimate(
        flops=int(flops), bytes_accessed=int(bytes_accessed), transcendentals=int(transcendentals)
    )


def split_three(values):
    high = values.astype(BF)
    rest = values - high.astype(F32)
    middle = rest.astype(BF)
    return high, middle, (rest - middle.astype(F32)).astype(BF)


def normalise(values):
    average = jnp.mean(values, axis=-1, keepdims=True)
    centred = values - average
    variance = jnp.mean(centred * centred, axis=-1, keepdims=True)
    inverse = lax.rsqrt(variance + EPS)
    return centred * inverse, inverse


def norm_backward(normal, inverse, gain, gradient):
    scaled = gain * gradient
    first = jnp.mean(scaled, axis=-1, keepdims=True)
    second = jnp.mean(scaled * normal, axis=-1, keepdims=True)
    return (scaled - first - normal * second) * inverse


def selection(target_row, first, count):
    rows = lax.broadcasted_iota(jnp.int32, (count, target_row.shape[1]), 0) + first
    return jnp.where(rows == target_row, 1.0, 0.0).astype(BF)


def route_kernel(length_ref, expert_ref, cotangent_ref, out_ref, row_ref, column_ref, *, experts):
    step = pl.program_id(0)
    rows = cotangent_ref.shape[0]
    block = out_ref.shape[0]

    @pl.when(step == 0)
    def _():
        length = length_ref[0]
        position = lax.broadcasted_iota(jnp.int32, (1, rows), 1)
        named = jnp.where(position < length, expert_ref[...], -1)
        number = lax.broadcasted_iota(jnp.int32, (experts, rows), 0)
        onehot = jnp.where(number == named, 1.0, 0.0)
        before = lax.broadcasted_iota(jnp.int32, (rows, rows), 0)
        after = lax.broadcasted_iota(jnp.int32, (rows, rows), 1)
        earlier = jnp.where(before < after, 1.0, 0.0).astype(BF)
        counts = dot(onehot.astype(BF), earlier)
        slots = counts + (number * (rows // experts)).astype(F32)
        target = jnp.sum(onehot * slots, axis=0, keepdims=True)
        target = jnp.where(named >= 0, target, -1.0)
        row_ref[...] = jnp.broadcast_to(target, row_ref.shape).astype(jnp.int32)
        column_ref[...] = jnp.broadcast_to(target, (128, rows)).T.astype(jnp.int32)

    chosen = selection(row_ref[0:1, :], step * block, block)
    out_ref[...] = dot(chosen, cotangent_ref[...]).astype(BF)


def route(length, expert_index, cotangent, experts):
    rows, width = cotangent.shape
    block = 256
    return pl.pallas_call(
        functools.partial(route_kernel, experts=experts),
        out_shape=[
            jax.ShapeDtypeStruct((rows, width), BF),
            jax.ShapeDtypeStruct((8, rows), jnp.int32),
            jax.ShapeDtypeStruct((rows, 128), jnp.int32),
        ],
        grid_spec=pltpu.PrefetchScalarGridSpec(
            num_scalar_prefetch=1,
            grid=(rows // block,),
            in_specs=[
                pl.BlockSpec((1, rows), lambda i, l: (0, 0)),
                pl.BlockSpec((rows, width), lambda i, l: (0, 0)),
            ],
            out_specs=[
                pl.BlockSpec((block, width), lambda i, l: (i, 0)),
                pl.BlockSpec((8, rows), lambda i, l: (0, 0)),
                pl.BlockSpec((rows, 128), lambda i, l: (0, 0)),
            ],
        ),
        compiler_params=params(),
        cost_estimate=cost(2 * rows * rows * width, 4 * rows * width),
        name="route",
    )(length, expert_index.reshape(1, rows), cotangent)


def project_kernel(tokens_ref, weight_ref, gain_ref, shift_ref, out_ref):
    normal, _ = normalise(tokens_ref[...].astype(F32))
    normed = (normal * gain_ref[...] + shift_ref[...]).astype(BF)
    out_ref[...] = dot(normed, weight_ref[...]).astype(BF)


def project(tokens, weight, gain, shift):
    rows, width = tokens.shape
    columns = weight.shape[1]
    block = 256
    return pl.pallas_call(
        project_kernel,
        out_shape=jax.ShapeDtypeStruct((rows, columns), BF),
        grid=(rows // block,),
        in_specs=[
            pl.BlockSpec((block, width), lambda i: (i, 0)),
            pl.BlockSpec((width, columns), lambda i: (0, 0)),
            pl.BlockSpec((1, width), lambda i: (0, 0)),
            pl.BlockSpec((1, width), lambda i: (0, 0)),
        ],
        out_specs=pl.BlockSpec((block, columns), lambda i: (i, 0)),
        compiler_params=params(),
        cost_estimate=cost(2 * rows * width * columns, 2 * (rows + width) * columns),
        name="project",
    )(tokens, weight, gain, shift)


def attend_kernel(length_ref, query_ref, key_ref, value_ref, mixed_ref, total_ref, *, scale, half):
    rows = query_ref.shape[0]
    lane = lax.broadcasted_iota(jnp.int32, (1, 2 * half), 1)
    length = length_ref[0]
    zero, one = jnp.zeros((), BF), jnp.ones((), BF)
    for begin in range(0, rows, QUERY_ROWS):
        end = begin + QUERY_ROWS

        @pl.when(begin < length)
        def _(begin=begin, end=end):
            row = lax.broadcasted_iota(jnp.int32, (QUERY_ROWS, 1), 0) + begin
            limit = jnp.minimum(row, length - 1)
            column = lax.broadcasted_iota(jnp.int32, (QUERY_ROWS, QUERY_ROWS), 1) + begin
            allowed = column <= limit
            outs, totals = [], []
            for head in range(2):
                mine = (lane // half) == head
                other = half * (1 - head)
                query = jnp.where(mine, query_ref[begin:end, :] * jnp.asarray(scale, BF), zero)
                value = jnp.where(mine, value_ref[:end, :], jnp.where(lane == other, one, zero))
                scores = dot(query, key_ref[:end, :], 1, 1)
                last = jnp.where(allowed, scores[:, begin:], EXCLUDED)
                scores = jnp.concatenate([scores[:, :begin], last], axis=1) if begin else last
                top = jnp.max(scores, axis=1, keepdims=True)
                weights = jnp.exp(scores - top).astype(BF)
                out = dot(weights, value)
                total = out[:, other : other + 1]
                outs.append(out / total)
                totals.append(top + jnp.log(total))
            first = lane < half
            mixed_ref[begin:end, :] = jnp.where(first, outs[0], outs[1]).astype(BF)
            total_ref[begin:end, :] = jnp.where(first, totals[0], totals[1])

        @pl.when(begin >= length)
        def _(begin=begin, end=end):
            mixed_ref[begin:end, :] = jnp.zeros((QUERY_ROWS, 2 * half), BF)
            total_ref[begin:end, :] = jnp.zeros((QUERY_ROWS, 2 * half), F32)


def pair_specs(rows, wide, pairs, thirds):
    return [pl.BlockSpec((rows, wide), lambda i, l, o=o: (0, i + o * pairs)) for o in range(thirds)]


def attend(length, projected):
    rows, width = projected.shape[0], projected.shape[1] // 3
    size = width // HEADS
    pairs = HEADS // 2
    one = pl.BlockSpec((rows, 2 * size), lambda i, l: (0, i))
    return pl.pallas_call(
        functools.partial(attend_kernel, scale=size**-0.5, half=size),
        out_shape=[
            jax.ShapeDtypeStruct((rows, width), BF),
            jax.ShapeDtypeStruct((rows, width), F32),
        ],
        grid_spec=pltpu.PrefetchScalarGridSpec(
            num_scalar_prefetch=1,
            grid=(pairs,),
            in_specs=pair_specs(rows, 2 * size, pairs, 3),
            out_specs=[one, one],
        ),
        compiler_params=params(),
        cost_estimate=cost(
            16 * rows * rows * width, 12 * rows * width, HEADS * rows * rows // 2
        ),
        name="attend",
    )(length, projected, projected, projected)


def attend_back_kernel(
    length_ref,
    query_ref,
    key_ref,
    value_ref,
    mixed_ref,
    total_ref,
    incoming_ref,
    query_out,
    key_out,
    value_out,
    key_sum,
    value_sum,
    *,
    scale,
    half,
):
    rows = query_ref.shape[0]
    lane = lax.broadcasted_iota(jnp.int32, (1, 2 * half), 1)
    length = length_ref[0]
    zero, one = jnp.zeros((), BF), jnp.ones((), BF)
    key_sum[...] = jnp.zeros_like(key_sum)
    value_sum[...] = jnp.zeros_like(value_sum)
    for begin in range(0, rows, QUERY_ROWS):
        end = begin + QUERY_ROWS

        @pl.when(begin < length)
        def _(begin=begin, end=end):
            row = lax.broadcasted_iota(jnp.int32, (QUERY_ROWS, 1), 0) + begin
            column = lax.broadcasted_iota(jnp.int32, (QUERY_ROWS, QUERY_ROWS), 1) + begin
            allowed = (row <= column) & (row < length)
            incoming = incoming_ref[begin:end, :]
            product = incoming.astype(F32) * mixed_ref[begin:end, :].astype(F32)
            query_gradient = None
            for head in range(2):
                mine = (lane // half) == head
                other = half * (1 - head)
                ones = jnp.where((lane >= other) & (lane < other + 3), one, zero)

                def extend(base, column, mine=mine, other=other):
                    a, b, c = split_three(-column)
                    rest = jnp.where(lane == other + 2, c, zero)
                    rest = jnp.where(lane == other + 1, b, rest)
                    return jnp.where(mine, base, jnp.where(lane == other, a, rest))

                query = jnp.where(mine, query_ref[begin:end, :] * jnp.asarray(scale, BF), zero)
                grad = jnp.where(mine, incoming, zero)
                inner = jnp.sum(jnp.where(mine, product, 0.0), axis=1, keepdims=True)
                total = total_ref[begin:end, head * half : head * half + 1]
                key = key_ref[:end, :]
                scores = dot(jnp.where(mine, key, ones), extend(query, total), 1, 1)
                last = jnp.where(allowed, scores[begin:, :], EXCLUDED)
                scores = jnp.concatenate([scores[:begin, :], last], axis=0) if begin else last
                probs = jnp.exp(scores)
                centred = dot(
                    jnp.where(mine, value_ref[:end, :], ones), extend(grad, inner), 1, 1
                )
                score_gradient = (probs * centred).astype(BF)
                value_sum[:end, :] += dot(probs.astype(BF), grad)
                key_sum[:end, :] += dot(score_gradient, query)
                part = dot(score_gradient, jnp.where(mine, key, zero), 0, 0)
                query_gradient = part if query_gradient is None else query_gradient + part
            query_out[begin:end, :] = (query_gradient * scale).astype(BF)

        @pl.when(begin >= length)
        def _(begin=begin, end=end):
            query_out[begin:end, :] = jnp.zeros((QUERY_ROWS, 2 * half), BF)

    key_out[...] = key_sum[...].astype(BF)
    value_out[...] = value_sum[...].astype(BF)


def attend_back(length, projected, mixed, total, incoming):
    rows, width = projected.shape[0], projected.shape[1] // 3
    size = width // HEADS
    pairs = HEADS // 2
    one = pl.BlockSpec((rows, 2 * size), lambda i, l: (0, i))
    return pl.pallas_call(
        functools.partial(attend_back_kernel, scale=size**-0.5, half=size),
        out_shape=[jax.ShapeDtypeStruct((rows, width), BF)] * 3,
        grid_spec=pltpu.PrefetchScalarGridSpec(
            num_scalar_prefetch=1,
            grid=(pairs,),
            in_specs=pair_specs(rows, 2 * size, pairs, 3) + [one] * 3,
            out_specs=[one] * 3,
            scratch_shapes=[pltpu.VMEM((rows, 2 * size), F32)] * 2,
        ),
        compiler_params=params(),
        cost_estimate=cost(
            30 * rows * rows * width, 20 * rows * width, HEADS * rows * rows // 2
        ),
        name="attend_back",
    )(length, projected, projected, projected, mixed, total, incoming)


def picked_rows(column_ref, centroids_ref, capacity):
    experts, width = centroids_ref.shape
    pieces = [piece.astype(F32) for piece in split_three(centroids_ref[...])]
    rest = jnp.zeros((128 - 3 * experts, width), F32)
    table = jnp.concatenate(pieces + [rest], axis=0).astype(BF)
    target = column_ref[...]
    lane = lax.broadcasted_iota(jnp.int32, (1, 128), 1)
    low = jnp.where(lane < 3 * experts, (lane % experts) * capacity, 1 << 20)
    onehot = jnp.where((target >= low) & (target < low + capacity), 1.0, 0.0).astype(BF)
    return dot(onehot, table)


def present_rows(block_index, count, length):
    row = lax.broadcasted_iota(jnp.int32, (count, 1), 0) + block_index * count
    return jnp.where(row < length, 1.0, 0.0)


def hidden_kernel(
    length_ref,
    mixed_ref,
    tokens_ref,
    weight_ref,
    gain_ref,
    shift_ref,
    centroids_ref,
    row_ref,
    column_ref,
    residual_ref,
    gate_ref,
    out_ref,
    hidden_low,
    *,
    blocks,
):
    step = pl.program_id(0)
    count = mixed_ref.shape[0]

    @pl.when(step < blocks)
    def _():
        branch = dot(mixed_ref[...], weight_ref[...])
        mask = present_rows(step, count, length_ref[0])
        residual = tokens_ref[...].astype(F32) + mask * branch
        residual_ref[...] = residual
        normal, _ = normalise(residual)
        hidden = normal * gain_ref[...] + shift_ref[...]
        picked = picked_rows(column_ref, centroids_ref, row_ref.shape[1] // centroids_ref.shape[0])
        gate = jax.nn.sigmoid(jnp.sum(hidden * picked, axis=-1, keepdims=True))
        gate_ref[...] = jnp.broadcast_to(gate, gate_ref.shape)
        hidden_low[pl.ds(pl.multiple_of(step * count, count), count), :] = hidden.astype(BF)

    @pl.when(step >= blocks)
    def _():
        chosen = selection(row_ref[0:1, :], (step - blocks) * count, count)
        out_ref[...] = dot(chosen, hidden_low[...]).astype(BF)


def hidden_rows(length, mixed, tokens, weight, gain, shift, centroids, target_row, target_column):
    rows, width = tokens.shape
    experts = centroids.shape[0]
    block = 256
    blocks = rows // block
    early = lambda i, l: (jnp.minimum(i, blocks - 1), 0)
    late = lambda i, l: (jnp.maximum(i - blocks, 0), 0)
    still = lambda i, l: (0, 0)
    return pl.pallas_call(
        functools.partial(hidden_kernel, blocks=blocks),
        out_shape=[
            jax.ShapeDtypeStruct((rows, width), F32),
            jax.ShapeDtypeStruct((rows, 128), F32),
            jax.ShapeDtypeStruct((rows, width), BF),
        ],
        grid_spec=pltpu.PrefetchScalarGridSpec(
            num_scalar_prefetch=1,
            grid=(2 * blocks,),
            in_specs=[
                pl.BlockSpec((block, width), early),
                pl.BlockSpec((block, width), early),
                pl.BlockSpec((width, width), still),
                pl.BlockSpec((1, width), still),
                pl.BlockSpec((1, width), still),
                pl.BlockSpec((experts, width), still),
                pl.BlockSpec((8, rows), still),
                pl.BlockSpec((block, 128), early),
            ],
            out_specs=[
                pl.BlockSpec((block, width), early),
                pl.BlockSpec((block, 128), early),
                pl.BlockSpec((block, width), late),
            ],
            scratch_shapes=[pltpu.VMEM((rows, width), BF)],
        ),
        compiler_params=params(),
        cost_estimate=cost(2 * rows * (rows + width) * width, 12 * rows * width),
        name="hidden_rows",
    )(length, mixed, tokens, weight, gain, shift, centroids, target_row, target_column)


def expert_kernel(
    rows_ref,
    cotangent_ref,
    centroid_ref,
    up_ref,
    down_ref,
    produced_ref,
    back_ref,
    down_grad_ref,
    up_grad_ref,
    produced_sum,
    back_sum,
    transposed,
    gradient,
):
    step = pl.program_id(0)

    @pl.when(step == 0)
    def _():
        hidden = rows_ref[...]
        transposed[...] = hidden.T
        logit = jnp.sum(hidden.astype(F32) * centroid_ref[...], axis=-1, keepdims=True)
        gate = jax.nn.sigmoid(logit)
        gradient[...] = (gate * cotangent_ref[...].astype(F32)).astype(BF)
        produced_sum[...] = jnp.zeros_like(produced_sum)
        back_sum[...] = jnp.zeros_like(back_sum)

    upper = dot(rows_ref[...], up_ref[...])
    share = 0.5 + 0.5 * lax.erf(upper * (0.5**0.5))
    density = jnp.exp(upper * upper * -0.5) * 0.3989422804014327
    active = (upper * share).astype(BF)
    slope = share + upper * density
    active_gradient = dot(gradient[...], down_ref[...], 1, 1)
    upper_gradient = (active_gradient * slope).astype(BF)
    produced_sum[...] += dot(active, down_ref[...])
    down_grad_ref[...] = dot(active, gradient[...], 0, 0).astype(BF)
    back_sum[...] += dot(upper_gradient, up_ref[...], 1, 1)
    up_grad_ref[...] = dot(transposed[...], upper_gradient).astype(BF)

    @pl.when(step == pl.num_programs(0) - 1)
    def _():
        produced_ref[...] = produced_sum[...].astype(BF)
        back_ref[...] = back_sum[...].astype(BF)


def expert(rows, cotangent, centroid, up, down):
    count, width = rows.shape
    inner = up.shape[1]
    chunk = 512
    whole = pl.BlockSpec((count, width), lambda c: (0, 0))
    tall = pl.BlockSpec((chunk, width), lambda c: (c, 0))
    wide = pl.BlockSpec((width, chunk), lambda c: (0, c))
    return pl.pallas_call(
        expert_kernel,
        out_shape=[
            jax.ShapeDtypeStruct((count, width), BF),
            jax.ShapeDtypeStruct((count, width), BF),
            jax.ShapeDtypeStruct((inner, width), BF),
            jax.ShapeDtypeStruct((width, inner), BF),
        ],
        grid=(inner // chunk,),
        in_specs=[whole, whole, pl.BlockSpec((1, width), lambda c: (0, 0)), wide, tall],
        out_specs=[whole, whole, tall, wide],
        scratch_shapes=[
            pltpu.VMEM((count, width), F32),
            pltpu.VMEM((count, width), F32),
            pltpu.VMEM((width, count), BF),
            pltpu.VMEM((count, width), BF),
        ],
        compiler_params=params(),
        cost_estimate=cost(12 * count * width * inner, 8 * inner * width, 2 * count * inner),
        name="expert",
    )(rows, cotangent, centroid, up, down)


def combine_kernel(
    length_ref,
    produced_ref,
    back_ref,
    column_ref,
    cotangent_ref,
    residual_ref,
    gate_ref,
    gain_ref,
    centroids_ref,
    mixed_ref,
    weight_ref,
    layer_ref,
    residual_grad_ref,
    mixed_grad_ref,
    weight_grad_ref,
    gains_ref,
    weight_sum,
):
    step = pl.program_id(0)
    count, width = cotangent_ref.shape
    slots = produced_ref.shape[0]

    @pl.when(step == 0)
    def _():
        weight_sum[...] = jnp.zeros_like(weight_sum)
        gains_ref[...] = jnp.zeros_like(gains_ref)

    target = column_ref[:, 0:1]
    place = lax.broadcasted_iota(jnp.int32, (count, slots), 1)
    chosen = jnp.where(place == target, 1.0, 0.0).astype(BF)
    term = dot(chosen, produced_ref[...])
    back = dot(chosen, back_ref[...])
    mask = present_rows(step, count, length_ref[0])
    gate = gate_ref[:, 0:1]
    cotangent = cotangent_ref[...].astype(F32)
    residual = residual_ref[...]
    layer_ref[...] = (residual + mask * gate * term).astype(BF)
    along = jnp.sum(cotangent * term, axis=-1, keepdims=True)
    logit_gradient = mask * along * gate * (1.0 - gate)
    picked = picked_rows(column_ref, centroids_ref, slots // centroids_ref.shape[0])
    hidden_gradient = back + logit_gradient * picked
    normal, inverse = normalise(residual)
    gains_ref[0:1, :] += jnp.sum(hidden_gradient * normal, axis=0, keepdims=True)
    gains_ref[1:2, :] += jnp.sum(hidden_gradient, axis=0, keepdims=True)
    residual_gradient = cotangent + norm_backward(
        normal, inverse, gain_ref[...], hidden_gradient
    )
    residual_grad_ref[...] = residual_gradient
    branch_gradient = (mask * residual_gradient).astype(BF)
    mixed_grad_ref[...] = dot(branch_gradient, weight_ref[...], 1, 1).astype(BF)
    weight_sum[...] += dot(mixed_ref[...], branch_gradient, 0, 0)

    @pl.when(step == pl.num_programs(0) - 1)
    def _():
        weight_grad_ref[...] = weight_sum[...].astype(BF)


def combine(
    length, produced, back, target_column, cotangent, residual, gate, gain, centroids, mixed, weight
):
    rows, width = cotangent.shape
    experts = centroids.shape[0]
    block = 256
    part = pl.BlockSpec((block, width), lambda i, l: (i, 0))
    thin = pl.BlockSpec((block, 128), lambda i, l: (i, 0))
    still = lambda i, l: (0, 0)
    return pl.pallas_call(
        combine_kernel,
        out_shape=[
            jax.ShapeDtypeStruct((rows, width), BF),
            jax.ShapeDtypeStruct((rows, width), F32),
            jax.ShapeDtypeStruct((rows, width), BF),
            jax.ShapeDtypeStruct((width, width), BF),
            jax.ShapeDtypeStruct((8, width), F32),
        ],
        grid_spec=pltpu.PrefetchScalarGridSpec(
            num_scalar_prefetch=1,
            grid=(rows // block,),
            in_specs=[
                pl.BlockSpec((rows, width), still),
                pl.BlockSpec((rows, width), still),
                thin,
                part,
                part,
                thin,
                pl.BlockSpec((1, width), still),
                pl.BlockSpec((experts, width), still),
                part,
                pl.BlockSpec((width, width), still),
            ],
            out_specs=[
                part,
                part,
                part,
                pl.BlockSpec((width, width), still),
                pl.BlockSpec((8, width), still),
            ],
            scratch_shapes=[pltpu.VMEM((width, width), F32)],
        ),
        compiler_params=params(),
        cost_estimate=cost(4 * rows * (rows + width) * width, 24 * rows * width),
        name="combine",
    )(
        length,
        produced,
        back,
        target_column,
        cotangent,
        residual,
        gate,
        gain,
        centroids,
        mixed,
        weight,
    )


def project_back_kernel(
    query_ref,
    key_ref,
    value_ref,
    tokens_ref,
    residual_grad_ref,
    weight_ref,
    gain_ref,
    shift_ref,
    output_grad_ref,
    second_ref,
    input_grad_ref,
    packed_ref,
    weight_sum,
    gains,
    *,
    shares,
):
    step = pl.program_id(0)
    width = tokens_ref.shape[1]
    share = width // shares

    @pl.when(step == 0)
    def _():
        weight_sum[...] = jnp.zeros_like(weight_sum)
        gains[...] = jnp.zeros_like(gains)

    normal, inverse = normalise(tokens_ref[...].astype(F32))
    gain = gain_ref[...]
    normed = (normal * gain + shift_ref[...]).astype(BF)
    gradient = None
    for number, ref in enumerate((query_ref, key_ref, value_ref)):
        columns = slice(number * width, (number + 1) * width)
        part = dot(ref[...], weight_ref[:, columns], 1, 1)
        gradient = part if gradient is None else gradient + part
        weight_sum[number] += dot(normed, ref[...], 0, 0)
    gains[0:1, :] += jnp.sum(gradient * normal, axis=0, keepdims=True)
    gains[1:2, :] += jnp.sum(gradient, axis=0, keepdims=True)
    input_part = norm_backward(normal, inverse, gain, gradient)
    input_grad_ref[...] = (residual_grad_ref[...] + input_part).astype(BF)

    @pl.when(step == pl.num_programs(0) - 1)
    def _():
        rest = jnp.zeros((GAIN_ROWS - 4, width), F32)
        tail = jnp.concatenate([gains[0:2, :], second_ref[0:2, :], rest], axis=0).astype(BF)
        for number in range(shares):
            rows = slice(number * share, (number + 1) * share)
            for third in range(3):
                at = slice(third * share, (third + 1) * share)
                packed_ref[number, at, :] = weight_sum[third, rows, :].astype(BF)
            packed_ref[number, 3 * share : 4 * share, :] = output_grad_ref[rows, :]
            packed_ref[number, 4 * share :, :] = tail


def project_back(
    query, key, value, tokens, residual_grad, weight, gain, shift, output_grad, second, shares
):
    rows, width = tokens.shape
    block = 256
    packed_rows = 4 * (width // shares) + GAIN_ROWS
    part = pl.BlockSpec((block, width), lambda i: (i, 0))
    line = pl.BlockSpec((1, width), lambda i: (0, 0))
    return pl.pallas_call(
        functools.partial(project_back_kernel, shares=shares),
        out_shape=[
            jax.ShapeDtypeStruct((rows, width), BF),
            jax.ShapeDtypeStruct((shares, packed_rows, width), BF),
        ],
        grid=(rows // block,),
        in_specs=[
            part,
            part,
            part,
            part,
            part,
            pl.BlockSpec(weight.shape, lambda i: (0, 0)),
            line,
            line,
            pl.BlockSpec((width, width), lambda i: (0, 0)),
            pl.BlockSpec((8, width), lambda i: (0, 0)),
        ],
        out_specs=[part, pl.BlockSpec((shares, packed_rows, width), lambda i: (0, 0, 0))],
        scratch_shapes=[pltpu.VMEM((3, width, width), F32), pltpu.VMEM((8, width), F32)],
        compiler_params=params(),
        cost_estimate=cost(12 * rows * width * width, 40 * rows * width),
        name="project_back",
    )(query, key, value, tokens, residual_grad, weight, gain, shift, output_grad, second)


def line_scatter(parts, axis):
    n = lax.axis_size(axis)
    me = lax.axis_index(axis)

    def own(part, index):
        return lax.dynamic_index_in_dim(part, jnp.clip(index, 0, n - 1), 0, keepdims=False)

    results = []
    for part in parts:
        right = left = None
        for slot in range(n - 1):
            send = own(part, n - 1 - slot + me)
            send = send if right is None else send + right
            right = lax.ppermute(send, axis, [(z, z + 1) for z in range(slot + 1)])
            send = own(part, slot - (n - 1) + me)
            send = send if left is None else send + left
            left = lax.ppermute(send, axis, [(n - 1 - z, n - 2 - z) for z in range(slot + 1)])
        total = own(part, me).astype(F32)
        for arrived in (right, left):
            if arrived is not None:
                total = total + arrived.astype(F32)
        results.append(total)
    return results


def partner_pairs(axis, bit):
    return [(i, i ^ bit) for i in range(lax.axis_size(axis))]


def halve(values, axis, bit, dimension):
    upper = (lax.axis_index(axis) & bit) != 0
    size = values.shape[dimension] // 2
    low = lax.slice_in_dim(values, 0, size, axis=dimension)
    high = lax.slice_in_dim(values, size, 2 * size, axis=dimension)
    sent = lax.ppermute(jnp.where(upper, low, high), axis, partner_pairs(axis, bit))
    return jnp.where(upper, high, low) + sent


def unite(values, axis, bit, dimension):
    upper = (lax.axis_index(axis) & bit) != 0
    other = lax.ppermute(values, axis, partner_pairs(axis, bit))
    low = jnp.where(upper, other, values)
    high = jnp.where(upper, values, other)
    return jnp.concatenate([low, high], axis=dimension)


def on_device(
    tokens,
    lengths,
    expert_index,
    centroids,
    input_weight,
    output_weight,
    first_gain,
    first_shift,
    second_gain,
    second_shift,
    up_weight,
    down_weight,
    cotangent,
):
    rows, width = tokens.shape
    experts = centroids.shape[0]
    capacity = rows // experts
    shares = lax.axis_size("dp")
    share = width // shares
    line = lambda vector: vector.reshape(1, width)
    exchange = lambda values: lax.all_to_all(
        values.reshape(experts, capacity, width), "expert", split_axis=0, concat_axis=0, tiled=True
    ).reshape(rows, width)

    outgoing_cotangent, target_row, target_column = route(
        lengths, expert_index, cotangent, experts
    )
    arrived_cotangent = exchange(outgoing_cotangent)
    projected = project(tokens, input_weight, line(first_gain), line(first_shift))
    mixed, total = attend(lengths, projected)
    residual, gate, outgoing = hidden_rows(
        lengths,
        mixed,
        tokens,
        output_weight,
        line(second_gain),
        line(second_shift),
        centroids,
        target_row,
        target_column,
    )
    arrived = exchange(outgoing)
    centroid = lax.dynamic_slice_in_dim(centroids, lax.axis_index("expert"), 1, 0)
    produced, back, down_grad, up_grad = expert(
        arrived, arrived_cotangent, centroid, up_weight[0], down_weight[0]
    )
    returned = exchange(produced)
    returned_back = exchange(back)
    inner = up_weight.shape[2]
    down_share, up_share = line_scatter(
        [
            down_grad.reshape(shares, inner // shares, width),
            up_grad.reshape(shares, share, inner),
        ],
        "dp",
    )
    layer_output, residual_grad, mixed_grad, output_grad, second_gains = combine(
        lengths,
        returned,
        returned_back,
        target_column,
        cotangent,
        residual,
        gate,
        line(second_gain),
        centroids,
        mixed,
        output_weight,
    )
    query, key, value = attend_back(lengths, projected, mixed, total, mixed_grad)
    input_gradient, packed = project_back(
        query,
        key,
        value,
        tokens,
        residual_grad,
        input_weight,
        line(first_gain),
        line(first_shift),
        output_grad,
        second_gains,
        shares,
    )
    bits = []
    bit = 1
    while bit < experts:
        bits.append((bit, 2 if bit == 1 else 1))
        bit *= 2
    for bit, dimension in bits:
        packed = halve(packed, "expert", bit, dimension)
    summed = line_scatter([packed], "dp")[0].astype(BF)
    for bit, dimension in reversed(bits):
        summed = unite(summed, "expert", bit, dimension - 1)
    summed = summed.astype(F32)
    input_share = jnp.concatenate(
        [summed[number * share : (number + 1) * share] for number in range(3)], axis=1
    )
    output_share = summed[3 * share : 4 * share]
    gains = lax.dynamic_slice_in_dim(
        summed[4 * share : 4 * share + 4], lax.axis_index("dp") * share, share, 1
    )
    return (
        layer_output,
        input_gradient,
        input_share,
        output_share,
        gains[0],
        gains[1],
        gains[2],
        gains[3],
        up_share[None],
        down_share[None],
    )


def solution(mesh):
    both = P(("dp", "expert"))
    rows = P(("dp", "expert"), None)
    weights = P("expert", None, None)
    return jax.shard_map(
        on_device,
        mesh=mesh,
        in_specs=(rows, both, both, P(), P(), P(), P(), P(), P(), P(), weights, weights, rows),
        out_specs=(
            rows,
            rows,
            P("dp", None),
            P("dp", None),
            P("dp"),
            P("dp"),
            P("dp"),
            P("dp"),
            P("expert", "dp", None),
            P("expert", "dp", None),
        ),
        check_vma=False,
    )
```

```python
import functools

import jax
import jax.numpy as jnp
from jax import lax
from jax.experimental import pallas as pl
from jax.experimental.pallas import tpu as pltpu
from jax.sharding import PartitionSpec as P

HEADS = 12
EPS = 1e-05
EXCLUDED = -1e30
BF = jnp.bfloat16
F32 = jnp.float32
QUERY_ROWS = 256
SEEN = 1
LEAD = 2


def dot(left, right, left_axis=1, right_axis=0):
    return lax.dot_general(
        left,
        right,
        (((left_axis,), (right_axis,)), ((), ())),
        preferred_element_type=F32,
    )


def params(limit=60):
    return pltpu.CompilerParams(vmem_limit_bytes=limit << 20)


def cost(flops, bytes_accessed, transcendentals=0):
    return pl.CostEstimate(
        flops=int(flops * SEEN),
        bytes_accessed=int(bytes_accessed * SEEN),
        transcendentals=int(transcendentals * SEEN),
    )


def split_three(values):
    high = values.astype(BF)
    rest = values - high.astype(F32)
    middle = rest.astype(BF)
    return high, middle, (rest - middle.astype(F32)).astype(BF)


def normalise(values):
    average = jnp.mean(values, axis=-1, keepdims=True)
    centred = values - average
    variance = jnp.mean(centred * centred, axis=-1, keepdims=True)
    inverse = lax.rsqrt(variance + EPS)
    return centred * inverse, inverse


def norm_backward(normal, inverse, gain, gradient):
    scaled = gain * gradient
    first = jnp.mean(scaled, axis=-1, keepdims=True)
    second = jnp.mean(scaled * normal, axis=-1, keepdims=True)
    return (scaled - first - normal * second) * inverse


def selection(target, first, count):
    rows = lax.broadcasted_iota(jnp.int32, (count, target.shape[1]), 0) + first
    return jnp.where(rows == target, 1.0, 0.0).astype(BF)


def route_kernel(length_ref, expert_ref, cotangent_ref, out_ref, row_ref, column_ref, *, experts):
    step = pl.program_id(0)
    rows = cotangent_ref.shape[0]
    block = out_ref.shape[0]

    @pl.when(step == 0)
    def _():
        length = length_ref[0]
        position = lax.broadcasted_iota(jnp.int32, (1, rows), 1)
        named = jnp.where(position < length, expert_ref[...], -1)
        number = lax.broadcasted_iota(jnp.int32, (experts, rows), 0)
        onehot = jnp.where(number == named, 1.0, 0.0)
        before = lax.broadcasted_iota(jnp.int32, (rows, rows), 0)
        after = lax.broadcasted_iota(jnp.int32, (rows, rows), 1)
        earlier = jnp.where(before < after, 1.0, 0.0).astype(BF)
        counts = dot(onehot.astype(BF), earlier)
        slot = jnp.sum(onehot * counts, axis=0, keepdims=True).astype(jnp.int32)
        target = jnp.where(named >= 0, named * (rows // experts) + slot, -1)
        row_ref[...] = jnp.broadcast_to(target, row_ref.shape)
        wide = jnp.broadcast_to(target.astype(F32), (128, rows))
        column_ref[...] = wide.T.astype(jnp.int32)

    chosen = selection(row_ref[0:1, :], step * block, block)
    out_ref[...] = dot(chosen, cotangent_ref[...]).astype(BF)


def route(length, expert_index, cotangent, experts):
    rows, width = cotangent.shape
    block = 256
    return pl.pallas_call(
        functools.partial(route_kernel, experts=experts),
        out_shape=[
            jax.ShapeDtypeStruct((rows, width), BF),
            jax.ShapeDtypeStruct((8, rows), jnp.int32),
            jax.ShapeDtypeStruct((rows, 128), jnp.int32),
        ],
        grid_spec=pltpu.PrefetchScalarGridSpec(
            num_scalar_prefetch=1,
            grid=(rows // block,),
            in_specs=[
                pl.BlockSpec((1, rows), lambda i, l: (0, 0)),
                pl.BlockSpec((rows, width), lambda i, l: (0, 0)),
            ],
            out_specs=[
                pl.BlockSpec((block, width), lambda i, l: (i, 0)),
                pl.BlockSpec((8, rows), lambda i, l: (0, 0)),
                pl.BlockSpec((rows, 128), lambda i, l: (0, 0)),
            ],
        ),
        compiler_params=params(),
        cost_estimate=cost(2 * rows * rows * width, 4 * rows * width),
        name="route",
    )(length, expert_index.reshape(1, rows), cotangent)


def project_kernel(tokens_ref, weight_ref, norms_ref, out_ref):
    normal, _ = normalise(tokens_ref[...].astype(F32))
    normed = (normal * norms_ref[0:1, :] + norms_ref[1:2, :]).astype(BF)
    out_ref[...] = dot(normed, weight_ref[...]).astype(BF)


def project(tokens, weight, norms):
    rows, width = tokens.shape
    columns = weight.shape[1]
    block = 256
    return pl.pallas_call(
        project_kernel,
        out_shape=jax.ShapeDtypeStruct((rows, columns), BF),
        grid=(rows // block,),
        in_specs=[
            pl.BlockSpec((block, width), lambda i: (i, 0)),
            pl.BlockSpec((width, columns), lambda i: (0, 0)),
            pl.BlockSpec((4, width), lambda i: (0, 0)),
        ],
        out_specs=pl.BlockSpec((block, columns), lambda i: (i, 0)),
        compiler_params=params(),
        cost_estimate=cost(2 * rows * width * columns, 2 * (rows + width) * columns),
        name="project",
    )(tokens, weight, norms)


def staggered(items, begin, finish, ahead=1):
    waiting = []
    for item in items:
        waiting.append((item, begin(item)))
        if len(waiting) > ahead:
            finish(*waiting.pop(0))
    for item, values in waiting:
        finish(item, values)


def by_blocks(rows, length, work, empty):
    starts = list(range(0, rows, QUERY_ROWS))

    @pl.when(length > starts[-1])
    def _():
        work(starts)

    @pl.when(length <= starts[-1])
    def _():
        for start in starts:
            pl.when(start < length)(functools.partial(work, [start]))
            pl.when(start >= length)(functools.partial(empty, start))


def attend_kernel(length_ref, query_ref, key_ref, value_ref, mixed_ref, total_ref, *, scale, half):
    lane = lax.broadcasted_iota(jnp.int32, (1, 2 * half), 1)
    length = length_ref[0]
    zero, one = jnp.zeros((), BF), jnp.ones((), BF)
    done = {}

    def scores_of(item):
        start, head = item
        end = start + QUERY_ROWS
        row = lax.broadcasted_iota(jnp.int32, (QUERY_ROWS, 1), 0) + start
        limit = jnp.minimum(row, length - 1)
        column = lax.broadcasted_iota(jnp.int32, (QUERY_ROWS, QUERY_ROWS), 1) + start
        scaled = query_ref[start:end, :] * jnp.asarray(scale, BF)
        query = jnp.where((lane // half) == head, scaled, zero)
        scores = dot(query, key_ref[:end, :], 1, 1)
        last = jnp.where(column <= limit, scores[:, start:], EXCLUDED)
        return jnp.concatenate([scores[:, :start], last], axis=1) if start else last

    def mix(item, scores):
        start, head = item
        end = start + QUERY_ROWS
        other = half * (1 - head)
        ones = jnp.where(lane == other, one, zero)
        value = jnp.where((lane // half) == head, value_ref[:end, :], ones)
        top = jnp.max(scores, axis=1, keepdims=True)
        out = dot(jnp.exp(scores - top).astype(BF), value)
        total = out[:, other : other + 1]
        done[item] = (out / total, top + jnp.log(total))
        if head == 1:
            first = lane < half
            low, high = done[start, 0], done[start, 1]
            mixed_ref[start:end, :] = jnp.where(first, low[0], high[0]).astype(BF)
            total_ref[start:end, :] = jnp.where(first, low[1], high[1])

    def work(starts):
        staggered([(start, head) for start in starts for head in range(2)], scores_of, mix)

    def empty(start):
        end = start + QUERY_ROWS
        mixed_ref[start:end, :] = jnp.zeros((QUERY_ROWS, 2 * half), BF)
        total_ref[start:end, :] = jnp.zeros((QUERY_ROWS, 2 * half), F32)

    by_blocks(query_ref.shape[0], length, work, empty)


def pair_specs(rows, wide, pairs, thirds):
    return [pl.BlockSpec((rows, wide), lambda i, l, o=o: (0, i + o * pairs)) for o in range(thirds)]


def attend(length, projected):
    rows, width = projected.shape[0], projected.shape[1] // 3
    size = width // HEADS
    pairs = HEADS // 2
    one = pl.BlockSpec((rows, 2 * size), lambda i, l: (0, i))
    return pl.pallas_call(
        functools.partial(attend_kernel, scale=size**-0.5, half=size),
        out_shape=[
            jax.ShapeDtypeStruct((rows, width), BF),
            jax.ShapeDtypeStruct((rows, width), F32),
        ],
        grid_spec=pltpu.PrefetchScalarGridSpec(
            num_scalar_prefetch=1,
            grid=(pairs,),
            in_specs=pair_specs(rows, 2 * size, pairs, 3),
            out_specs=[one, one],
        ),
        compiler_params=params(),
        cost_estimate=cost(
            16 * rows * rows * width, 12 * rows * width, HEADS * rows * rows // 2
        ),
        name="attend",
    )(length, projected, projected, projected)


def attend_back_kernel(
    length_ref,
    query_ref,
    key_ref,
    value_ref,
    mixed_ref,
    total_ref,
    incoming_ref,
    query_out,
    key_out,
    value_out,
    key_sum,
    value_sum,
    *,
    scale,
    half,
):
    lane = lax.broadcasted_iota(jnp.int32, (1, 2 * half), 1)
    length = length_ref[0]
    zero, one = jnp.zeros((), BF), jnp.ones((), BF)
    key_sum[...] = jnp.zeros_like(key_sum)
    value_sum[...] = jnp.zeros_like(value_sum)
    parts = {}

    def products(item):
        start, head = item
        end = start + QUERY_ROWS
        mine = (lane // half) == head
        other = half * (1 - head)
        ones = jnp.where((lane >= other) & (lane < other + 3), one, zero)

        def extend(base, column):
            a, b, c = split_three(-column)
            rest = jnp.where(lane == other + 2, c, zero)
            rest = jnp.where(lane == other + 1, b, rest)
            return jnp.where(mine, base, jnp.where(lane == other, a, rest))

        row = lax.broadcasted_iota(jnp.int32, (QUERY_ROWS, 1), 0) + start
        column = lax.broadcasted_iota(jnp.int32, (QUERY_ROWS, QUERY_ROWS), 1) + start
        allowed = (row <= column) & (row < length)
        incoming = incoming_ref[start:end, :]
        product = incoming.astype(F32) * mixed_ref[start:end, :].astype(F32)
        query = jnp.where(mine, query_ref[start:end, :] * jnp.asarray(scale, BF), zero)
        grad = jnp.where(mine, incoming, zero)
        inner = jnp.sum(jnp.where(mine, product, 0.0), axis=1, keepdims=True)
        total = total_ref[start:end, head * half : head * half + 1]
        key = jnp.where(mine, key_ref[:end, :], ones)
        scores = dot(key, extend(query, total), 1, 1)
        last = jnp.where(allowed, scores[start:, :], EXCLUDED)
        scores = jnp.concatenate([scores[:start, :], last], axis=0) if start else last
        value = jnp.where(mine, value_ref[:end, :], ones)
        return scores, dot(value, extend(grad, inner), 1, 1), query, grad

    def gradients(item, values):
        start, head = item
        scores, centred, query, grad = values
        end = start + QUERY_ROWS
        probs = jnp.exp(scores)
        score_gradient = (probs * centred).astype(BF)
        value_sum[:end, :] += dot(probs.astype(BF), grad)
        key_sum[:end, :] += dot(score_gradient, query)
        key = jnp.where((lane // half) == head, key_ref[:end, :], zero)
        parts[item] = dot(score_gradient, key, 0, 0)
        if head == 1:
            total = parts[start, 0] + parts[start, 1]
            query_out[start:end, :] = (total * scale).astype(BF)

    def work(starts):
        staggered([(start, head) for start in starts for head in range(2)], products, gradients)

    def empty(start):
        query_out[start : start + QUERY_ROWS, :] = jnp.zeros((QUERY_ROWS, 2 * half), BF)

    by_blocks(query_ref.shape[0], length, work, empty)
    key_out[...] = key_sum[...].astype(BF)
    value_out[...] = value_sum[...].astype(BF)


def attend_back(length, projected, mixed, total, incoming):
    rows, width = projected.shape[0], projected.shape[1] // 3
    size = width // HEADS
    pairs = HEADS // 2
    one = pl.BlockSpec((rows, 2 * size), lambda i, l: (0, i))
    return pl.pallas_call(
        functools.partial(attend_back_kernel, scale=size**-0.5, half=size),
        out_shape=[jax.ShapeDtypeStruct((rows, width), BF)] * 3,
        grid_spec=pltpu.PrefetchScalarGridSpec(
            num_scalar_prefetch=1,
            grid=(pairs,),
            in_specs=pair_specs(rows, 2 * size, pairs, 3) + [one] * 3,
            out_specs=[one] * 3,
            scratch_shapes=[pltpu.VMEM((rows, 2 * size), F32)] * 2,
        ),
        compiler_params=params(),
        cost_estimate=cost(
            30 * rows * rows * width, 20 * rows * width, HEADS * rows * rows // 2
        ),
        name="attend_back",
    )(length, projected, projected, projected, mixed, total, incoming)


def picked_rows(column_ref, centroids_ref, capacity):
    experts, width = centroids_ref.shape
    pieces = [piece.astype(F32) for piece in split_three(centroids_ref[...])]
    rest = jnp.zeros((128 - 3 * experts, width), F32)
    table = jnp.concatenate(pieces + [rest], axis=0).astype(BF)
    target = column_ref[...]
    lane = lax.broadcasted_iota(jnp.int32, (1, 128), 1)
    low = jnp.where(lane < 3 * experts, (lane % experts) * capacity, 1 << 20)
    onehot = jnp.where((target >= low) & (target < low + capacity), 1.0, 0.0).astype(BF)
    return dot(onehot, table)


def present_rows(block_index, count, length):
    row = lax.broadcasted_iota(jnp.int32, (count, 1), 0) + block_index * count
    return jnp.where(row < length, 1.0, 0.0)


def hidden_kernel(
    length_ref,
    mixed_ref,
    tokens_ref,
    weight_ref,
    norms_ref,
    centroids_ref,
    row_ref,
    column_ref,
    residual_ref,
    gate_ref,
    out_ref,
    hidden_low,
    *,
    blocks,
):
    step = pl.program_id(0)
    count = mixed_ref.shape[0]
    rows = row_ref.shape[1]

    @pl.when(step < blocks)
    def _():
        branch = dot(mixed_ref[...], weight_ref[...])
        mask = present_rows(step, count, length_ref[0])
        residual = tokens_ref[...].astype(F32) + mask * branch
        residual_ref[...] = residual
        normal, _ = normalise(residual)
        hidden = normal * norms_ref[2:3, :] + norms_ref[3:4, :]
        picked = picked_rows(column_ref, centroids_ref, rows // centroids_ref.shape[0])
        gate = jax.nn.sigmoid(jnp.sum(hidden * picked, axis=-1, keepdims=True))
        gate_ref[...] = jnp.broadcast_to(gate, gate_ref.shape)
        hidden_low[pl.ds(pl.multiple_of(step * count, count), count), :] = hidden.astype(BF)

    @pl.when(step == blocks)
    def _():
        for first in range(0, rows, 256):
            chosen = selection(row_ref[0:1, :], first, 256)
            out_ref[first : first + 256, :] = dot(chosen, hidden_low[...]).astype(BF)


def hidden_rows(length, mixed, tokens, weight, norms, centroids, target_row, target_column):
    rows, width = tokens.shape
    experts = centroids.shape[0]
    block = 256
    blocks = rows // block
    early = lambda i, l: (jnp.minimum(i, blocks - 1), 0)
    still = lambda i, l: (0, 0)
    return pl.pallas_call(
        functools.partial(hidden_kernel, blocks=blocks),
        out_shape=[
            jax.ShapeDtypeStruct((rows, width), F32),
            jax.ShapeDtypeStruct((rows, 128), F32),
            jax.ShapeDtypeStruct((rows, width), BF),
        ],
        grid_spec=pltpu.PrefetchScalarGridSpec(
            num_scalar_prefetch=1,
            grid=(blocks + 1,),
            in_specs=[
                pl.BlockSpec((block, width), early),
                pl.BlockSpec((block, width), early),
                pl.BlockSpec((width, width), still),
                pl.BlockSpec((4, width), still),
                pl.BlockSpec((experts, width), still),
                pl.BlockSpec((8, rows), still),
                pl.BlockSpec((block, 128), early),
            ],
            out_specs=[
                pl.BlockSpec((block, width), early),
                pl.BlockSpec((block, 128), early),
                pl.BlockSpec((rows, width), still),
            ],
            scratch_shapes=[pltpu.VMEM((rows, width), BF)],
        ),
        compiler_params=params(),
        cost_estimate=cost(2 * rows * (rows + width) * width, 12 * rows * width),
        name="hidden_rows",
    )(length, mixed, tokens, weight, norms, centroids, target_row, target_column)


def far_first(number, place, shares):
    return jnp.where(place < shares // 2, shares - 1 - number, number)


def expert_kernel(
    me_ref,
    place_ref,
    rows_ref,
    cotangent_ref,
    centroids_ref,
    up_ref,
    down_ref,
    back_ref,
    *refs,
    shares,
):
    arrays = shares - LEAD + 1
    downs, ups = refs[:arrays], refs[arrays : 2 * arrays]
    produced_sum, back_sum, transposed, gradient = refs[2 * arrays :]
    step = pl.program_id(0)
    width = rows_ref.shape[1]
    share = width // shares
    low = place_ref[0] < shares // 2

    @pl.when(step == 0)
    def _():
        hidden = rows_ref[...].astype(F32)
        centroid = centroids_ref[pl.ds(me_ref[0], 1), :]
        gate = jax.nn.sigmoid(jnp.sum(hidden * centroid, axis=-1, keepdims=True))
        gradient[...] = (gate * cotangent_ref[...].astype(F32)).astype(BF)
        produced_sum[...] = jnp.zeros_like(produced_sum)
        back_sum[...] = jnp.zeros_like(back_sum)

    def transpose(order):
        values = rows_ref[...].T
        for number in range(shares):
            at = slice(order[number] * share, (order[number] + 1) * share)
            transposed[number * share : (number + 1) * share, :] = values[at, :]

    pl.when((step == 0) & low)(functools.partial(transpose, list(range(shares))[::-1]))
    pl.when((step == 0) & jnp.logical_not(low))(functools.partial(transpose, list(range(shares))))

    upper = dot(rows_ref[...], up_ref[...])
    part = 0.5 + 0.5 * lax.erf(upper * (0.5**0.5))
    density = jnp.exp(upper * upper * -0.5) * 0.3989422804014327
    active = (upper * part).astype(BF)
    slope = part + upper * density
    active_gradient = dot(gradient[...], down_ref[...], 1, 1)
    upper_gradient = (active_gradient * slope).astype(BF)
    produced_sum[...] += dot(active, down_ref[...])
    down = dot(active, gradient[...], 0, 0).astype(BF)
    back_sum[...] += dot(upper_gradient, up_ref[...], 1, 1)
    up = dot(transposed[...], upper_gradient).astype(BF)
    for number in range(shares):
        at = slice(number * share, (number + 1) * share)
        if number < LEAD:
            ups[0][number, 0] = up[at]
        else:
            ups[number - LEAD + 1][0, 0] = up[at]

        @pl.when(step == number)
        def _(number=number):
            downs[max(number - LEAD + 1, 0)][0, 0] = down

    @pl.when(step == pl.num_programs(0) - 1)
    def _():
        back_ref[:, :width] = produced_sum[...].astype(BF)
        back_ref[:, width:] = back_sum[...].astype(BF)


def expert(me, place, hidden, cotangent, centroids, up, down, shares):
    count, width = hidden.shape
    inner = up.shape[1]
    chunk, share = inner // shares, width // shares
    still = lambda c, m, p: (0, 0)
    whole = pl.BlockSpec((count, width), still)
    real = lambda c, p: far_first(c, p[0], shares)
    sizes = [LEAD] + [1] * (shares - LEAD)
    down_specs = [
        pl.BlockSpec((1, 1, chunk, width), lambda c, m, p: (jnp.minimum(c, LEAD - 1), 0, 0, 0))
    ] + [pl.BlockSpec((1, 1, chunk, width), lambda c, m, p: (0, 0, 0, 0))] * (shares - LEAD)
    up_specs = [
        pl.BlockSpec((size, 1, share, chunk), lambda c, m, p: (0, real(c, p), 0, 0))
        for size in sizes
    ]
    outs = pl.pallas_call(
        functools.partial(expert_kernel, shares=shares),
        out_shape=[jax.ShapeDtypeStruct((count, 2 * width), BF)]
        + [jax.ShapeDtypeStruct((size, 1, chunk, width), BF) for size in sizes]
        + [jax.ShapeDtypeStruct((size, shares, share, chunk), BF) for size in sizes],
        grid_spec=pltpu.PrefetchScalarGridSpec(
            num_scalar_prefetch=2,
            grid=(shares,),
            in_specs=[
                whole,
                whole,
                pl.BlockSpec(centroids.shape, still),
                pl.BlockSpec((width, chunk), lambda c, m, p: (0, real(c, p))),
                pl.BlockSpec((chunk, width), lambda c, m, p: (real(c, p), 0)),
            ],
            out_specs=[pl.BlockSpec((count, 2 * width), still)] + down_specs + up_specs,
            scratch_shapes=[
                pltpu.VMEM((count, width), F32),
                pltpu.VMEM((count, width), F32),
                pltpu.VMEM((width, count), BF),
                pltpu.VMEM((count, width), BF),
            ],
        ),
        compiler_params=params(),
        cost_estimate=cost(12 * count * width * inner, 8 * inner * width, 2 * count * inner),
        name="expert",
    )(me, place, hidden, cotangent, centroids, up, down)
    arrays = len(sizes)
    return outs[0], list(outs[1 : 1 + arrays]), list(outs[1 + arrays :])


def combine_kernel(
    length_ref,
    returned_ref,
    column_ref,
    cotangent_ref,
    residual_ref,
    gate_ref,
    norms_ref,
    centroids_ref,
    mixed_ref,
    weight_ref,
    layer_ref,
    residual_grad_ref,
    mixed_grad_ref,
    weight_grad_ref,
    gains_ref,
    weight_sum,
):
    step = pl.program_id(0)
    count, width = cotangent_ref.shape
    slots = returned_ref.shape[0]

    @pl.when(step == 0)
    def _():
        weight_sum[...] = jnp.zeros_like(weight_sum)
        gains_ref[...] = jnp.zeros_like(gains_ref)

    target = column_ref[:, 0:1]
    place = lax.broadcasted_iota(jnp.int32, (count, slots), 1)
    chosen = jnp.where(place == target, 1.0, 0.0).astype(BF)
    term = dot(chosen, returned_ref[:, :width])
    back = dot(chosen, returned_ref[:, width:])
    mask = present_rows(step, count, length_ref[0])
    gate = gate_ref[:, 0:1]
    cotangent = cotangent_ref[...].astype(F32)
    residual = residual_ref[...]
    layer_ref[...] = (residual + mask * gate * term).astype(BF)
    along = jnp.sum(cotangent * term, axis=-1, keepdims=True)
    logit_gradient = mask * along * gate * (1.0 - gate)
    picked = picked_rows(column_ref, centroids_ref, slots // centroids_ref.shape[0])
    hidden_gradient = back + logit_gradient * picked
    normal, inverse = normalise(residual)
    gains_ref[0:1, :] += jnp.sum(hidden_gradient * normal, axis=0, keepdims=True)
    gains_ref[1:2, :] += jnp.sum(hidden_gradient, axis=0, keepdims=True)
    residual_gradient = cotangent + norm_backward(
        normal, inverse, norms_ref[2:3, :], hidden_gradient
    )
    residual_grad_ref[...] = residual_gradient
    branch_gradient = (mask * residual_gradient).astype(BF)
    mixed_grad_ref[...] = dot(branch_gradient, weight_ref[...], 1, 1).astype(BF)
    weight_sum[...] += dot(mixed_ref[...], branch_gradient, 0, 0)

    @pl.when(step == pl.num_programs(0) - 1)
    def _():
        weight_grad_ref[...] = weight_sum[...].astype(BF)


def combine(
    length, returned, target_column, cotangent, residual, gate, norms, centroids, mixed, weight
):
    rows, width = cotangent.shape
    experts = centroids.shape[0]
    block = 256
    part = pl.BlockSpec((block, width), lambda i, l: (i, 0))
    thin = pl.BlockSpec((block, 128), lambda i, l: (i, 0))
    still = lambda i, l: (0, 0)
    return pl.pallas_call(
        combine_kernel,
        out_shape=[
            jax.ShapeDtypeStruct((rows, width), BF),
            jax.ShapeDtypeStruct((rows, width), F32),
            jax.ShapeDtypeStruct((rows, width), BF),
            jax.ShapeDtypeStruct((width, width), BF),
            jax.ShapeDtypeStruct((8, width), F32),
        ],
        grid_spec=pltpu.PrefetchScalarGridSpec(
            num_scalar_prefetch=1,
            grid=(rows // block,),
            in_specs=[
                pl.BlockSpec((rows, 2 * width), still),
                thin,
                part,
                part,
                thin,
                pl.BlockSpec((4, width), still),
                pl.BlockSpec((experts, width), still),
                part,
                pl.BlockSpec((width, width), still),
            ],
            out_specs=[
                part,
                part,
                part,
                pl.BlockSpec((width, width), still),
                pl.BlockSpec((8, width), still),
            ],
            scratch_shapes=[pltpu.VMEM((width, width), F32)],
        ),
        compiler_params=params(),
        cost_estimate=cost(4 * rows * (rows + width) * width, 24 * rows * width),
        name="combine",
    )(
        length,
        returned,
        target_column,
        cotangent,
        residual,
        gate,
        norms,
        centroids,
        mixed,
        weight,
    )


def packed_rows(share, devices):
    unit = 16 * max(1, devices // 2)
    units = -(-(4 * share + 5) // unit)
    return [-(-units // 2) * unit, units // 2 * unit]


def pack_kernel(
    me_ref,
    query_ref,
    key_ref,
    value_ref,
    tokens_ref,
    norms_ref,
    output_grad_ref,
    second_ref,
    *refs,
    shares,
):
    keeps, sends, normed, sums = refs[0:2], refs[2:4], refs[4], refs[5]
    step = pl.program_id(0)
    width = tokens_ref.shape[1]
    share = width // shares
    half = width // 2
    upper = (me_ref[0] & 1) != 0

    def put(number, first, values):
        border = keeps[0].shape[1]
        low, high = values[:, :half], values[:, half:]
        keep = jnp.where(upper, high, low).astype(BF)
        send = jnp.where(upper, low, high).astype(BF)
        for stream, (begin, end) in enumerate(((0, border), (border, 1 << 30))):
            a, b = max(first, begin), min(first + values.shape[0], end)
            if a < b:
                keeps[stream][number, a - begin : b - begin, :] = keep[a - first : b - first]
                sends[stream][number, a - begin : b - begin, :] = send[a - first : b - first]

    @pl.when(step == 0)
    def _():
        for first in range(0, tokens_ref.shape[0], 256):
            at = slice(first, first + 256)
            normal, _ = normalise(tokens_ref[at, :].astype(F32))
            low = (normal * norms_ref[0:1, :] + norms_ref[1:2, :]).astype(BF)
            normed[:, at] = low.T

    for third, ref in enumerate((query_ref, key_ref, value_ref)):

        @pl.when(step == third)
        def _(third=third, ref=ref):
            values = ref[...]
            total = dot(normed[...], values)
            sums[third : third + 1, :] = jnp.sum(values.astype(F32), axis=0, keepdims=True)
            for number in range(shares):
                put(number, third * share, total[number * share : (number + 1) * share, :])

    @pl.when(step == pl.num_programs(0) - 1)
    def _():
        total_rows = keeps[0].shape[1] + keeps[1].shape[1]
        rest = jnp.zeros((total_rows - 4 * share - 5, width), F32)
        tail = jnp.concatenate([sums[0:3, :], second_ref[0:2, :], rest], axis=0)
        for number in range(shares):
            rows = slice(number * share, (number + 1) * share)
            put(number, 3 * share, output_grad_ref[rows, :].astype(F32))
            put(number, 4 * share, tail)


def pack(me, query, key, value, tokens, norms, output_grad, second, shares, devices):
    rows, width = tokens.shape
    shapes = [(shares, count, width // 2) for count in packed_rows(width // shares, devices)] * 2
    whole = lambda shape: pl.BlockSpec(shape, lambda i, m: (0,) * len(shape))
    outs = pl.pallas_call(
        functools.partial(pack_kernel, shares=shares),
        out_shape=[jax.ShapeDtypeStruct(shape, BF) for shape in shapes],
        grid_spec=pltpu.PrefetchScalarGridSpec(
            num_scalar_prefetch=1,
            grid=(3,),
            in_specs=[whole((rows, width))] * 4
            + [whole((4, width)), whole((width, width)), whole((8, width))],
            out_specs=[whole(shape) for shape in shapes],
            scratch_shapes=[pltpu.VMEM((width, rows), BF), pltpu.VMEM((8, width), F32)],
        ),
        compiler_params=params(),
        cost_estimate=cost(6 * rows * width * width, 20 * rows * width),
        name="pack",
    )(me, query, key, value, tokens, norms, output_grad, second)
    return outs[:2], outs[2:]


def project_back_kernel(
    query_ref, key_ref, value_ref, tokens_ref, residual_grad_ref, weight_ref, norms_ref, out_ref
):
    width = tokens_ref.shape[1]
    gradient = None
    for number, ref in enumerate((query_ref, key_ref, value_ref)):
        columns = slice(number * width, (number + 1) * width)
        part = dot(ref[...], weight_ref[:, columns], 1, 1)
        gradient = part if gradient is None else gradient + part
    normal, inverse = normalise(tokens_ref[...].astype(F32))
    input_part = norm_backward(normal, inverse, norms_ref[0:1, :], gradient)
    out_ref[...] = (residual_grad_ref[...] + input_part).astype(BF)


def project_back(query, key, value, tokens, residual_grad, weight, norms):
    rows, width = tokens.shape
    block = 256
    part = pl.BlockSpec((block, width), lambda i: (i, 0))
    return pl.pallas_call(
        project_back_kernel,
        out_shape=jax.ShapeDtypeStruct((rows, width), BF),
        grid=(rows // block,),
        in_specs=[part] * 5
        + [pl.BlockSpec(weight.shape, lambda i: (0, 0)), pl.BlockSpec((4, width), lambda i: (0, 0))],
        out_specs=part,
        compiler_params=params(),
        cost_estimate=cost(6 * rows * width * width, 20 * rows * width),
        name="project_back",
    )(query, key, value, tokens, residual_grad, weight, norms)


def add_kernel(left_ref, right_ref, out_ref):
    out_ref[...] = (left_ref[...].astype(F32) + right_ref[...].astype(F32)).astype(BF)


def add(left, right, count):
    (left, i), (right, j) = left, right
    _, some, rows, columns = left.shape
    splits = 2 if some == 1 else 1
    together = max(1, some // 2)
    shape = (1, together, rows // splits, columns)
    spec = lambda base: pl.BlockSpec(shape, lambda k, a, b: (k + base, a, b, 0))
    size = count * some * rows * columns
    return pl.pallas_call(
        add_kernel,
        out_shape=jax.ShapeDtypeStruct((count, some, rows, columns), BF),
        grid=(count, some // together, splits),
        in_specs=[spec(i), spec(j)],
        out_specs=spec(0),
        compiler_params=params(),
        cost_estimate=cost(size, 6 * size),
        name="add",
    )(left, right)


def total_kernel(place_ref, *refs, shares):
    owns, arrived, out_ref = refs[: shares - shares // 2], refs[shares - shares // 2 : -1], refs[-1]
    number = jnp.maximum(place_ref[0], shares - 1 - place_ref[0])
    total = owns[0][...].astype(F32)
    for other in range(1, len(owns)):
        total = jnp.where(number == shares // 2 + other, owns[other][...].astype(F32), total)
    for ref in arrived:
        total = total + ref[...].astype(F32)
    out_ref[...] = total


class LineSum:
    def __init__(self, parts, axis, me):
        self.parts, self.axis, self.me = parts, axis, me
        self.n = lax.axis_size(axis)
        self.got = {}

    def part(self, number):
        return (self.parts[0], number) if number < LEAD else (self.parts[number - LEAD + 1], 0)

    def send(self, hop, share, count=1):
        n = self.n
        number = n - 1 - share if hop < n // 2 else share
        if hop:
            values = add(self.part(number), self.got[hop - 1, share], count)
        else:
            values = self.part(number)[0]
        pairs = [(hop, hop + 1), (n - 1 - hop, n - 2 - hop)]
        arrived = lax.ppermute(values, self.axis, pairs)
        for below in range(count):
            self.got[hop, share - below] = (arrived, below)

    def send_rest(self):
        for hop in range(self.n - 1):
            for share in range(self.n - 1, hop, -1):
                if (hop, share) not in self.got:
                    self.send(hop, share)

    def hold(self, keys, values):
        keys = [key for key in keys if key in self.got]
        arrays = [self.got[key][0] for key in keys]
        arrays, values = lax.optimization_barrier((arrays, values))
        for key, array in zip(keys, arrays):
            before = self.got[key][0]
            for other, (held, index) in self.got.items():
                if held is before:
                    self.got[other] = (array, index)
        return values

    def total(self):
        n = self.n
        _, some, rows, columns = self.parts[0].shape
        splits = 2 if some == 1 else 1
        here = lambda base: pl.BlockSpec(
            (None, None, rows // splits, columns), lambda a, b, p: (base, a, b, 0)
        )
        ins = [self.part(number) for number in range(n // 2, n)]
        ins += [self.got[hop, hop + 1] for hop in range(n - 1)]
        return pl.pallas_call(
            functools.partial(total_kernel, shares=n),
            out_shape=jax.ShapeDtypeStruct((rows, some * columns), F32),
            grid_spec=pltpu.PrefetchScalarGridSpec(
                num_scalar_prefetch=1,
                grid=(some, splits),
                in_specs=[here(base) for _, base in ins],
                out_specs=pl.BlockSpec((rows // splits, columns), lambda a, b, p: (b, a)),
            ),
            compiler_params=params(),
            cost_estimate=cost(4 * self.parts[0].size, 12 * self.parts[0].size),
            name="line_total",
        )(self.me, *[array for array, _ in ins])


def partner_pairs(axis, bit):
    return [(i, i ^ bit) for i in range(lax.axis_size(axis))]


def halves_kernel(me_ref, *refs, edges, bits):
    streams = len(bits)
    ins, outs = refs[: len(refs) - 2 * streams], refs[len(refs) - 2 * streams :]
    for stream, (first, last) in enumerate(edges):
        keep, got = ins[:2] if len(ins) == 2 else ins[2 * stream : 2 * stream + 2]
        kept, sent = outs[2 * stream : 2 * stream + 2]
        size = (last - first) // 2
        upper = (me_ref[0] // bits[stream]) % 2
        mine = pl.multiple_of(first + upper * size, 16)
        other = pl.multiple_of(first + (1 - upper) * size, 16)
        for at, out in ((mine, kept), (other, sent)):
            total = keep[:, pl.ds(at, size), :].astype(F32) + got[:, pl.ds(at, size), :].astype(F32)
            out[...] = total.astype(BF)


def halves(me, bits, edges, pairs):
    shares = pairs[0][0].shape[0]
    spec = lambda rows, columns: pl.BlockSpec((1, rows, columns), lambda z, m: (z, 0, 0))
    in_specs, out_specs, out_shape = [], [], []
    for keep, _ in pairs:
        in_specs += [spec(*keep.shape[1:])] * 2
    columns = pairs[0][0].shape[2]
    for first, last in edges:
        rows = (last - first) // 2
        out_specs += [spec(rows, columns)] * 2
        out_shape += [jax.ShapeDtypeStruct((shares, rows, columns), BF)] * 2
    size = sum(keep.size for keep, _ in pairs)
    outs = pl.pallas_call(
        functools.partial(halves_kernel, edges=edges, bits=bits),
        out_shape=out_shape,
        grid_spec=pltpu.PrefetchScalarGridSpec(
            num_scalar_prefetch=1, grid=(shares,), in_specs=in_specs, out_specs=out_specs
        ),
        compiler_params=params(),
        cost_estimate=cost(size, 6 * size),
        name="halves",
    )(me, *[array for pair in pairs for array in pair])
    return [(outs[2 * i], outs[2 * i + 1]) for i in range(len(bits))]


def on_device(
    tokens,
    lengths,
    expert_index,
    centroids,
    input_weight,
    output_weight,
    first_gain,
    first_shift,
    second_gain,
    second_shift,
    up_weight,
    down_weight,
    cotangent,
):
    rows, width = tokens.shape
    experts = centroids.shape[0]
    capacity = rows // experts
    shares = lax.axis_size("dp")
    share = width // shares
    me = lax.axis_index("expert").reshape(1).astype(jnp.int32)
    place = lax.axis_index("dp").reshape(1).astype(jnp.int32)
    norms = jnp.stack([first_gain, first_shift, second_gain, second_shift])

    def exchange(values, axis="expert"):
        return lax.all_to_all(values, axis, split_axis=0, concat_axis=0, tiled=True)

    def dispatch(values):
        return exchange(values.reshape(experts, capacity, -1)).reshape(rows, -1)

    outgoing_cotangent, target_row, target_column = route(
        lengths, expert_index, cotangent, experts
    )
    arrived_cotangent = dispatch(outgoing_cotangent)
    held_tokens, target_row = lax.optimization_barrier((tokens, target_row))
    projected = project(held_tokens, input_weight, norms)
    mixed, total = attend(lengths, projected)
    mixed, arrived_cotangent = lax.optimization_barrier((mixed, arrived_cotangent))
    residual, gate, outgoing = hidden_rows(
        lengths, mixed, tokens, output_weight, norms, centroids, target_row, target_column
    )
    arrived = dispatch(outgoing)
    back, down, up = expert(
        me, place, arrived, arrived_cotangent, centroids, up_weight[0], down_weight[0], shares
    )
    down_line, up_line = LineSum(down, "dp", place), LineSum(up, "dp", place)
    last = shares - 1
    down_line.send(0, last, LEAD)
    up_line.send(0, last, LEAD)
    returned = dispatch(back)
    layer_output, residual_grad, mixed_grad, output_grad, second_gains = combine(
        lengths,
        returned,
        target_column,
        cotangent,
        residual,
        gate,
        norms,
        centroids,
        mixed,
        output_weight,
    )
    mixed_grad = down_line.hold([(0, last)], mixed_grad)
    if shares > 2:
        down_line.send(1, last, min(LEAD, shares - 2))
    query, key, value = attend_back(lengths, projected, mixed, total, mixed_grad)
    keeps, sends = pack(
        me, query, key, value, tokens, norms, output_grad, second_gains, shares, experts
    )
    swap = lambda values, bit: lax.ppermute(values, "expert", partner_pairs("expert", bit))
    pairs = [(keep, swap(send, 1)) for keep, send in zip(keeps, sends)]
    bits = [2**i for i in range(1, (experts - 1).bit_length())]
    orders = [bits, bits[::-1]]
    for level, now in enumerate(zip(*orders)):
        if level == 0:
            pairs = up_line.hold([(0, last)], pairs)
            for number in range(last, max(last - LEAD, 1), -1):
                up_line.send(1, number)
            down_line.send(0, 1)
            up_line.send(0, 1)
        if level == 1:
            pairs = down_line.hold([(1, last)], pairs)
            down_line.send_rest()
        made = halves(me, now, [(0, keep.shape[1]) for keep, _ in pairs], pairs)
        pairs = [(kept, swap(sent, bit)) for (kept, sent), bit in zip(made, now)]
    if shares > 2:
        query = up_line.hold([(1, last)], query)
    up_line.send_rest()
    input_gradient = project_back(query, key, value, tokens, residual_grad, input_weight, norms)
    input_gradient, pairs = lax.optimization_barrier((input_gradient, pairs))
    for each in (down_line, up_line):
        pairs = each.hold([(0, 1)], pairs)
    pairs = down_line.hold([(last - 1, last)], pairs)
    pairs = up_line.hold([(1, 2)], pairs)
    pieces = [kept + got for kept, got in pairs]
    piece = jnp.concatenate(pieces, axis=1)
    over_line = exchange(piece, "dp")
    piece = jnp.sum(over_line.astype(F32), axis=0).astype(BF)
    gathered = exchange(jnp.broadcast_to(piece, (experts, *piece.shape)))
    columns = []
    for core in range(2):
        streams = []
        first = 0
        for (kept, _), order in zip(pairs, orders):
            count = kept.shape[1]
            blocks = []
            for number in range(2 ** len(bits)):
                digits = [(number >> (len(bits) - 1 - level)) & 1 for level in range(len(bits))]
                device = core + sum(digit * bit for digit, bit in zip(digits, order))
                blocks.append(gathered[device, first : first + count])
            streams.append(jnp.concatenate(blocks, axis=0))
            first += count
        columns.append(jnp.concatenate(streams, axis=0))
    summed = jnp.concatenate(columns, axis=1).astype(F32)
    input_share = jnp.concatenate(
        [summed[number * share : (number + 1) * share] for number in range(3)], axis=1
    )
    output_share = summed[3 * share : 4 * share]
    begin = lax.axis_index("dp") * share
    mine = lambda vector: lax.dynamic_slice_in_dim(vector, begin, share, vector.ndim - 1)
    tail = summed[4 * share : 4 * share + 5]
    weight_share = lax.dynamic_slice_in_dim(input_weight, begin, share, 0).astype(F32)
    shift_sum = jnp.sum(weight_share * tail[:3].reshape(1, 3 * width), axis=1)
    gain_sum = jnp.sum(weight_share * input_share, axis=1)
    gain_sum = (gain_sum - mine(first_shift) * shift_sum) / mine(first_gain)
    second = mine(tail[3:5])
    return (
        layer_output,
        input_gradient,
        input_share,
        output_share,
        gain_sum,
        shift_sum,
        second[0],
        second[1],
        up_line.total()[None],
        down_line.total()[None],
    )


def solution(mesh):
    both = P(("dp", "expert"))
    rows = P(("dp", "expert"), None)
    weights = P("expert", None, None)
    return jax.shard_map(
        on_device,
        mesh=mesh,
        in_specs=(rows, both, both, P(), P(), P(), P(), P(), P(), P(), weights, weights, rows),
        out_specs=(
            rows,
            rows,
            P("dp", None),
            P("dp", None),
            P("dp"),
            P("dp"),
            P("dp"),
            P("dp"),
            P("expert", "dp", None),
            P("expert", "dp", None),
        ),
        check_vma=False,
    )
```

```python
import functools

import jax
import jax.numpy as jnp
from jax import lax
from jax.experimental import pallas as pl
from jax.experimental.pallas import tpu as pltpu
from jax.sharding import PartitionSpec as P

HEADS = 12
EPS = 1e-05
EXCLUDED = -1e30
BF = jnp.bfloat16
F32 = jnp.float32
QUERY_ROWS = 256
SEEN = 1
EXPERT_MIB = 54
HIDDEN_MIB = 60


def dot(left, right, left_axis=1, right_axis=0):
    return lax.dot_general(
        left,
        right,
        (((left_axis,), (right_axis,)), ((), ())),
        preferred_element_type=F32,
    )


def params(limit=60):
    return pltpu.CompilerParams(vmem_limit_bytes=limit << 20)


def cost(flops, bytes_accessed, transcendentals=0):
    return pl.CostEstimate(
        flops=int(flops * SEEN),
        bytes_accessed=int(bytes_accessed * SEEN),
        transcendentals=int(transcendentals * SEEN),
    )


def split_three(values):
    high = values.astype(BF)
    rest = values - high.astype(F32)
    middle = rest.astype(BF)
    return high, middle, (rest - middle.astype(F32)).astype(BF)


def normalise(values):
    average = jnp.mean(values, axis=-1, keepdims=True)
    centred = values - average
    variance = jnp.mean(centred * centred, axis=-1, keepdims=True)
    inverse = lax.rsqrt(variance + EPS)
    return centred * inverse, inverse


def norm_backward(normal, inverse, gain, gradient):
    scaled = gain * gradient
    first = jnp.mean(scaled, axis=-1, keepdims=True)
    second = jnp.mean(scaled * normal, axis=-1, keepdims=True)
    return (scaled - first - normal * second) * inverse


def selection(target, first, count):
    rows = lax.broadcasted_iota(jnp.int32, (count, target.shape[1]), 0) + first
    return jnp.where(rows == target, 1.0, 0.0).astype(BF)


def route_kernel(length_ref, expert_ref, cotangent_ref, out_ref, row_ref, column_ref, *, experts):
    step = pl.program_id(0)
    rows = cotangent_ref.shape[0]
    block = out_ref.shape[0]

    @pl.when(step == 0)
    def _():
        length = length_ref[0]
        position = lax.broadcasted_iota(jnp.int32, (1, rows), 1)
        named = jnp.where(position < length, expert_ref[...], -1)
        number = lax.broadcasted_iota(jnp.int32, (experts, rows), 0)
        onehot = jnp.where(number == named, 1.0, 0.0)
        before = lax.broadcasted_iota(jnp.int32, (rows, rows), 0)
        after = lax.broadcasted_iota(jnp.int32, (rows, rows), 1)
        earlier = jnp.where(before < after, 1.0, 0.0).astype(BF)
        counts = dot(onehot.astype(BF), earlier)
        slot = jnp.sum(onehot * counts, axis=0, keepdims=True).astype(jnp.int32)
        target = jnp.where(named >= 0, named * (rows // experts) + slot, -1)
        row_ref[...] = jnp.broadcast_to(target, row_ref.shape)
        wide = jnp.broadcast_to(target.astype(F32), (128, rows))
        column_ref[...] = wide.T.astype(jnp.int32)

    chosen = selection(row_ref[0:1, :], step * block, block)
    out_ref[...] = dot(chosen, cotangent_ref[...]).astype(BF)


def route(length, expert_index, cotangent, experts):
    rows, width = cotangent.shape
    block = 256
    return pl.pallas_call(
        functools.partial(route_kernel, experts=experts),
        out_shape=[
            jax.ShapeDtypeStruct((rows, width), BF),
            jax.ShapeDtypeStruct((8, rows), jnp.int32),
            jax.ShapeDtypeStruct((rows, 128), jnp.int32),
        ],
        grid_spec=pltpu.PrefetchScalarGridSpec(
            num_scalar_prefetch=1,
            grid=(rows // block,),
            in_specs=[
                pl.BlockSpec((1, rows), lambda i, l: (0, 0)),
                pl.BlockSpec((rows, width), lambda i, l: (0, 0)),
            ],
            out_specs=[
                pl.BlockSpec((block, width), lambda i, l: (i, 0)),
                pl.BlockSpec((8, rows), lambda i, l: (0, 0)),
                pl.BlockSpec((rows, 128), lambda i, l: (0, 0)),
            ],
        ),
        compiler_params=params(60),
        cost_estimate=cost(2 * rows * rows * width, 4 * rows * width),
        name="route",
    )(length, expert_index.reshape(1, rows), cotangent)


def project_kernel(tokens_ref, weight_ref, norms_ref, out_ref):
    normal, _ = normalise(tokens_ref[...].astype(F32))
    normed = (normal * norms_ref[0:1, :] + norms_ref[1:2, :]).astype(BF)
    out_ref[...] = dot(normed, weight_ref[...]).astype(BF)


def project(tokens, weight, norms):
    rows, width = tokens.shape
    columns = weight.shape[1]
    block = 256
    return pl.pallas_call(
        project_kernel,
        out_shape=jax.ShapeDtypeStruct((rows, columns), BF),
        grid=(rows // block,),
        in_specs=[
            pl.BlockSpec((block, width), lambda i: (i, 0)),
            pl.BlockSpec((width, columns), lambda i: (0, 0)),
            pl.BlockSpec((4, width), lambda i: (0, 0)),
        ],
        out_specs=pl.BlockSpec((block, columns), lambda i: (i, 0)),
        compiler_params=params(24),
        cost_estimate=cost(2 * rows * width * columns, 2 * (rows + width) * columns),
        name="project",
    )(tokens, weight, norms)


def staggered(items, begin, finish, ahead=1):
    waiting = []
    for item in items:
        waiting.append((item, begin(item)))
        if len(waiting) > ahead:
            finish(*waiting.pop(0))
    for item, values in waiting:
        finish(item, values)


def length_bias(rows, length):
    row = lax.broadcasted_iota(jnp.int32, (rows, 1), 0)
    return jnp.where(row < length, 0.0, EXCLUDED).astype(BF)


def attend_kernel(length_ref, query_ref, key_ref, value_ref, mixed_ref, total_ref, *, scale, half):
    rows = query_ref.shape[0]
    lane = lax.broadcasted_iota(jnp.int32, (1, 2 * half), 1)
    zero, one = jnp.zeros((), BF), jnp.ones((), BF)
    bias = length_bias(rows, length_ref[0])
    done = {}
    place = lax.broadcasted_iota(jnp.int32, (1, 128), 1)
    first = 2 * pl.program_id(0)
    keys = [jnp.where(lane == half * (1 - head), bias, key_ref[...]) for head in range(2)]

    def scores_of(item):
        start, head = item
        end = start + QUERY_ROWS
        row = lax.broadcasted_iota(jnp.int32, (QUERY_ROWS, QUERY_ROWS), 0)
        column = lax.broadcasted_iota(jnp.int32, (QUERY_ROWS, QUERY_ROWS), 1)
        scaled = query_ref[start:end, :] * jnp.asarray(scale, BF)
        rest = jnp.where(lane == half * (1 - head), one, zero)
        scores = dot(jnp.where((lane // half) == head, scaled, rest), keys[head][:end], 1, 1)
        last = jnp.where(column <= row, scores[:, start:], EXCLUDED)
        return jnp.concatenate([scores[:, :start], last], axis=1) if start else last

    def mix(item, scores):
        start, head = item
        end = start + QUERY_ROWS
        other = half * (1 - head)
        ones = jnp.where(lane == other, one, zero)
        value = jnp.where((lane // half) == head, value_ref[:end, :], ones)
        top = jnp.max(scores, axis=1, keepdims=True)
        out = dot(jnp.exp(scores - top).astype(BF), value)
        total = out[:, other : other + 1]
        done[item] = (out / total, top + jnp.log(total))
        if head == 1:
            low, high = done[start, 0], done[start, 1]
            mixed_ref[start:end, :] = jnp.where(lane < half, low[0], high[0]).astype(BF)
            other = jnp.where(place == first + 1, high[1], total_ref[start:end, :])
            total_ref[start:end, :] = jnp.where(place == first, low[1], other)

    starts = range(0, rows, QUERY_ROWS)
    staggered([(start, head) for start in starts for head in range(2)], scores_of, mix, 2)


def pair_specs(rows, wide, pairs, thirds):
    return [pl.BlockSpec((rows, wide), lambda i, l, o=o: (0, i + o * pairs)) for o in range(thirds)]


def attend(length, projected):
    rows, width = projected.shape[0], projected.shape[1] // 3
    size = width // HEADS
    pairs = HEADS // 2
    one = pl.BlockSpec((rows, 2 * size), lambda i, l: (0, i))
    return pl.pallas_call(
        functools.partial(attend_kernel, scale=size**-0.5, half=size),
        out_shape=[
            jax.ShapeDtypeStruct((rows, width), BF),
            jax.ShapeDtypeStruct((rows, 128), F32),
        ],
        grid_spec=pltpu.PrefetchScalarGridSpec(
            num_scalar_prefetch=1,
            grid=(pairs,),
            in_specs=pair_specs(rows, 2 * size, pairs, 3),
            out_specs=[one, pl.BlockSpec((rows, 128), lambda i, l: (0, 0))],
        ),
        compiler_params=params(16),
        cost_estimate=cost(
            16 * rows * rows * width, 12 * rows * width, HEADS * rows * rows // 2
        ),
        name="attend",
    )(length, projected, projected, projected)


def attend_back_kernel(
    length_ref,
    query_ref,
    key_ref,
    value_ref,
    mixed_ref,
    total_ref,
    incoming_ref,
    out_ref,
    key_sum,
    value_sum,
    *,
    scale,
    half,
):
    lane = lax.broadcasted_iota(jnp.int32, (1, 2 * half), 1)
    bias = length_bias(query_ref.shape[0], length_ref[0])
    zero, one = jnp.zeros((), BF), jnp.ones((), BF)
    key_sum[...] = jnp.zeros_like(key_sum)
    value_sum[...] = jnp.zeros_like(value_sum)
    parts = {}

    def products(item):
        start, head = item
        end = start + QUERY_ROWS
        mine = (lane // half) == head
        other = half * (1 - head)
        ones = jnp.where((lane >= other) & (lane < other + 3), one, zero)

        def extend(base, column, spare):
            a, b, c = split_three(-column)
            rest = jnp.where(lane == other + 2, c, jnp.where(lane == other + 3, spare, zero))
            rest = jnp.where(lane == other + 1, b, rest)
            return jnp.where(mine, base, jnp.where(lane == other, a, rest))

        row = lax.broadcasted_iota(jnp.int32, (QUERY_ROWS, QUERY_ROWS), 0)
        column = lax.broadcasted_iota(jnp.int32, (QUERY_ROWS, QUERY_ROWS), 1)
        incoming = incoming_ref[start:end, :]
        product = incoming.astype(F32) * mixed_ref[start:end, :].astype(F32)
        query = jnp.where(mine, query_ref[start:end, :] * jnp.asarray(scale, BF), zero)
        grad = jnp.where(mine, incoming, zero)
        inner = jnp.sum(jnp.where(mine, product, 0.0), axis=1, keepdims=True)
        at = lax.broadcasted_iota(jnp.int32, (1, 128), 1) == 2 * pl.program_id(0) + head
        total = jnp.sum(jnp.where(at, total_ref[start:end, :], 0.0), axis=1, keepdims=True)
        spare = jnp.where(lane == other + 3, bias[:end], ones)
        key = jnp.where(mine, key_ref[:end, :], spare)
        scores = dot(key, extend(query, total, one), 1, 1)
        last = jnp.where(row <= column, scores[start:, :], EXCLUDED)
        scores = jnp.concatenate([scores[:start, :], last], axis=0) if start else last
        value = jnp.where(mine, value_ref[:end, :], ones)
        return scores, dot(value, extend(grad, inner, zero), 1, 1), query, grad

    def gradients(item, values):
        start, head = item
        scores, centred, query, grad = values
        end = start + QUERY_ROWS
        probs = jnp.exp(scores)
        score_gradient = (probs * centred).astype(BF)
        value_sum[:end, :] += dot(probs.astype(BF), grad)
        key_sum[:end, :] += dot(score_gradient, query)
        key = jnp.where((lane // half) == head, key_ref[:end, :], zero)
        parts[item] = dot(score_gradient, key, 0, 0)
        if head == 1:
            total = parts[start, 0] + parts[start, 1]
            out_ref[0, start:end, :] = (total * scale).astype(BF)

    starts = range(0, query_ref.shape[0], QUERY_ROWS)
    staggered([(start, head) for start in starts for head in range(2)], products, gradients)
    out_ref[1] = key_sum[...].astype(BF)
    out_ref[2] = value_sum[...].astype(BF)


def attend_back(length, projected, mixed, total, incoming):
    rows, width = projected.shape[0], projected.shape[1] // 3
    size = width // HEADS
    pairs = HEADS // 2
    one = pl.BlockSpec((rows, 2 * size), lambda i, l: (0, i))
    return pl.pallas_call(
        functools.partial(attend_back_kernel, scale=size**-0.5, half=size),
        out_shape=jax.ShapeDtypeStruct((3, rows, width), BF),
        grid_spec=pltpu.PrefetchScalarGridSpec(
            num_scalar_prefetch=1,
            grid=(pairs,),
            in_specs=pair_specs(rows, 2 * size, pairs, 3)
            + [one, pl.BlockSpec((rows, 128), lambda i, l: (0, 0)), one],
            out_specs=pl.BlockSpec((3, rows, 2 * size), lambda i, l: (0, 0, i)),
            scratch_shapes=[pltpu.VMEM((rows, 2 * size), F32)] * 2,
        ),
        compiler_params=params(24),
        cost_estimate=cost(
            30 * rows * rows * width, 20 * rows * width, HEADS * rows * rows // 2
        ),
        name="attend_back",
    )(length, projected, projected, projected, mixed, total, incoming)


def picked_rows(target, centroids_ref, capacity):
    experts, width = centroids_ref.shape
    pieces = [piece.astype(F32) for piece in split_three(centroids_ref[...])]
    rest = jnp.zeros((128 - 3 * experts, width), F32)
    table = jnp.concatenate(pieces + [rest], axis=0).astype(BF)
    lane = lax.broadcasted_iota(jnp.int32, (1, 128), 1)
    low = jnp.where(lane < 3 * experts, (lane % experts) * capacity, 1 << 20)
    onehot = jnp.where((target >= low) & (target < low + capacity), 1.0, 0.0).astype(BF)
    return dot(onehot, table)


def present_rows(block_index, count, length):
    row = lax.broadcasted_iota(jnp.int32, (count, 1), 0) + block_index * count
    return jnp.where(row < length, 1.0, 0.0)


def hidden_kernel(
    length_ref,
    mixed_ref,
    tokens_ref,
    weight_ref,
    norms_ref,
    centroids_ref,
    row_ref,
    column_ref,
    residual_ref,
    gate_ref,
    out_ref,
    hidden_low,
):
    rows = row_ref.shape[1]
    count = 256

    def branch_of(number):
        return dot(mixed_ref[number * count : (number + 1) * count, :], weight_ref[...])

    def finish(number, branch):
        at = slice(number * count, (number + 1) * count)
        mask = present_rows(number, count, length_ref[0])
        residual = tokens_ref[at, :].astype(F32) + mask * branch
        residual_ref[at, :] = residual
        normal, _ = normalise(residual)
        hidden = normal * norms_ref[2:3, :] + norms_ref[3:4, :]
        picked = picked_rows(column_ref[at, :], centroids_ref, rows // centroids_ref.shape[0])
        gate = jax.nn.sigmoid(jnp.sum(hidden * picked, axis=-1, keepdims=True))
        gate_ref[at, :] = jnp.broadcast_to(gate, (count, 128))
        hidden_low[at, :] = hidden.astype(BF)

    staggered(range(rows // count), branch_of, finish)

    @pl.loop(0, rows // (2 * count))
    def _(number):
        for part in range(2):
            first = pl.multiple_of((2 * number + part) * count, count)
            chosen = selection(row_ref[0:1, :], first, count)
            out_ref[pl.ds(first, count), :] = dot(chosen, hidden_low[...]).astype(BF)


def hidden_rows(length, mixed, tokens, weight, norms, centroids, target_row, target_column):
    rows, width = tokens.shape
    experts = centroids.shape[0]
    whole = lambda *shape: pl.BlockSpec(shape, lambda i, l: (0,) * len(shape))
    return pl.pallas_call(
        hidden_kernel,
        out_shape=[
            jax.ShapeDtypeStruct((rows, width), F32),
            jax.ShapeDtypeStruct((rows, 128), F32),
            jax.ShapeDtypeStruct((rows, width), BF),
        ],
        grid_spec=pltpu.PrefetchScalarGridSpec(
            num_scalar_prefetch=1,
            grid=(1,),
            in_specs=[
                whole(rows, width),
                whole(rows, width),
                whole(width, width),
                whole(4, width),
                whole(experts, width),
                whole(8, rows),
                whole(rows, 128),
            ],
            out_specs=[whole(rows, width), whole(rows, 128), whole(rows, width)],
            scratch_shapes=[pltpu.VMEM((rows, width), BF)],
        ),
        compiler_params=params(HIDDEN_MIB),
        cost_estimate=cost(2 * rows * (rows + width) * width, 12 * rows * width),
        name="hidden_rows",
    )(length, mixed, tokens, weight, norms, centroids, target_row, target_column)


LINE = 4
MIDDLE = 2


def far_first(number, place, shares):
    return jnp.where(place < shares // 2, shares - 1 - number, number)


def expert_kernel(
    me_ref,
    place_ref,
    rows_ref,
    cotangent_ref,
    centroids_ref,
    up_ref,
    down_ref,
    back_ref,
    *refs,
    shares,
    together,
):
    outs, scratch = refs[:-7], refs[-7:]
    produced_sum, back_sum, transposed, gradient, downs, ups, sems = scratch
    step = pl.program_id(0)
    width = rows_ref.shape[1]
    share = width // shares

    @pl.when(step == 0)
    def _():
        hidden = rows_ref[...].astype(F32)
        centroid = centroids_ref[pl.ds(me_ref[0], 1), :]
        gate = jax.nn.sigmoid(jnp.sum(hidden * centroid, axis=-1, keepdims=True))
        gradient[...] = (gate * cotangent_ref[...].astype(F32)).astype(BF)
        produced_sum[...] = jnp.zeros_like(produced_sum)
        back_sum[...] = jnp.zeros_like(back_sum)
        values = rows_ref[...].T
        for number in range(shares):
            to = pl.multiple_of(far_first(number, place_ref[0], shares) * share, 16)
            transposed[pl.ds(to, share), :] = values[number * share : (number + 1) * share]

    upper = dot(rows_ref[...], up_ref[...])
    part = 0.5 + 0.5 * lax.erf(upper * (0.5**0.5))
    density = jnp.exp(upper * upper * -0.5) * 0.3989422804014327
    active = (upper * part).astype(BF)
    slope = part + upper * density
    active_gradient = dot(gradient[...], down_ref[...], 1, 1)
    upper_gradient = (active_gradient * slope).astype(BF)
    produced_sum[...] += dot(active, down_ref[...])
    down = dot(active, gradient[...], 0, 0).astype(BF)
    back_sum[...] += dot(upper_gradient, up_ref[...], 1, 1)
    up = dot(transposed[...], upper_gradient).astype(BF)
    real = far_first(step, place_ref[0], shares)
    slot = lax.rem(step, 2)
    pieces = down.shape[0] // share
    places = out_places(shares, pieces, together)

    def down_copy(number, slot):
        target = outs[places[number][0][0]].at[pl.ds(0, pieces)]
        return pltpu.make_async_copy(downs.at[slot], target, sems.at[slot, shares])

    def up_copy(number, slot, piece):
        array, first = places[number][1]
        target = outs[array].at[first + piece]
        return pltpu.make_async_copy(ups.at[slot, number], target, sems.at[slot, number])

    def wait(slot):
        down_copy(0, slot).wait()
        for number in range(shares):
            up_copy(number, slot, 0).wait()

    @pl.when(step >= 2)
    def _():
        wait(slot)

    for piece in range(pieces):
        downs[slot, piece] = down[piece * share : (piece + 1) * share]
    for number in range(shares):
        ups[slot, number] = up[number * share : (number + 1) * share]
        up_copy(number, slot, real).start()

        @pl.when(step == number)
        def _(number=number):
            down_copy(number, slot).start()

    @pl.when(step == pl.num_programs(0) - 1)
    def _():
        back_ref[:, :width] = produced_sum[...].astype(BF)
        back_ref[:, width:] = back_sum[...].astype(BF)
        wait(1 - slot)
        wait(slot)


def out_places(shares, pieces, together):
    places, count = [], 0
    for number in range(shares):
        if together and number != MIDDLE:
            places.append(((count, 0), (count, pieces)))
            count += 1
        else:
            places.append(((count, 0), (count + 1, 0)))
            count += 2
    return places


def expert(me, place, hidden, cotangent, centroids, up, down, shares):
    count, width = hidden.shape
    inner = up.shape[1]
    chunk, share = inner // shares, width // shares
    together = shares == LINE and chunk == width
    still = lambda c, m, p: (0, 0)
    once = pl.Buffered(1)
    whole = pl.BlockSpec((count, width), still, pipeline_mode=once)
    real = lambda c, p: far_first(c, p[0], shares)
    pieces = chunk // share
    places = out_places(shares, pieces, together)
    shapes = []
    for number in range(shares):
        if together and number != MIDDLE:
            shapes.append((pieces + shares, share, width))
        else:
            shapes += [(pieces, share, width), (shares, share, chunk)]
    outs = pl.pallas_call(
        functools.partial(expert_kernel, shares=shares, together=together),
        out_shape=[jax.ShapeDtypeStruct((count, 2 * width), BF)]
        + [jax.ShapeDtypeStruct(shape, BF) for shape in shapes],
        grid_spec=pltpu.PrefetchScalarGridSpec(
            num_scalar_prefetch=2,
            grid=(shares,),
            in_specs=[
                whole,
                whole,
                pl.BlockSpec(centroids.shape, still, pipeline_mode=once),
                pl.BlockSpec((width, chunk), lambda c, m, p: (0, real(c, p))),
                pl.BlockSpec((chunk, width), lambda c, m, p: (real(c, p), 0)),
            ],
            out_specs=[pl.BlockSpec((count, 2 * width), still, pipeline_mode=once)]
            + [pl.BlockSpec(memory_space=pl.ANY)] * len(shapes),
            scratch_shapes=[
                pltpu.VMEM((count, width), F32),
                pltpu.VMEM((count, width), F32),
                pltpu.VMEM((width, count), BF),
                pltpu.VMEM((count, width), BF),
                pltpu.VMEM((2, pieces, share, width), BF),
                pltpu.VMEM((2, shares, share, chunk), BF),
                pltpu.SemaphoreType.DMA((2, shares + 1)),
            ],
        ),
        compiler_params=params(EXPERT_MIB),
        cost_estimate=cost(12 * count * width * inner, 8 * inner * width, 2 * count * inner),
        name="expert",
    )(me, place, hidden, cotangent, centroids, up, down)
    back, arrays = outs[0], outs[1:]
    return back, [[(arrays[number], first) for number, first in pair] for pair in places]


def combine_kernel(
    length_ref,
    returned_ref,
    column_ref,
    cotangent_ref,
    residual_ref,
    gate_ref,
    norms_ref,
    centroids_ref,
    mixed_ref,
    weight_ref,
    layer_ref,
    residual_grad_ref,
    mixed_grad_ref,
    weight_grad_ref,
    gains_ref,
    weight_sum,
):
    step = pl.program_id(0)
    count, width = cotangent_ref.shape
    slots = returned_ref.shape[0]

    @pl.when(step == 0)
    def _():
        weight_sum[...] = jnp.zeros_like(weight_sum)
        gains_ref[...] = jnp.zeros_like(gains_ref)

    target = column_ref[:, 0:1]
    place = lax.broadcasted_iota(jnp.int32, (count, slots), 1)
    chosen = jnp.where(place == target, 1.0, 0.0).astype(BF)
    term = dot(chosen, returned_ref[:, :width])
    back = dot(chosen, returned_ref[:, width:])
    mask = present_rows(step, count, length_ref[0])
    gate = gate_ref[:, 0:1]
    cotangent = cotangent_ref[...].astype(F32)
    residual = residual_ref[...]
    layer_ref[...] = (residual + mask * gate * term).astype(BF)
    along = jnp.sum(cotangent * term, axis=-1, keepdims=True)
    logit_gradient = mask * along * gate * (1.0 - gate)
    picked = picked_rows(column_ref[...], centroids_ref, slots // centroids_ref.shape[0])
    hidden_gradient = back + logit_gradient * picked
    normal, inverse = normalise(residual)
    gains_ref[0:1, :] += jnp.sum(hidden_gradient * normal, axis=0, keepdims=True)
    gains_ref[1:2, :] += jnp.sum(hidden_gradient, axis=0, keepdims=True)
    residual_gradient = cotangent + norm_backward(
        normal, inverse, norms_ref[2:3, :], hidden_gradient
    )
    residual_grad_ref[...] = residual_gradient
    branch_gradient = (mask * residual_gradient).astype(BF)
    mixed_grad_ref[...] = dot(branch_gradient, weight_ref[...], 1, 1).astype(BF)
    weight_sum[...] += dot(mixed_ref[...], branch_gradient, 0, 0)

    @pl.when(step == pl.num_programs(0) - 1)
    def _():
        weight_grad_ref[...] = weight_sum[...].astype(BF)


def combine(
    length, returned, target_column, cotangent, residual, gate, norms, centroids, mixed, weight
):
    rows, width = cotangent.shape
    experts = centroids.shape[0]
    block = 256
    part = pl.BlockSpec((block, width), lambda i, l: (i, 0))
    thin = pl.BlockSpec((block, 128), lambda i, l: (i, 0))
    still = lambda i, l: (0, 0)
    return pl.pallas_call(
        combine_kernel,
        out_shape=[
            jax.ShapeDtypeStruct((rows, width), BF),
            jax.ShapeDtypeStruct((rows, width), F32),
            jax.ShapeDtypeStruct((rows, width), BF),
            jax.ShapeDtypeStruct((width, width), BF),
            jax.ShapeDtypeStruct((8, width), F32),
        ],
        grid_spec=pltpu.PrefetchScalarGridSpec(
            num_scalar_prefetch=1,
            grid=(rows // block,),
            in_specs=[
                pl.BlockSpec((rows, 2 * width), still),
                thin,
                part,
                part,
                thin,
                pl.BlockSpec((4, width), still),
                pl.BlockSpec((experts, width), still),
                part,
                pl.BlockSpec((width, width), still),
            ],
            out_specs=[
                part,
                part,
                part,
                pl.BlockSpec((width, width), still),
                pl.BlockSpec((8, width), still),
            ],
            scratch_shapes=[pltpu.VMEM((width, width), F32)],
        ),
        compiler_params=params(60),
        cost_estimate=cost(4 * rows * (rows + width) * width, 24 * rows * width),
        name="combine",
    )(
        length,
        returned,
        target_column,
        cotangent,
        residual,
        gate,
        norms,
        centroids,
        mixed,
        weight,
    )


def packed_rows(share, devices):
    unit = 16 * max(1, devices // 2)
    units = -(-(4 * share + 5) // unit)
    return [-(-units // 2) * unit, units // 2 * unit]


def pack_kernel(
    me_ref,
    grads_ref,
    tokens_ref,
    norms_ref,
    output_grad_ref,
    second_ref,
    *refs,
    shares,
):
    keeps, sends, (normed, sums, product) = refs[0:2], refs[2:4], refs[4:]
    step = pl.program_id(0)
    width = tokens_ref.shape[1]
    share = width // shares
    half = width // 2
    upper = (me_ref[0] & 1) != 0

    def put(number, first, values):
        border = keeps[0].shape[1]
        low, high = values[:, :half], values[:, half:]
        keep = jnp.where(upper, high, low).astype(BF)
        send = jnp.where(upper, low, high).astype(BF)
        for stream, (begin, end) in enumerate(((0, border), (border, 1 << 30))):
            a, b = max(first, begin), min(first + values.shape[0], end)
            if a < b:
                keeps[stream][number, a - begin : b - begin, :] = keep[a - first : b - first]
                sends[stream][number, a - begin : b - begin, :] = send[a - first : b - first]

    @pl.when(step == 0)
    def _():
        for first in range(0, tokens_ref.shape[0], 256):
            at = slice(first, first + 256)
            normal, _ = normalise(tokens_ref[at, :].astype(F32))
            low = (normal * norms_ref[0:1, :] + norms_ref[1:2, :]).astype(BF)
            normed[:, at] = low.T

    product[...] = dot(normed[...], grads_ref[...])
    sums[pl.ds(step, 1), :] = jnp.sum(grads_ref[...].astype(F32), axis=0, keepdims=True)
    for third in range(3):

        @pl.when(step == third)
        def _(third=third):
            @pl.loop(0, shares)
            def _(number):
                first = pl.multiple_of(number * share, 16)
                put(number, third * share, product[pl.ds(first, share), :])

    @pl.when(step == pl.num_programs(0) - 1)
    def _():
        total_rows = keeps[0].shape[1] + keeps[1].shape[1]
        rest = jnp.zeros((total_rows - 4 * share - 5, width), F32)
        tail = jnp.concatenate([sums[0:3, :], second_ref[0:2, :], rest], axis=0)

        @pl.loop(0, shares)
        def _(number):
            first = pl.multiple_of(number * share, 16)
            put(number, 3 * share, output_grad_ref[pl.ds(first, share), :].astype(F32))
            put(number, 4 * share, tail)


def pack(me, grads, tokens, norms, output_grad, second, shares, devices):
    rows, width = tokens.shape
    shapes = [(shares, count, width // 2) for count in packed_rows(width // shares, devices)] * 2
    whole = lambda shape: pl.BlockSpec(shape, lambda i, m: (0,) * len(shape))
    outs = pl.pallas_call(
        functools.partial(pack_kernel, shares=shares),
        out_shape=[jax.ShapeDtypeStruct(shape, BF) for shape in shapes],
        grid_spec=pltpu.PrefetchScalarGridSpec(
            num_scalar_prefetch=1,
            grid=(3,),
            in_specs=[
                pl.BlockSpec((None, rows, width), lambda i, m: (i, 0, 0)),
                whole((rows, width)),
                whole((4, width)),
                whole((width, width)),
                whole((8, width)),
            ],
            out_specs=[whole(shape) for shape in shapes],
            scratch_shapes=[
                pltpu.VMEM((width, rows), BF),
                pltpu.VMEM((8, width), F32),
                pltpu.VMEM((width, width), F32),
            ],
        ),
        compiler_params=params(40),
        cost_estimate=cost(6 * rows * width * width, 20 * rows * width),
        name="pack",
    )(me, grads, tokens, norms, output_grad, second)
    return outs[:2], outs[2:]


def project_back_kernel(
    grads_ref, tokens_ref, residual_grad_ref, weight_ref, norms_ref, out_ref
):
    width = tokens_ref.shape[1]
    gradient = None
    for number in range(3):
        columns = slice(number * width, (number + 1) * width)
        part = dot(grads_ref[number], weight_ref[:, columns], 1, 1)
        gradient = part if gradient is None else gradient + part
    normal, inverse = normalise(tokens_ref[...].astype(F32))
    input_part = norm_backward(normal, inverse, norms_ref[0:1, :], gradient)
    out_ref[...] = (residual_grad_ref[...] + input_part).astype(BF)


def project_back(grads, tokens, residual_grad, weight, norms):
    rows, width = tokens.shape
    block = 256
    part = pl.BlockSpec((block, width), lambda i: (i, 0))
    return pl.pallas_call(
        project_back_kernel,
        out_shape=jax.ShapeDtypeStruct((rows, width), BF),
        grid=(rows // block,),
        in_specs=[pl.BlockSpec((3, block, width), lambda i: (0, i, 0)), part, part]
        + [pl.BlockSpec(weight.shape, lambda i: (0, 0)), pl.BlockSpec((4, width), lambda i: (0, 0))],
        out_specs=part,
        compiler_params=params(24),
        cost_estimate=cost(18 * rows * width * width, 60 * rows * width),
        name="project_back",
    )(grads, tokens, residual_grad, weight, norms)


def add_kernel(left_ref, right_ref, out_ref):
    out_ref[...] = (left_ref[...].astype(F32) + right_ref[...].astype(F32)).astype(BF)


def add(left, right, pieces):
    (left, i), (right, j) = left, right
    _, rows, columns = left.shape
    half = pieces // 2
    spec = lambda first: pl.BlockSpec((half, rows, columns), lambda a: (first // half + a, 0, 0))
    size = pieces * rows * columns
    return pl.pallas_call(
        add_kernel,
        out_shape=jax.ShapeDtypeStruct((pieces, rows, columns), BF),
        grid=(2,),
        in_specs=[spec(i), spec(j)],
        out_specs=spec(0),
        compiler_params=params(10),
        cost_estimate=cost(0, 0),
        name="add",
    )(left, right)


def total_kernel(place_ref, middle_ref, end_ref, *refs, across):
    arrived, out_ref = refs[:-1], refs[-1]
    end = (place_ref[0] == 0) | (place_ref[0] == LINE - 1)
    rows, columns = middle_ref.shape[1:]
    for piece in range(middle_ref.shape[0]):
        total = jnp.where(end, end_ref[piece].astype(F32), middle_ref[piece].astype(F32))
        for ref in arrived:
            total = total + ref[piece].astype(F32)
        if across:
            out_ref[:, piece * columns : (piece + 1) * columns] = total
        else:
            out_ref[piece * rows : (piece + 1) * rows, :] = total


def line_total(place, middle, end, arrived, across):
    ins = [middle, end, *arrived]
    pieces, rows, columns = middle[0].shape
    shape = (rows, pieces * columns) if across else (pieces * rows, columns)
    half = pieces // 2
    block = (rows, half * columns) if across else (half * rows, columns)
    spec = lambda first: pl.BlockSpec((half, rows, columns), lambda a, p: (first // half + a, 0, 0))
    return pl.pallas_call(
        functools.partial(total_kernel, across=across),
        out_shape=jax.ShapeDtypeStruct(shape, F32),
        grid_spec=pltpu.PrefetchScalarGridSpec(
            num_scalar_prefetch=1,
            grid=(2,),
            in_specs=[spec(first) for _, first in ins],
            out_specs=pl.BlockSpec(block, lambda a, p: (0, a) if across else (a, 0)),
        ),
        compiler_params=params(16),
        cost_estimate=cost(0, 0),
        name="line_total",
    )(place, *[array for array, _ in ins])


class LineSum:
    def __init__(self, pairs, axis, place):
        self.axis, self.place = axis, place
        self.shares = lax.axis_size(axis)
        self.pairs = pairs
        self.line = self.shares == LINE and pairs[0][0][0] is pairs[0][1][0]
        self.got = {}

    def send(self, name, matrix=None):
        if not self.line:
            return
        ends = [(0, 1), (3, 2)]
        middles = [(1, 2), (2, 1)]
        out = [(2, 3), (1, 0)]

        def plus(number, before):
            if matrix is None:
                own = (self.pairs[number][0][0], 0)
                return add(own, (self.got[before], 0), own[0].shape[0])
            own = self.pairs[number][matrix]
            return add(own, (self.got[before], own[1]), self.pairs[MIDDLE][matrix][0].shape[0])

        values, route = {
            "far": lambda: (self.pairs[0][0][0], ends),
            "near": lambda: (self.pairs[1][0][0], ends),
            "own": lambda: (self.pairs[MIDDLE][matrix][0], ends),
            "far_on": lambda: (plus(0, "far"), middles),
            "near_on": lambda: (plus(1, "near"), middles),
            "far_out": lambda: (plus(3, "far_on"), out),
        }[name]()
        key = name if matrix is None else (name, matrix)
        self.got[key] = lax.ppermute(values, self.axis, route)

    def hold(self, name, values):
        if not self.line:
            return values
        self.got[name], values = lax.optimization_barrier((self.got[name], values))
        return values

    def totals(self):
        if self.line:
            sums = []
            for matrix in range(2):
                arrived = [(self.got[name, matrix], 0) for name in ("own", "near_on", "far_out")]
                ins = self.pairs[2][matrix], self.pairs[3][matrix]
                sums.append(line_total(self.place, *ins, arrived, across=matrix == 1))
            return sums
        sums = []
        for matrix in range(2):
            stacked = jnp.stack([pair[matrix][0] for pair in self.pairs])
            total = lax.psum_scatter(stacked, self.axis, scatter_dimension=0).astype(F32)
            pieces, rows, columns = total.shape
            if matrix:
                sums.append(total.swapaxes(0, 1).reshape(rows, pieces * columns))
            else:
                sums.append(total.reshape(pieces * rows, columns))
        return sums


def partner_pairs(axis, bit):
    return [(i, i ^ bit) for i in range(lax.axis_size(axis))]


def halves_kernel(me_ref, *refs, edges, bits):
    streams = len(bits)
    ins, outs = refs[: len(refs) - 2 * streams], refs[len(refs) - 2 * streams :]
    for stream, (first, last) in enumerate(edges):
        keep, got = ins[:2] if len(ins) == 2 else ins[2 * stream : 2 * stream + 2]
        kept, sent = outs[2 * stream : 2 * stream + 2]
        size = (last - first) // 2
        upper = (me_ref[0] // bits[stream]) % 2
        mine = pl.multiple_of(first + upper * size, 16)
        other = pl.multiple_of(first + (1 - upper) * size, 16)
        for at, out in ((mine, kept), (other, sent)):
            total = keep[:, pl.ds(at, size), :].astype(F32) + got[:, pl.ds(at, size), :].astype(F32)
            out[...] = total.astype(BF)


def halves(me, bits, edges, pairs):
    shares = pairs[0][0].shape[0]
    spec = lambda rows, columns: pl.BlockSpec((1, rows, columns), lambda z, m: (z, 0, 0))
    in_specs, out_specs, out_shape = [], [], []
    for keep, _ in pairs:
        in_specs += [spec(*keep.shape[1:])] * 2
    columns = pairs[0][0].shape[2]
    for first, last in edges:
        rows = (last - first) // 2
        out_specs += [spec(rows, columns)] * 2
        out_shape += [jax.ShapeDtypeStruct((shares, rows, columns), BF)] * 2
    size = sum(keep.size for keep, _ in pairs)
    outs = pl.pallas_call(
        functools.partial(halves_kernel, edges=edges, bits=bits),
        out_shape=out_shape,
        grid_spec=pltpu.PrefetchScalarGridSpec(
            num_scalar_prefetch=1, grid=(shares,), in_specs=in_specs, out_specs=out_specs
        ),
        compiler_params=params(20),
        cost_estimate=cost(0, 0),
        name="halves",
    )(me, *[array for pair in pairs for array in pair])
    return [(outs[2 * i], outs[2 * i + 1]) for i in range(len(bits))]


def join_kernel(*refs):
    ins, out_ref = refs[:-1], refs[-1]
    first = 0
    for keep, got in zip(ins[::2], ins[1::2]):
        last = first + keep.shape[1]
        total = keep[...].astype(F32) + got[...].astype(F32)
        out_ref[:, first:last, :] = total.astype(BF)
        first = last


def join(pairs):
    shares, _, columns = pairs[0][0].shape
    rows = sum(keep.shape[1] for keep, _ in pairs)
    size = shares * rows * columns
    return pl.pallas_call(
        join_kernel,
        out_shape=jax.ShapeDtypeStruct((shares, rows, columns), BF),
        compiler_params=params(12),
        cost_estimate=cost(0, 0),
        name="join",
    )(*[array for pair in pairs for array in pair])


def spread_kernel(parts_ref, out_ref):
    total = jnp.sum(parts_ref[...].astype(F32), axis=0).astype(BF)
    for number in range(out_ref.shape[0]):
        out_ref[number] = total


def spread(parts, devices):
    _, rows, columns = parts.shape
    size = parts.size + devices * rows * columns
    return pl.pallas_call(
        spread_kernel,
        out_shape=jax.ShapeDtypeStruct((devices, rows, columns), BF),
        compiler_params=params(12),
        cost_estimate=cost(0, 0),
        name="spread",
    )(parts)


def assemble_kernel(
    place_ref,
    gathered_ref,
    weight_ref,
    norms_ref,
    input_ref,
    output_ref,
    column_ref,
    tail_ref,
    summed,
    *,
    sources,
):
    half = gathered_ref.shape[2]
    share, width = output_ref.shape
    for device, first, count, to, side in sources:
        values = gathered_ref[device, first : first + count, :].astype(F32)
        summed[to : to + count, side * half : (side + 1) * half] = values
    shift_sum = gain_sum = 0.0
    for third in range(3):
        columns = slice(third * width, (third + 1) * width)
        values = summed[third * share : (third + 1) * share, :]
        input_ref[:, columns] = values
        weight = weight_ref[:, columns].astype(F32)
        line = summed[4 * share + third : 4 * share + third + 1, :]
        shift_sum = shift_sum + jnp.sum(weight * line, axis=1, keepdims=True)
        gain_sum = gain_sum + jnp.sum(weight * values, axis=1, keepdims=True)
    output_ref[...] = summed[3 * share : 4 * share, :]
    lane = lax.broadcasted_iota(jnp.int32, (1, 128), 1)
    column_ref[...] = jnp.where(lane == 0, gain_sum, shift_sum)
    tail_ref[...] = summed[4 * share : 4 * share + 8, :]


def assemble(place, gathered, weight, norms, share, orders, streams):
    devices, _, half = gathered.shape
    width = 2 * half
    levels = len(orders[0])
    sources = []
    for side in range(2):
        first, to = 0, 0
        for count, order in zip(streams, orders):
            for number in range(2**levels):
                digits = [(number >> (levels - 1 - level)) & 1 for level in range(levels)]
                device = side + sum(digit * bit for digit, bit in zip(digits, order))
                sources.append((device, first, count, to, side))
                to += count
            first += count
    total = sum(streams) * 2**levels
    whole = lambda shape: pl.BlockSpec(shape, lambda i, p: (0,) * len(shape))
    return pl.pallas_call(
        functools.partial(assemble_kernel, sources=sources),
        out_shape=[
            jax.ShapeDtypeStruct((share, 3 * width), F32),
            jax.ShapeDtypeStruct((share, width), F32),
            jax.ShapeDtypeStruct((share, 128), F32),
            jax.ShapeDtypeStruct((8, width), F32),
        ],
        grid_spec=pltpu.PrefetchScalarGridSpec(
            num_scalar_prefetch=1,
            grid=(1,),
            in_specs=[
                whole(gathered.shape),
                pl.BlockSpec((share, 3 * width), lambda i, p: (p[0], 0)),
                whole(norms.shape),
            ],
            out_specs=[
                whole((share, 3 * width)),
                whole((share, width)),
                whole((share, 128)),
                whole((8, width)),
            ],
            scratch_shapes=[pltpu.VMEM((total, width), F32)],
        ),
        compiler_params=params(24),
        cost_estimate=cost(0, 0),
        name="assemble",
    )(place, gathered, weight, norms)


def on_device(
    tokens,
    lengths,
    expert_index,
    centroids,
    input_weight,
    output_weight,
    first_gain,
    first_shift,
    second_gain,
    second_shift,
    up_weight,
    down_weight,
    cotangent,
):
    rows, width = tokens.shape
    experts = centroids.shape[0]
    capacity = rows // experts
    shares = lax.axis_size("dp")
    share = width // shares
    me = lax.axis_index("expert").reshape(1).astype(jnp.int32)
    place = lax.axis_index("dp").reshape(1).astype(jnp.int32)
    norms = jnp.stack([first_gain, first_shift, second_gain, second_shift])

    def exchange(values, axis="expert"):
        return lax.all_to_all(values, axis, split_axis=0, concat_axis=0, tiled=True)

    def dispatch(values):
        return exchange(values.reshape(experts, capacity, -1)).reshape(rows, -1)

    outgoing_cotangent, target_row, target_column = route(
        lengths, expert_index, cotangent, experts
    )
    arrived_cotangent = dispatch(outgoing_cotangent)
    held_tokens, target_row = lax.optimization_barrier((tokens, target_row))
    projected = project(held_tokens, input_weight, norms)
    mixed, total = attend(lengths, projected)
    mixed, arrived_cotangent = lax.optimization_barrier((mixed, arrived_cotangent))
    residual, gate, outgoing = hidden_rows(
        lengths, mixed, tokens, output_weight, norms, centroids, target_row, target_column
    )
    arrived = dispatch(outgoing)
    order = place if shares == LINE else jnp.full_like(place, shares)
    back, pairs = expert(
        me, order, arrived, arrived_cotangent, centroids, up_weight[0], down_weight[0], shares
    )
    line = LineSum(pairs, "dp", place)
    line.send("far")
    line.send("near")
    returned = dispatch(back)
    layer_output, residual_grad, mixed_grad, output_grad, second_gains = combine(
        lengths,
        returned,
        target_column,
        cotangent,
        residual,
        gate,
        norms,
        centroids,
        mixed,
        output_weight,
    )
    mixed_grad = line.hold("far", mixed_grad)
    line.send("far_on")
    grads = attend_back(lengths, projected, mixed, total, mixed_grad)
    keeps, sends = pack(
        me, grads, tokens, norms, output_grad, second_gains, shares, experts
    )
    swap = lambda values, bit: lax.ppermute(values, "expert", partner_pairs("expert", bit))
    pairs = [(keep, swap(send, 1)) for keep, send in zip(keeps, sends)]
    bits = [2**i for i in range(1, (experts - 1).bit_length())]
    orders = [bits, bits[::-1]]
    for level, now in enumerate(zip(*orders)):
        if level == 0:
            pairs = line.hold("near", pairs)
            line.send("near_on", 0)
            line.send("own", 0)
        made = halves(me, now, [(0, keep.shape[1]) for keep, _ in pairs], pairs)
        pairs = [(kept, swap(sent, bit)) for (kept, sent), bit in zip(made, now)]
        if level == 0:
            kept, got = pairs[0]
            pairs[0] = (line.hold("far_on", kept), got)
            line.send("far_out", 0)
    grads = line.hold(("own", 0), grads)
    input_gradient = project_back(grads, tokens, residual_grad, input_weight, norms)
    input_gradient, pairs = lax.optimization_barrier((input_gradient, pairs))
    for name in ("far_out", "near_on"):
        pairs = line.hold((name, 0), pairs)
    streams = [keep.shape[1] for keep, _ in pairs]
    over_line = exchange(join(pairs), "dp")
    for name in ("far_out", "near_on", "own"):
        line.send(name, 1)
    gathered = exchange(spread(over_line, experts))
    input_share, output_share, sums, tail = assemble(
        place, gathered, input_weight, norms, share, orders, streams
    )
    for name in ("far_out", "near_on", "own"):
        sums = line.hold((name, 1), sums)
    begin = lax.axis_index("dp") * share
    mine = lambda vector: lax.dynamic_slice_in_dim(vector, begin, share, vector.ndim - 1)
    shift_sum = sums[:, 1]
    gain_sum = (sums[:, 0] - mine(first_shift) * shift_sum) / mine(first_gain)
    second = mine(tail[3:5])
    down_share, up_share = line.totals()
    return (
        layer_output,
        input_gradient,
        input_share,
        output_share,
        gain_sum,
        shift_sum,
        second[0],
        second[1],
        up_share[None],
        down_share[None],
    )


def solution(mesh):
    both = P(("dp", "expert"))
    rows = P(("dp", "expert"), None)
    weights = P("expert", None, None)
    return jax.shard_map(
        on_device,
        mesh=mesh,
        in_specs=(rows, both, both, P(), P(), P(), P(), P(), P(), P(), weights, weights, rows),
        out_specs=(
            rows,
            rows,
            P("dp", None),
            P("dp", None),
            P("dp"),
            P("dp"),
            P("dp"),
            P("dp"),
            P("expert", "dp", None),
            P("expert", "dp", None),
        ),
        check_vma=False,
    )
```

```python
import functools

import jax
import jax.numpy as jnp
from jax import lax
from jax.experimental import pallas as pl
from jax.experimental.pallas import tpu as pltpu
from jax.sharding import PartitionSpec as P

HEADS = 12
EPS = 1e-05
EXCLUDED = -1e30
BF = jnp.bfloat16
F32 = jnp.float32
QUERY_ROWS = 256
SEEN = 1
EXPERT_MIB = 54
HIDDEN_MIB = 60
OWN_EARLY = True


def dot(left, right, left_axis=1, right_axis=0):
    return lax.dot_general(
        left,
        right,
        (((left_axis,), (right_axis,)), ((), ())),
        preferred_element_type=F32,
    )


def params(limit=60):
    return pltpu.CompilerParams(vmem_limit_bytes=limit << 20)


def cost(flops, bytes_accessed, transcendentals=0):
    return pl.CostEstimate(
        flops=int(flops * SEEN),
        bytes_accessed=int(bytes_accessed * SEEN),
        transcendentals=int(transcendentals * SEEN),
    )


def split_three(values):
    high = values.astype(BF)
    rest = values - high.astype(F32)
    middle = rest.astype(BF)
    return high, middle, (rest - middle.astype(F32)).astype(BF)


def normalise(values):
    average = jnp.mean(values, axis=-1, keepdims=True)
    centred = values - average
    variance = jnp.mean(centred * centred, axis=-1, keepdims=True)
    inverse = lax.rsqrt(variance + EPS)
    return centred * inverse, inverse


def norm_backward(normal, inverse, gain, gradient):
    scaled = gain * gradient
    first = jnp.mean(scaled, axis=-1, keepdims=True)
    second = jnp.mean(scaled * normal, axis=-1, keepdims=True)
    return (scaled - first - normal * second) * inverse


def selection(target, first, count):
    rows = lax.broadcasted_iota(jnp.int32, (count, target.shape[1]), 0) + first
    return jnp.where(rows == target, 1.0, 0.0).astype(BF)


def route_kernel(length_ref, expert_ref, cotangent_ref, out_ref, row_ref, column_ref, *, experts):
    step = pl.program_id(0)
    rows = cotangent_ref.shape[0]
    block = out_ref.shape[0]

    @pl.when(step == 0)
    def _():
        length = length_ref[0]
        position = lax.broadcasted_iota(jnp.int32, (1, rows), 1)
        named = jnp.where(position < length, expert_ref[...], -1)
        number = lax.broadcasted_iota(jnp.int32, (experts, rows), 0)
        onehot = jnp.where(number == named, 1.0, 0.0)
        before = lax.broadcasted_iota(jnp.int32, (rows, rows), 0)
        after = lax.broadcasted_iota(jnp.int32, (rows, rows), 1)
        earlier = jnp.where(before < after, 1.0, 0.0).astype(BF)
        counts = dot(onehot.astype(BF), earlier)
        slot = jnp.sum(onehot * counts, axis=0, keepdims=True).astype(jnp.int32)
        target = jnp.where(named >= 0, named * (rows // experts) + slot, -1)
        row_ref[...] = jnp.broadcast_to(target, row_ref.shape)
        wide = jnp.broadcast_to(target.astype(F32), (128, rows))
        column_ref[...] = wide.T.astype(jnp.int32)

    chosen = selection(row_ref[0:1, :], step * block, block)
    out_ref[...] = dot(chosen, cotangent_ref[...]).astype(BF)


def route(length, expert_index, cotangent, experts):
    rows, width = cotangent.shape
    block = 256
    return pl.pallas_call(
        functools.partial(route_kernel, experts=experts),
        out_shape=[
            jax.ShapeDtypeStruct((rows, width), BF),
            jax.ShapeDtypeStruct((8, rows), jnp.int32),
            jax.ShapeDtypeStruct((rows, 128), jnp.int32),
        ],
        grid_spec=pltpu.PrefetchScalarGridSpec(
            num_scalar_prefetch=1,
            grid=(rows // block,),
            in_specs=[
                pl.BlockSpec((1, rows), lambda i, l: (0, 0)),
                pl.BlockSpec((rows, width), lambda i, l: (0, 0)),
            ],
            out_specs=[
                pl.BlockSpec((block, width), lambda i, l: (i, 0)),
                pl.BlockSpec((8, rows), lambda i, l: (0, 0)),
                pl.BlockSpec((rows, 128), lambda i, l: (0, 0)),
            ],
        ),
        compiler_params=params(60),
        cost_estimate=cost(2 * rows * rows * width, 4 * rows * width),
        name="route",
    )(length, expert_index.reshape(1, rows), cotangent)


def project_kernel(tokens_ref, weight_ref, norms_ref, out_ref):
    normal, _ = normalise(tokens_ref[...].astype(F32))
    normed = (normal * norms_ref[0:1, :] + norms_ref[1:2, :]).astype(BF)
    out_ref[...] = dot(normed, weight_ref[...]).astype(BF)


def project(tokens, weight, norms):
    rows, width = tokens.shape
    columns = weight.shape[1]
    block = 256
    return pl.pallas_call(
        project_kernel,
        out_shape=jax.ShapeDtypeStruct((rows, columns), BF),
        grid=(rows // block,),
        in_specs=[
            pl.BlockSpec((block, width), lambda i: (i, 0)),
            pl.BlockSpec((width, columns), lambda i: (0, 0)),
            pl.BlockSpec((4, width), lambda i: (0, 0)),
        ],
        out_specs=pl.BlockSpec((block, columns), lambda i: (i, 0)),
        compiler_params=params(24),
        cost_estimate=cost(2 * rows * width * columns, 2 * (rows + width) * columns),
        name="project",
    )(tokens, weight, norms)


def staggered(items, begin, finish, ahead=1):
    waiting = []
    for item in items:
        waiting.append((item, begin(item)))
        if len(waiting) > ahead:
            finish(*waiting.pop(0))
    for item, values in waiting:
        finish(item, values)


def length_bias(rows, length):
    row = lax.broadcasted_iota(jnp.int32, (rows, 1), 0)
    return jnp.where(row < length, 0.0, EXCLUDED).astype(BF)


def attend_kernel(length_ref, query_ref, key_ref, value_ref, mixed_ref, total_ref, *, scale, half):
    rows = query_ref.shape[0]
    lane = lax.broadcasted_iota(jnp.int32, (1, 2 * half), 1)
    zero, one = jnp.zeros((), BF), jnp.ones((), BF)
    bias = length_bias(rows, length_ref[0])
    done = {}
    place = lax.broadcasted_iota(jnp.int32, (1, 128), 1)
    first = 2 * pl.program_id(0)
    keys = [jnp.where(lane == half * (1 - head), bias, key_ref[...]) for head in range(2)]

    def scores_of(item):
        start, head = item
        end = start + QUERY_ROWS
        row = lax.broadcasted_iota(jnp.int32, (QUERY_ROWS, QUERY_ROWS), 0)
        column = lax.broadcasted_iota(jnp.int32, (QUERY_ROWS, QUERY_ROWS), 1)
        scaled = query_ref[start:end, :] * jnp.asarray(scale, BF)
        rest = jnp.where(lane == half * (1 - head), one, zero)
        scores = dot(jnp.where((lane // half) == head, scaled, rest), keys[head][:end], 1, 1)
        last = jnp.where(column <= row, scores[:, start:], EXCLUDED)
        return jnp.concatenate([scores[:, :start], last], axis=1) if start else last

    def mix(item, scores):
        start, head = item
        end = start + QUERY_ROWS
        other = half * (1 - head)
        ones = jnp.where(lane == other, one, zero)
        value = jnp.where((lane // half) == head, value_ref[:end, :], ones)
        top = jnp.max(scores, axis=1, keepdims=True)
        out = dot(jnp.exp(scores - top).astype(BF), value)
        total = out[:, other : other + 1]
        done[item] = (out / total, top + jnp.log(total))
        if head == 1:
            low, high = done[start, 0], done[start, 1]
            mixed_ref[start:end, :] = jnp.where(lane < half, low[0], high[0]).astype(BF)
            other = jnp.where(place == first + 1, high[1], total_ref[start:end, :])
            total_ref[start:end, :] = jnp.where(place == first, low[1], other)

    starts = range(0, rows, QUERY_ROWS)
    staggered([(start, head) for start in starts for head in range(2)], scores_of, mix, 2)


def pair_specs(rows, wide, pairs, thirds):
    return [pl.BlockSpec((rows, wide), lambda i, l, o=o: (0, i + o * pairs)) for o in range(thirds)]


def attend(length, projected):
    rows, width = projected.shape[0], projected.shape[1] // 3
    size = width // HEADS
    pairs = HEADS // 2
    one = pl.BlockSpec((rows, 2 * size), lambda i, l: (0, i))
    return pl.pallas_call(
        functools.partial(attend_kernel, scale=size**-0.5, half=size),
        out_shape=[
            jax.ShapeDtypeStruct((rows, width), BF),
            jax.ShapeDtypeStruct((rows, 128), F32),
        ],
        grid_spec=pltpu.PrefetchScalarGridSpec(
            num_scalar_prefetch=1,
            grid=(pairs,),
            in_specs=pair_specs(rows, 2 * size, pairs, 3),
            out_specs=[one, pl.BlockSpec((rows, 128), lambda i, l: (0, 0))],
        ),
        compiler_params=params(16),
        cost_estimate=cost(
            16 * rows * rows * width, 12 * rows * width, HEADS * rows * rows // 2
        ),
        name="attend",
    )(length, projected, projected, projected)


def attend_back_kernel(
    length_ref,
    query_ref,
    key_ref,
    value_ref,
    mixed_ref,
    total_ref,
    incoming_ref,
    out_ref,
    key_sum,
    value_sum,
    *,
    scale,
    half,
):
    lane = lax.broadcasted_iota(jnp.int32, (1, 2 * half), 1)
    bias = length_bias(query_ref.shape[0], length_ref[0])
    zero, one = jnp.zeros((), BF), jnp.ones((), BF)
    key_sum[...] = jnp.zeros_like(key_sum)
    value_sum[...] = jnp.zeros_like(value_sum)
    parts = {}

    def products(item):
        start, head = item
        end = start + QUERY_ROWS
        mine = (lane // half) == head
        other = half * (1 - head)
        ones = jnp.where((lane >= other) & (lane < other + 3), one, zero)

        def extend(base, column, spare):
            a, b, c = split_three(-column)
            rest = jnp.where(lane == other + 2, c, jnp.where(lane == other + 3, spare, zero))
            rest = jnp.where(lane == other + 1, b, rest)
            return jnp.where(mine, base, jnp.where(lane == other, a, rest))

        row = lax.broadcasted_iota(jnp.int32, (QUERY_ROWS, QUERY_ROWS), 0)
        column = lax.broadcasted_iota(jnp.int32, (QUERY_ROWS, QUERY_ROWS), 1)
        incoming = incoming_ref[start:end, :]
        product = incoming.astype(F32) * mixed_ref[start:end, :].astype(F32)
        query = jnp.where(mine, query_ref[start:end, :] * jnp.asarray(scale, BF), zero)
        grad = jnp.where(mine, incoming, zero)
        inner = jnp.sum(jnp.where(mine, product, 0.0), axis=1, keepdims=True)
        number = 2 * pl.program_id(0) + head
        at = lax.broadcasted_iota(jnp.int32, (1, 128), 1) == number
        total = jnp.sum(jnp.where(at, total_ref[start:end, :], 0.0), axis=1, keepdims=True)
        spare = jnp.where(lane == other + 3, bias[:end], ones)
        key = jnp.where(mine, key_ref[:end, :], spare)
        scores = dot(key, extend(query, total, one), 1, 1)
        last = jnp.where(row <= column, scores[start:, :], EXCLUDED)
        scores = jnp.concatenate([scores[:start, :], last], axis=0) if start else last
        value = jnp.where(mine, value_ref[:end, :], ones)
        return scores, dot(value, extend(grad, inner, zero), 1, 1), query, grad

    def gradients(item, values):
        start, head = item
        scores, centred, query, grad = values
        end = start + QUERY_ROWS
        probs = jnp.exp(scores)
        score_gradient = (probs * centred).astype(BF)
        value_sum[:end, :] += dot(probs.astype(BF), grad)
        key_sum[:end, :] += dot(score_gradient, query)
        key = jnp.where((lane // half) == head, key_ref[:end, :], zero)
        parts[item] = dot(score_gradient, key, 0, 0)
        if head == 1:
            total = parts[start, 0] + parts[start, 1]
            out_ref[0, start:end, :] = (total * scale).astype(BF)

    starts = range(0, query_ref.shape[0], QUERY_ROWS)
    staggered([(start, head) for start in starts for head in range(2)], products, gradients)
    out_ref[1] = key_sum[...].astype(BF)
    out_ref[2] = value_sum[...].astype(BF)


def attend_back(length, projected, mixed, total, incoming):
    rows, width = projected.shape[0], projected.shape[1] // 3
    size = width // HEADS
    pairs = HEADS // 2
    one = pl.BlockSpec((rows, 2 * size), lambda i, l: (0, i))
    return pl.pallas_call(
        functools.partial(attend_back_kernel, scale=size**-0.5, half=size),
        out_shape=jax.ShapeDtypeStruct((3, rows, width), BF),
        grid_spec=pltpu.PrefetchScalarGridSpec(
            num_scalar_prefetch=1,
            grid=(pairs,),
            in_specs=pair_specs(rows, 2 * size, pairs, 3)
            + [one, pl.BlockSpec((rows, 128), lambda i, l: (0, 0)), one],
            out_specs=pl.BlockSpec((3, rows, 2 * size), lambda i, l: (0, 0, i)),
            scratch_shapes=[pltpu.VMEM((rows, 2 * size), F32)] * 2,
        ),
        compiler_params=params(24),
        cost_estimate=cost(
            30 * rows * rows * width, 20 * rows * width
        ),
        name="attend_back",
    )(length, projected, projected, projected, mixed, total, incoming)


def picked_rows(target, centroids_ref, capacity):
    experts, width = centroids_ref.shape
    pieces = [piece.astype(F32) for piece in split_three(centroids_ref[...])]
    rest = jnp.zeros((128 - 3 * experts, width), F32)
    table = jnp.concatenate(pieces + [rest], axis=0).astype(BF)
    lane = lax.broadcasted_iota(jnp.int32, (1, 128), 1)
    low = jnp.where(lane < 3 * experts, (lane % experts) * capacity, 1 << 20)
    onehot = jnp.where((target >= low) & (target < low + capacity), 1.0, 0.0).astype(BF)
    return dot(onehot, table)


def present_rows(block_index, count, length):
    row = lax.broadcasted_iota(jnp.int32, (count, 1), 0) + block_index * count
    return jnp.where(row < length, 1.0, 0.0)


def hidden_kernel(
    length_ref,
    mixed_ref,
    tokens_ref,
    weight_ref,
    norms_ref,
    centroids_ref,
    row_ref,
    column_ref,
    residual_ref,
    gate_ref,
    out_ref,
    hidden_low,
):
    rows = row_ref.shape[1]
    count = 256

    def branch_of(number):
        return dot(mixed_ref[number * count : (number + 1) * count, :], weight_ref[...])

    def finish(number, branch):
        at = slice(number * count, (number + 1) * count)
        mask = present_rows(number, count, length_ref[0])
        residual = tokens_ref[at, :].astype(F32) + mask * branch
        residual_ref[at, :] = residual
        normal, _ = normalise(residual)
        hidden = normal * norms_ref[2:3, :] + norms_ref[3:4, :]
        picked = picked_rows(column_ref[at, :], centroids_ref, rows // centroids_ref.shape[0])
        gate = jax.nn.sigmoid(jnp.sum(hidden * picked, axis=-1, keepdims=True))
        gate_ref[at, :] = jnp.broadcast_to(gate, (count, 128))
        hidden_low[at, :] = hidden.astype(BF)

    staggered(range(rows // count), branch_of, finish)

    @pl.loop(0, rows // (2 * count))
    def _(number):
        for part in range(2):
            first = pl.multiple_of((2 * number + part) * count, count)
            chosen = selection(row_ref[0:1, :], first, count)
            out_ref[pl.ds(first, count), :] = dot(chosen, hidden_low[...]).astype(BF)


def hidden_rows(length, mixed, tokens, weight, norms, centroids, target_row, target_column):
    rows, width = tokens.shape
    experts = centroids.shape[0]
    whole = lambda *shape: pl.BlockSpec(shape, lambda i, l: (0,) * len(shape))
    return pl.pallas_call(
        hidden_kernel,
        out_shape=[
            jax.ShapeDtypeStruct((rows, width), F32),
            jax.ShapeDtypeStruct((rows, 128), F32),
            jax.ShapeDtypeStruct((rows, width), BF),
        ],
        grid_spec=pltpu.PrefetchScalarGridSpec(
            num_scalar_prefetch=1,
            grid=(1,),
            in_specs=[
                whole(rows, width),
                whole(rows, width),
                whole(width, width),
                whole(4, width),
                whole(experts, width),
                whole(8, rows),
                whole(rows, 128),
            ],
            out_specs=[whole(rows, width), whole(rows, 128), whole(rows, width)],
            scratch_shapes=[pltpu.VMEM((rows, width), BF)],
        ),
        compiler_params=params(HIDDEN_MIB),
        cost_estimate=cost(2 * rows * (rows + width) * width, 12 * rows * width),
        name="hidden_rows",
    )(length, mixed, tokens, weight, norms, centroids, target_row, target_column)


LINE = 4
MIDDLE = 2


def far_first(number, place, shares):
    return jnp.where(place < shares // 2, shares - 1 - number, number)


def expert_kernel(
    me_ref,
    place_ref,
    rows_ref,
    cotangent_ref,
    centroids_ref,
    up_ref,
    down_ref,
    produced_ref,
    back_ref,
    *refs,
    shares,
    together,
):
    outs, scratch = refs[:-8], refs[-8:]
    produced_sum, back_sum, transposed, gradient, gates, downs, ups, sems = scratch
    step = pl.program_id(0)
    count, width = rows_ref.shape
    share = width // shares

    @pl.when(step == 0)
    def _():
        hidden = rows_ref[...].astype(F32)
        centroid = centroids_ref[pl.ds(me_ref[0], 1), :]
        gate = jax.nn.sigmoid(jnp.sum(hidden * centroid, axis=-1, keepdims=True))
        gradient[...] = (gate * cotangent_ref[...].astype(F32)).astype(BF)
        gates[...] = jnp.broadcast_to(gate, gates.shape)
        produced_sum[...] = jnp.zeros_like(produced_sum)
        back_sum[...] = jnp.zeros_like(back_sum)
        values = rows_ref[...].T
        for number in range(shares):
            to = pl.multiple_of(far_first(number, place_ref[0], shares) * share, 16)
            transposed[pl.ds(to, share), :] = values[number * share : (number + 1) * share]

    upper = dot(rows_ref[...], up_ref[...])
    part = 0.5 + 0.5 * lax.erf(upper * (0.5**0.5))
    density = jnp.exp(upper * upper * -0.5) * 0.3989422804014327
    active = (upper * part).astype(BF)
    slope = part + upper * density
    active_gradient = dot(gradient[...], down_ref[...], 1, 1)
    upper_gradient = (active_gradient * slope).astype(BF)
    produced_sum[...] += dot(active, down_ref[...])
    down = dot(active, gradient[...], 0, 0).astype(BF)
    back_sum[...] += dot(upper_gradient, up_ref[...], 1, 1)
    up = dot(transposed[...], upper_gradient).astype(BF)
    real = far_first(step, place_ref[0], shares)
    slot = lax.rem(step, 2)
    pieces = down.shape[0] // share
    places = out_places(shares, pieces, together)

    def down_copy(number, slot):
        target = outs[places[number][0][0]].at[pl.ds(0, pieces)]
        return pltpu.make_async_copy(downs.at[slot], target, sems.at[slot, shares])

    def up_copy(number, slot, piece):
        array, first = places[number][1]
        target = outs[array].at[first + piece]
        return pltpu.make_async_copy(ups.at[slot, number], target, sems.at[slot, number])

    def wait(slot):
        down_copy(0, slot).wait()
        for number in range(shares):
            up_copy(number, slot, 0).wait()

    @pl.when(step >= 2)
    def _():
        wait(slot)

    for piece in range(pieces):
        downs[slot, piece] = down[piece * share : (piece + 1) * share]
    for number in range(shares):
        ups[slot, number] = up[number * share : (number + 1) * share]
        up_copy(number, slot, real).start()

        @pl.when(step == number)
        def _(number=number):
            down_copy(number, slot).start()

    @pl.when(step == pl.num_programs(0) - 1)
    def _():
        centroid = centroids_ref[pl.ds(me_ref[0], 1), :]

        @pl.loop(0, count // 256)
        def _(number):
            at = pl.ds(pl.multiple_of(number * 256, 256), 256)
            produced = produced_sum[at, :].astype(BF)
            produced_ref[at, :] = produced
            gate = gates[at, 0:1]
            cotangent = cotangent_ref[at, :].astype(F32)
            along = jnp.sum(cotangent * produced.astype(F32), axis=-1, keepdims=True)
            logit_gradient = along * gate * (1.0 - gate)
            back_ref[at, :] = (back_sum[at, :] + logit_gradient * centroid).astype(BF)
        wait(1 - slot)
        wait(slot)


def out_places(shares, pieces, together):
    places, count = [], 0
    for number in range(shares):
        if together and number != MIDDLE:
            places.append(((count, 0), (count, pieces)))
            count += 1
        else:
            places.append(((count, 0), (count + 1, 0)))
            count += 2
    return places


def expert(me, place, hidden, cotangent, centroids, up, down, shares):
    count, width = hidden.shape
    inner = up.shape[1]
    chunk, share = inner // shares, width // shares
    together = shares == LINE and chunk == width
    still = lambda c, m, p: (0, 0)
    once = pl.Buffered(1)
    whole = pl.BlockSpec((count, width), still, pipeline_mode=once)
    real = lambda c, p: far_first(c, p[0], shares)
    pieces = chunk // share
    places = out_places(shares, pieces, together)
    shapes = []
    for number in range(shares):
        if together and number != MIDDLE:
            shapes.append((pieces + shares, share, width))
        else:
            shapes += [(pieces, share, width), (shares, share, chunk)]
    outs = pl.pallas_call(
        functools.partial(expert_kernel, shares=shares, together=together),
        out_shape=[jax.ShapeDtypeStruct((count, width), BF)] * 2
        + [jax.ShapeDtypeStruct(shape, BF) for shape in shapes],
        grid_spec=pltpu.PrefetchScalarGridSpec(
            num_scalar_prefetch=2,
            grid=(shares,),
            in_specs=[
                whole,
                whole,
                pl.BlockSpec(centroids.shape, still, pipeline_mode=once),
                pl.BlockSpec((width, chunk), lambda c, m, p: (0, real(c, p))),
                pl.BlockSpec((chunk, width), lambda c, m, p: (real(c, p), 0)),
            ],
            out_specs=[whole, whole] + [pl.BlockSpec(memory_space=pl.ANY)] * len(shapes),
            scratch_shapes=[
                pltpu.VMEM((count, width), F32),
                pltpu.VMEM((count, width), F32),
                pltpu.VMEM((width, count), BF),
                pltpu.VMEM((count, width), BF),
                pltpu.VMEM((count, 128), F32),
                pltpu.VMEM((2, pieces, share, width), BF),
                pltpu.VMEM((2, shares, share, chunk), BF),
                pltpu.SemaphoreType.DMA((2, shares + 1)),
            ],
        ),
        compiler_params=params(EXPERT_MIB),
        cost_estimate=cost(12 * count * width * inner, 8 * inner * width, 2 * count * inner),
        name="expert",
    )(me, place, hidden, cotangent, centroids, up, down)
    arrays = outs[2:]
    pairs = [[(arrays[number], first) for number, first in pair] for pair in places]
    return outs[0], outs[1], pairs


def combine_kernel(
    length_ref,
    returned_ref,
    column_ref,
    cotangent_ref,
    residual_ref,
    norms_ref,
    mixed_ref,
    weight_ref,
    residual_grad_ref,
    mixed_grad_ref,
    weight_grad_ref,
    gains_ref,
    weight_sum,
):
    step = pl.program_id(0)
    count = cotangent_ref.shape[0]

    @pl.when(step == 0)
    def _():
        weight_sum[...] = jnp.zeros_like(weight_sum)
        gains_ref[...] = jnp.zeros_like(gains_ref)

    hidden_gradient = gathered_rows(column_ref, returned_ref)
    mask = present_rows(step, count, length_ref[0])
    normal, inverse = normalise(residual_ref[...])
    gains_ref[0:1, :] += jnp.sum(hidden_gradient * normal, axis=0, keepdims=True)
    gains_ref[1:2, :] += jnp.sum(hidden_gradient, axis=0, keepdims=True)
    residual_gradient = cotangent_ref[...].astype(F32) + norm_backward(
        normal, inverse, norms_ref[2:3, :], hidden_gradient
    )
    residual_grad_ref[...] = residual_gradient
    branch_gradient = (mask * residual_gradient).astype(BF)
    mixed_grad_ref[...] = dot(branch_gradient, weight_ref[...], 1, 1).astype(BF)
    weight_sum[...] += dot(mixed_ref[...], branch_gradient, 0, 0)

    @pl.when(step == pl.num_programs(0) - 1)
    def _():
        weight_grad_ref[...] = weight_sum[...].astype(BF)


def gathered_rows(column_ref, slots_ref):
    place = lax.broadcasted_iota(jnp.int32, (column_ref.shape[0], slots_ref.shape[0]), 1)
    chosen = jnp.where(place == column_ref[:, 0:1], 1.0, 0.0).astype(BF)
    return dot(chosen, slots_ref[...])


def combine(length, returned, target_column, cotangent, residual, norms, mixed, weight):
    rows, width = cotangent.shape
    block = 256
    part = pl.BlockSpec((block, width), lambda i, l: (i, 0))
    thin = pl.BlockSpec((block, 128), lambda i, l: (i, 0))
    still = lambda i, l: (0, 0)
    return pl.pallas_call(
        combine_kernel,
        out_shape=[
            jax.ShapeDtypeStruct((rows, width), F32),
            jax.ShapeDtypeStruct((rows, width), BF),
            jax.ShapeDtypeStruct((width, width), BF),
            jax.ShapeDtypeStruct((8, width), F32),
        ],
        grid_spec=pltpu.PrefetchScalarGridSpec(
            num_scalar_prefetch=1,
            grid=(rows // block,),
            in_specs=[
                pl.BlockSpec((rows, width), still),
                thin,
                part,
                part,
                pl.BlockSpec((4, width), still),
                part,
                pl.BlockSpec((width, width), still),
            ],
            out_specs=[
                part,
                part,
                pl.BlockSpec((width, width), still),
                pl.BlockSpec((8, width), still),
            ],
            scratch_shapes=[pltpu.VMEM((width, width), F32)],
        ),
        compiler_params=params(60),
        cost_estimate=cost(4 * rows * (rows + width) * width, 24 * rows * width),
        name="combine",
    )(length, returned, target_column, cotangent, residual, norms, mixed, weight)


def layer_kernel(length_ref, returned_ref, column_ref, residual_ref, gate_ref, out_ref):
    term = gathered_rows(column_ref, returned_ref)
    mask = present_rows(pl.program_id(0), column_ref.shape[0], length_ref[0])
    out_ref[...] = (residual_ref[...] + mask * gate_ref[:, 0:1] * term).astype(BF)


def layer(length, returned, target_column, residual, gate):
    rows, width = residual.shape
    block = 256
    part = pl.BlockSpec((block, width), lambda i, l: (i, 0))
    thin = pl.BlockSpec((block, 128), lambda i, l: (i, 0))
    return pl.pallas_call(
        layer_kernel,
        out_shape=jax.ShapeDtypeStruct((rows, width), BF),
        grid_spec=pltpu.PrefetchScalarGridSpec(
            num_scalar_prefetch=1,
            grid=(rows // block,),
            in_specs=[pl.BlockSpec((rows, width), lambda i, l: (0, 0)), thin, part, thin],
            out_specs=part,
        ),
        compiler_params=params(60),
        cost_estimate=cost(2 * rows * rows * width, 10 * rows * width),
        name="layer",
    )(length, returned, target_column, residual, gate)


def packed_rows(share, devices):
    unit = 16 * max(1, devices // 2)
    units = -(-(4 * share + 5) // unit)
    return [-(-units // 2) * unit, units // 2 * unit]


def pack_kernel(
    me_ref,
    grads_ref,
    tokens_ref,
    norms_ref,
    output_grad_ref,
    second_ref,
    *refs,
    shares,
):
    keeps, sends, (normed, sums, product) = refs[0:2], refs[2:4], refs[4:]
    step = pl.program_id(0)
    width = tokens_ref.shape[1]
    share = width // shares
    half = width // 2
    upper = (me_ref[0] & 1) != 0

    def put(number, first, values):
        border = keeps[0].shape[1]
        low, high = values[:, :half], values[:, half:]
        keep = jnp.where(upper, high, low).astype(BF)
        send = jnp.where(upper, low, high).astype(BF)
        for stream, (begin, end) in enumerate(((0, border), (border, 1 << 30))):
            a, b = max(first, begin), min(first + values.shape[0], end)
            if a < b:
                keeps[stream][number, a - begin : b - begin, :] = keep[a - first : b - first]
                sends[stream][number, a - begin : b - begin, :] = send[a - first : b - first]

    @pl.when(step == 0)
    def _():

        @pl.loop(0, tokens_ref.shape[0] // 256)
        def _(number):
            at = pl.ds(pl.multiple_of(number * 256, 256), 256)
            normal, _ = normalise(tokens_ref[at, :].astype(F32))
            low = (normal * norms_ref[0:1, :] + norms_ref[1:2, :]).astype(BF)
            normed[:, at] = low.T

    product[...] = dot(normed[...], grads_ref[...])
    sums[pl.ds(step, 1), :] = jnp.sum(grads_ref[...].astype(F32), axis=0, keepdims=True)
    for third in range(3):

        @pl.when(step == third)
        def _(third=third):
            @pl.loop(0, shares)
            def _(number):
                first = pl.multiple_of(number * share, 16)
                put(number, third * share, product[pl.ds(first, share), :])

    @pl.when(step == pl.num_programs(0) - 1)
    def _():
        total_rows = keeps[0].shape[1] + keeps[1].shape[1]
        rest = jnp.zeros((total_rows - 4 * share - 5, width), F32)
        tail = jnp.concatenate([sums[0:3, :], second_ref[0:2, :], rest], axis=0)

        @pl.loop(0, shares)
        def _(number):
            first = pl.multiple_of(number * share, 16)
            put(number, 3 * share, output_grad_ref[pl.ds(first, share), :].astype(F32))
            put(number, 4 * share, tail)


def pack(me, grads, tokens, norms, output_grad, second, shares, devices):
    rows, width = tokens.shape
    shapes = [(shares, count, width // 2) for count in packed_rows(width // shares, devices)] * 2
    whole = lambda shape: pl.BlockSpec(shape, lambda i, m: (0,) * len(shape))
    outs = pl.pallas_call(
        functools.partial(pack_kernel, shares=shares),
        out_shape=[jax.ShapeDtypeStruct(shape, BF) for shape in shapes],
        grid_spec=pltpu.PrefetchScalarGridSpec(
            num_scalar_prefetch=1,
            grid=(3,),
            in_specs=[
                pl.BlockSpec((None, rows, width), lambda i, m: (i, 0, 0)),
                whole((rows, width)),
                whole((4, width)),
                whole((width, width)),
                whole((8, width)),
            ],
            out_specs=[whole(shape) for shape in shapes],
            scratch_shapes=[
                pltpu.VMEM((width, rows), BF),
                pltpu.VMEM((8, width), F32),
                pltpu.VMEM((width, width), F32),
            ],
        ),
        compiler_params=params(40),
        cost_estimate=cost(6 * rows * width * width, 20 * rows * width),
        name="pack",
    )(me, grads, tokens, norms, output_grad, second)
    return outs[:2], outs[2:]


def project_back_kernel(
    grads_ref, tokens_ref, residual_grad_ref, weight_ref, norms_ref, out_ref
):
    width = tokens_ref.shape[1]
    gradient = None
    for number in range(3):
        columns = slice(number * width, (number + 1) * width)
        part = dot(grads_ref[number], weight_ref[:, columns], 1, 1)
        gradient = part if gradient is None else gradient + part
    normal, inverse = normalise(tokens_ref[...].astype(F32))
    input_part = norm_backward(normal, inverse, norms_ref[0:1, :], gradient)
    out_ref[...] = (residual_grad_ref[...] + input_part).astype(BF)


def project_back(grads, tokens, residual_grad, weight, norms):
    rows, width = tokens.shape
    block = 256
    part = pl.BlockSpec((block, width), lambda i: (i, 0))
    return pl.pallas_call(
        project_back_kernel,
        out_shape=jax.ShapeDtypeStruct((rows, width), BF),
        grid=(rows // block,),
        in_specs=[pl.BlockSpec((3, block, width), lambda i: (0, i, 0)), part, part]
        + [pl.BlockSpec(weight.shape, lambda i: (0, 0)), pl.BlockSpec((4, width), lambda i: (0, 0))],
        out_specs=part,
        compiler_params=params(24),
        cost_estimate=cost(1.8 * rows * width * width, 6 * rows * width),
        name="project_back",
    )(grads, tokens, residual_grad, weight, norms)


def add_kernel(left_ref, right_ref, out_ref):
    out_ref[...] = (left_ref[...].astype(F32) + right_ref[...].astype(F32)).astype(BF)


def add(left, right, pieces):
    (left, i), (right, j) = left, right
    _, rows, columns = left.shape
    half = pieces // 2
    spec = lambda first: pl.BlockSpec((half, rows, columns), lambda a: (first // half + a, 0, 0))
    size = pieces * rows * columns
    return pl.pallas_call(
        add_kernel,
        out_shape=jax.ShapeDtypeStruct((pieces, rows, columns), BF),
        grid=(2,),
        in_specs=[spec(i), spec(j)],
        out_specs=spec(0),
        compiler_params=params(10),
        cost_estimate=cost(0, 0),
        name="add",
    )(left, right)


def total_kernel(place_ref, middle_ref, end_ref, *refs, across):
    arrived, out_ref = refs[:-1], refs[-1]
    end = (place_ref[0] == 0) | (place_ref[0] == LINE - 1)
    rows, columns = middle_ref.shape[1:]
    for piece in range(middle_ref.shape[0]):
        total = jnp.where(end, end_ref[piece].astype(F32), middle_ref[piece].astype(F32))
        for ref in arrived:
            total = total + ref[piece].astype(F32)
        if across:
            out_ref[:, piece * columns : (piece + 1) * columns] = total
        else:
            out_ref[piece * rows : (piece + 1) * rows, :] = total


def line_total(place, middle, end, arrived, across):
    ins = [middle, end, *arrived]
    pieces, rows, columns = middle[0].shape
    shape = (rows, pieces * columns) if across else (pieces * rows, columns)
    half = pieces // 2
    block = (rows, half * columns) if across else (half * rows, columns)
    spec = lambda first: pl.BlockSpec((half, rows, columns), lambda a, p: (first // half + a, 0, 0))
    return pl.pallas_call(
        functools.partial(total_kernel, across=across),
        out_shape=jax.ShapeDtypeStruct(shape, F32),
        grid_spec=pltpu.PrefetchScalarGridSpec(
            num_scalar_prefetch=1,
            grid=(2,),
            in_specs=[spec(first) for _, first in ins],
            out_specs=pl.BlockSpec(block, lambda a, p: (0, a) if across else (a, 0)),
        ),
        compiler_params=params(60),
        cost_estimate=cost(0, 0),
        name="line_total",
    )(place, *[array for array, _ in ins])


class LineSum:
    def __init__(self, pairs, axis, place):
        self.axis, self.place = axis, place
        self.shares = lax.axis_size(axis)
        self.pairs = pairs
        self.line = self.shares == LINE and pairs[0][0][0] is pairs[0][1][0]
        self.got = {}

    def send(self, name, matrix=None):
        if not self.line:
            return
        ends = [(0, 1), (3, 2)]
        middles = [(1, 2), (2, 1)]
        out = [(2, 3), (1, 0)]

        def plus(number, before):
            if matrix is None:
                own = (self.pairs[number][0][0], 0)
                return add(own, (self.got[before], 0), own[0].shape[0])
            own = self.pairs[number][matrix]
            return add(own, (self.got[before], own[1]), self.pairs[MIDDLE][matrix][0].shape[0])

        values, route = {
            "far": lambda: (self.pairs[0][0][0], ends),
            "near": lambda: (self.pairs[1][0][0], ends),
            "own": lambda: (self.pairs[MIDDLE][matrix][0], ends),
            "far_on": lambda: (plus(0, "far"), middles),
            "near_on": lambda: (plus(1, "near"), middles),
            "far_out": lambda: (plus(3, "far_on"), out),
        }[name]()
        key = name if matrix is None else (name, matrix)
        self.got[key] = lax.ppermute(values, self.axis, route)

    def hold(self, name, values):
        if not self.line:
            return values
        self.got[name], values = lax.optimization_barrier((self.got[name], values))
        return values

    def totals(self):
        if self.line:
            sums = []
            for matrix in range(2):
                arrived = [(self.got[name, matrix], 0) for name in ("own", "near_on", "far_out")]
                ins = self.pairs[2][matrix], self.pairs[3][matrix]
                sums.append(line_total(self.place, *ins, arrived, across=matrix == 1))
            return sums
        sums = []
        for matrix in range(2):
            stacked = jnp.stack([pair[matrix][0] for pair in self.pairs])
            total = lax.psum_scatter(stacked, self.axis, scatter_dimension=0).astype(F32)
            pieces, rows, columns = total.shape
            if matrix:
                sums.append(total.swapaxes(0, 1).reshape(rows, pieces * columns))
            else:
                sums.append(total.reshape(pieces * rows, columns))
        return sums


def partner_pairs(axis, bit):
    return [(i, i ^ bit) for i in range(lax.axis_size(axis))]


def halves_kernel(me_ref, *refs, edges, bits):
    streams = len(bits)
    ins, outs = refs[: len(refs) - 2 * streams], refs[len(refs) - 2 * streams :]
    for stream, (first, last) in enumerate(edges):
        keep, got = ins[:2] if len(ins) == 2 else ins[2 * stream : 2 * stream + 2]
        kept, sent = outs[2 * stream : 2 * stream + 2]
        size = (last - first) // 2
        upper = (me_ref[0] // bits[stream]) % 2
        mine = pl.multiple_of(first + upper * size, 16)
        other = pl.multiple_of(first + (1 - upper) * size, 16)
        for at, out in ((mine, kept), (other, sent)):
            total = keep[:, pl.ds(at, size), :].astype(F32) + got[:, pl.ds(at, size), :].astype(F32)
            out[...] = total.astype(BF)


def halves(me, bits, edges, pairs, level):
    shares = pairs[0][0].shape[0]
    spec = lambda rows, columns: pl.BlockSpec((1, rows, columns), lambda z, m: (z, 0, 0))
    in_specs, out_specs, out_shape = [], [], []
    for keep, _ in pairs:
        in_specs += [spec(*keep.shape[1:])] * 2
    columns = pairs[0][0].shape[2]
    for first, last in edges:
        rows = (last - first) // 2
        out_specs += [spec(rows, columns)] * 2
        out_shape += [jax.ShapeDtypeStruct((shares, rows, columns), BF)] * 2
    size = sum(keep.size for keep, _ in pairs)
    outs = pl.pallas_call(
        functools.partial(halves_kernel, edges=edges, bits=bits),
        out_shape=out_shape,
        grid_spec=pltpu.PrefetchScalarGridSpec(
            num_scalar_prefetch=1, grid=(shares,), in_specs=in_specs, out_specs=out_specs
        ),
        compiler_params=params(20),
        cost_estimate=cost(0, 60 * size * level),
        name="halves",
    )(me, *[array for pair in pairs for array in pair])
    return [(outs[2 * i], outs[2 * i + 1]) for i in range(len(bits))]


def join_kernel(*refs):
    ins, out_ref = refs[:-1], refs[-1]
    first = 0
    for keep, got in zip(ins[::2], ins[1::2]):
        last = first + keep.shape[1]
        total = keep[...].astype(F32) + got[...].astype(F32)
        out_ref[:, first:last, :] = total.astype(BF)
        first = last


def join(pairs):
    shares, _, columns = pairs[0][0].shape
    rows = sum(keep.shape[1] for keep, _ in pairs)
    size = shares * rows * columns
    return pl.pallas_call(
        join_kernel,
        out_shape=jax.ShapeDtypeStruct((shares, rows, columns), BF),
        compiler_params=params(12),
        cost_estimate=cost(0, 0),
        name="join",
    )(*[array for pair in pairs for array in pair])


def spread_kernel(parts_ref, out_ref):
    total = jnp.sum(parts_ref[...].astype(F32), axis=0).astype(BF)
    for number in range(out_ref.shape[0]):
        out_ref[number] = total


def spread(parts, devices):
    _, rows, columns = parts.shape
    size = parts.size + devices * rows * columns
    return pl.pallas_call(
        spread_kernel,
        out_shape=jax.ShapeDtypeStruct((devices, rows, columns), BF),
        compiler_params=params(12),
        cost_estimate=cost(0, 0),
        name="spread",
    )(parts)


def assemble_kernel(
    place_ref,
    gathered_ref,
    weight_ref,
    norms_ref,
    input_ref,
    output_ref,
    column_ref,
    tail_ref,
    summed,
    *,
    sources,
):
    half = gathered_ref.shape[2]
    share, width = output_ref.shape
    for device, first, count, to, side in sources:
        values = gathered_ref[device, first : first + count, :].astype(F32)
        summed[to : to + count, side * half : (side + 1) * half] = values
    shift_sum = gain_sum = 0.0
    for third in range(3):
        columns = slice(third * width, (third + 1) * width)
        values = summed[third * share : (third + 1) * share, :]
        input_ref[:, columns] = values
        weight = weight_ref[:, columns].astype(F32)
        line = summed[4 * share + third : 4 * share + third + 1, :]
        shift_sum = shift_sum + jnp.sum(weight * line, axis=1, keepdims=True)
        gain_sum = gain_sum + jnp.sum(weight * values, axis=1, keepdims=True)
    output_ref[...] = summed[3 * share : 4 * share, :]
    lane = lax.broadcasted_iota(jnp.int32, (1, 128), 1)
    column_ref[...] = jnp.where(lane == 0, gain_sum, shift_sum)
    tail_ref[...] = summed[4 * share : 4 * share + 8, :]


def assemble(place, gathered, weight, norms, share, orders, streams):
    devices, _, half = gathered.shape
    width = 2 * half
    levels = len(orders[0])
    sources = []
    for side in range(2):
        first, to = 0, 0
        for count, order in zip(streams, orders):
            for number in range(2**levels):
                digits = [(number >> (levels - 1 - level)) & 1 for level in range(levels)]
                device = side + sum(digit * bit for digit, bit in zip(digits, order))
                sources.append((device, first, count, to, side))
                to += count
            first += count
    total = sum(streams) * 2**levels
    whole = lambda shape: pl.BlockSpec(shape, lambda i, p: (0,) * len(shape))
    return pl.pallas_call(
        functools.partial(assemble_kernel, sources=sources),
        out_shape=[
            jax.ShapeDtypeStruct((share, 3 * width), F32),
            jax.ShapeDtypeStruct((share, width), F32),
            jax.ShapeDtypeStruct((share, 128), F32),
            jax.ShapeDtypeStruct((8, width), F32),
        ],
        grid_spec=pltpu.PrefetchScalarGridSpec(
            num_scalar_prefetch=1,
            grid=(1,),
            in_specs=[
                whole(gathered.shape),
                pl.BlockSpec((share, 3 * width), lambda i, p: (p[0], 0)),
                whole(norms.shape),
            ],
            out_specs=[
                whole((share, 3 * width)),
                whole((share, width)),
                whole((share, 128)),
                whole((8, width)),
            ],
            scratch_shapes=[pltpu.VMEM((total, width), F32)],
        ),
        compiler_params=params(24),
        cost_estimate=cost(0, 0),
        name="assemble",
    )(place, gathered, weight, norms)


def on_device(
    tokens,
    lengths,
    expert_index,
    centroids,
    input_weight,
    output_weight,
    first_gain,
    first_shift,
    second_gain,
    second_shift,
    up_weight,
    down_weight,
    cotangent,
):
    rows, width = tokens.shape
    experts = centroids.shape[0]
    capacity = rows // experts
    shares = lax.axis_size("dp")
    share = width // shares
    me = lax.axis_index("expert").reshape(1).astype(jnp.int32)
    place = lax.axis_index("dp").reshape(1).astype(jnp.int32)
    norms = jnp.stack([first_gain, first_shift, second_gain, second_shift])

    def exchange(values, axis="expert"):
        return lax.all_to_all(values, axis, split_axis=0, concat_axis=0, tiled=True)

    def dispatch(values):
        return exchange(values.reshape(experts, capacity, -1)).reshape(rows, -1)

    outgoing_cotangent, target_row, target_column = route(
        lengths, expert_index, cotangent, experts
    )
    arrived_cotangent = dispatch(outgoing_cotangent)
    held_tokens, target_row = lax.optimization_barrier((tokens, target_row))
    projected = project(held_tokens, input_weight, norms)
    mixed, total = attend(lengths, projected)
    mixed, arrived_cotangent = lax.optimization_barrier((mixed, arrived_cotangent))
    residual, gate, outgoing = hidden_rows(
        lengths, mixed, tokens, output_weight, norms, centroids, target_row, target_column
    )
    arrived = dispatch(outgoing)
    order = place if shares == LINE else jnp.full_like(place, shares)
    produced, back, pairs = expert(
        me, order, arrived, arrived_cotangent, centroids, up_weight[0], down_weight[0], shares
    )
    line = LineSum(pairs, "dp", place)
    line.send("far")
    line.send("near")
    produced, returned = lax.optimization_barrier((produced, dispatch(back)))
    residual_grad, mixed_grad, output_grad, second_gains = combine(
        lengths, returned, target_column, cotangent, residual, norms, mixed, output_weight
    )
    produced, mixed_grad = lax.optimization_barrier((produced, mixed_grad))
    returned = dispatch(produced)
    mixed_grad = line.hold("far", mixed_grad)
    line.send("far_on")
    grads = attend_back(lengths, projected, mixed, total, mixed_grad)
    grads, returned = lax.optimization_barrier((grads, returned))
    keeps, sends = pack(
        me, grads, tokens, norms, output_grad, second_gains, shares, experts
    )
    swap = lambda values, bit: lax.ppermute(values, "expert", partner_pairs("expert", bit))
    pairs = [(keep, swap(send, 1)) for keep, send in zip(keeps, sends)]
    bits = [2**i for i in range(1, (experts - 1).bit_length())]
    orders = [bits, bits[::-1]]
    for level, now in enumerate(zip(*orders)):
        made = halves(me, now, [(0, keep.shape[1]) for keep, _ in pairs], pairs, level)
        pairs = [(kept, swap(sent, bit)) for (kept, sent), bit in zip(made, now)]
        if level == 0:
            kept, got = pairs[0]
            kept = line.hold("near", kept)
            line.send("own", 0)
            line.send("near_on", 0)
            kept = line.hold("far_on", kept)
            line.send("far_out", 0)
            pairs[0] = (kept, got)
    if OWN_EARLY:
        grads = line.hold(("own", 0), grads)
    input_gradient = project_back(grads, tokens, residual_grad, input_weight, norms)
    input_gradient, pairs = lax.optimization_barrier((input_gradient, pairs))
    for name in ("far_out", "near_on") if OWN_EARLY else ("far_out", "near_on", "own"):
        pairs = line.hold((name, 0), pairs)
    streams = [keep.shape[1] for keep, _ in pairs]
    joined = join(pairs)
    joined, returned = lax.optimization_barrier((joined, returned))
    over_line = exchange(joined, "dp")
    layer_output = layer(lengths, returned, target_column, residual, gate)
    for name in ("far_out", "near_on", "own"):
        line.send(name, 1)
    gathered = exchange(spread(over_line, experts))
    input_share, output_share, sums, tail = assemble(
        place, gathered, input_weight, norms, share, orders, streams
    )
    for name in ("far_out", "near_on", "own"):
        sums = line.hold((name, 1), sums)
    begin = lax.axis_index("dp") * share
    mine = lambda vector: lax.dynamic_slice_in_dim(vector, begin, share, vector.ndim - 1)
    shift_sum = sums[:, 1]
    gain_sum = (sums[:, 0] - mine(first_shift) * shift_sum) / mine(first_gain)
    second = mine(tail[3:5])
    down_share, up_share = line.totals()
    return (
        layer_output,
        input_gradient,
        input_share,
        output_share,
        gain_sum,
        shift_sum,
        second[0],
        second[1],
        up_share[None],
        down_share[None],
    )


def solution(mesh):
    both = P(("dp", "expert"))
    rows = P(("dp", "expert"), None)
    weights = P("expert", None, None)
    return jax.shard_map(
        on_device,
        mesh=mesh,
        in_specs=(rows, both, both, P(), P(), P(), P(), P(), P(), P(), weights, weights, rows),
        out_specs=(
            rows,
            rows,
            P("dp", None),
            P("dp", None),
            P("dp"),
            P("dp"),
            P("dp"),
            P("dp"),
            P("expert", "dp", None),
            P("expert", "dp", None),
        ),
        check_vma=False,
    )
```

```python
import functools

import jax
import jax.numpy as jnp
from jax import lax
from jax.experimental import pallas as pl
from jax.experimental.pallas import tpu as pltpu
from jax.sharding import PartitionSpec as P

HEADS = 12
EPS = 1e-05
EXCLUDED = -1e30
BF = jnp.bfloat16
F32 = jnp.float32
QUERY_ROWS = 256
SEEN = 1
EXPERT_MIB = 54
HIDDEN_MIB = 60


def dot(left, right, left_axis=1, right_axis=0):
    return lax.dot_general(
        left,
        right,
        (((left_axis,), (right_axis,)), ((), ())),
        preferred_element_type=F32,
    )


def params(limit=60):
    return pltpu.CompilerParams(vmem_limit_bytes=limit << 20)


def cost(flops, bytes_accessed, transcendentals=0):
    return pl.CostEstimate(
        flops=int(flops * SEEN),
        bytes_accessed=int(bytes_accessed * SEEN),
        transcendentals=int(transcendentals * SEEN),
    )


def split_three(values):
    high = values.astype(BF)
    rest = values - high.astype(F32)
    middle = rest.astype(BF)
    return high, middle, (rest - middle.astype(F32)).astype(BF)


def normalise(values):
    average = jnp.mean(values, axis=-1, keepdims=True)
    centred = values - average
    variance = jnp.mean(centred * centred, axis=-1, keepdims=True)
    inverse = lax.rsqrt(variance + EPS)
    return centred * inverse, inverse


def norm_backward(normal, inverse, gain, gradient):
    scaled = gain * gradient
    first = jnp.mean(scaled, axis=-1, keepdims=True)
    second = jnp.mean(scaled * normal, axis=-1, keepdims=True)
    return (scaled - first - normal * second) * inverse


def selection(target, first, count):
    rows = lax.broadcasted_iota(jnp.int32, (count, target.shape[1]), 0) + first
    return jnp.where(rows == target, 1.0, 0.0).astype(BF)


def route_kernel(length_ref, expert_ref, cotangent_ref, out_ref, row_ref, column_ref, *, experts):
    step = pl.program_id(0)
    rows = cotangent_ref.shape[0]
    block = out_ref.shape[0]

    @pl.when(step == 0)
    def _():
        length = length_ref[0]
        position = lax.broadcasted_iota(jnp.int32, (1, rows), 1)
        named = jnp.where(position < length, expert_ref[...], -1)
        number = lax.broadcasted_iota(jnp.int32, (experts, rows), 0)
        onehot = jnp.where(number == named, 1.0, 0.0)
        before = lax.broadcasted_iota(jnp.int32, (rows, rows), 0)
        after = lax.broadcasted_iota(jnp.int32, (rows, rows), 1)
        earlier = jnp.where(before < after, 1.0, 0.0).astype(BF)
        counts = dot(onehot.astype(BF), earlier)
        slot = jnp.sum(onehot * counts, axis=0, keepdims=True).astype(jnp.int32)
        target = jnp.where(named >= 0, named * (rows // experts) + slot, -1)
        row_ref[...] = jnp.broadcast_to(target, row_ref.shape)
        wide = jnp.broadcast_to(target.astype(F32), (128, rows))
        column_ref[...] = wide.T.astype(jnp.int32)

    chosen = selection(row_ref[0:1, :], step * block, block)
    out_ref[...] = dot(chosen, cotangent_ref[...]).astype(BF)


def route(length, expert_index, cotangent, experts):
    rows, width = cotangent.shape
    block = 256
    return pl.pallas_call(
        functools.partial(route_kernel, experts=experts),
        out_shape=[
            jax.ShapeDtypeStruct((rows, width), BF),
            jax.ShapeDtypeStruct((8, rows), jnp.int32),
            jax.ShapeDtypeStruct((rows, 128), jnp.int32),
        ],
        grid_spec=pltpu.PrefetchScalarGridSpec(
            num_scalar_prefetch=1,
            grid=(rows // block,),
            in_specs=[
                pl.BlockSpec((1, rows), lambda i, l: (0, 0)),
                pl.BlockSpec((rows, width), lambda i, l: (0, 0)),
            ],
            out_specs=[
                pl.BlockSpec((block, width), lambda i, l: (i, 0)),
                pl.BlockSpec((8, rows), lambda i, l: (0, 0)),
                pl.BlockSpec((rows, 128), lambda i, l: (0, 0)),
            ],
        ),
        compiler_params=params(60),
        cost_estimate=cost(2 * rows * rows * width, 4 * rows * width),
        name="route",
    )(length, expert_index.reshape(1, rows), cotangent)


def project_kernel(tokens_ref, weight_ref, norms_ref, out_ref):
    normal, _ = normalise(tokens_ref[...].astype(F32))
    normed = (normal * norms_ref[0:1, :] + norms_ref[1:2, :]).astype(BF)
    out_ref[...] = dot(normed, weight_ref[...]).astype(BF)


def project(tokens, weight, norms):
    rows, width = tokens.shape
    columns = weight.shape[1]
    block = 256
    return pl.pallas_call(
        project_kernel,
        out_shape=jax.ShapeDtypeStruct((rows, columns), BF),
        grid=(rows // block,),
        in_specs=[
            pl.BlockSpec((block, width), lambda i: (i, 0)),
            pl.BlockSpec((width, columns), lambda i: (0, 0)),
            pl.BlockSpec((4, width), lambda i: (0, 0)),
        ],
        out_specs=pl.BlockSpec((block, columns), lambda i: (i, 0)),
        compiler_params=params(24),
        cost_estimate=cost(2 * rows * width * columns, 2 * (rows + width) * columns),
        name="project",
    )(tokens, weight, norms)


def staggered(items, begin, finish, ahead=1):
    waiting = []
    for item in items:
        waiting.append((item, begin(item)))
        if len(waiting) > ahead:
            finish(*waiting.pop(0))
    for item, values in waiting:
        finish(item, values)


def length_bias(rows, length):
    row = lax.broadcasted_iota(jnp.int32, (rows, 1), 0)
    return jnp.where(row < length, 0.0, EXCLUDED).astype(BF)


def attend_kernel(length_ref, query_ref, key_ref, value_ref, mixed_ref, total_ref, *, scale, half):
    rows = query_ref.shape[0]
    lane = lax.broadcasted_iota(jnp.int32, (1, 2 * half), 1)
    zero, one = jnp.zeros((), BF), jnp.ones((), BF)
    bias = length_bias(rows, length_ref[0])
    done = {}
    place = lax.broadcasted_iota(jnp.int32, (1, 128), 1)
    first = 2 * pl.program_id(0)
    keys = [jnp.where(lane == half * (1 - head), bias, key_ref[...]) for head in range(2)]

    def scores_of(item):
        start, head = item
        end = start + QUERY_ROWS
        row = lax.broadcasted_iota(jnp.int32, (QUERY_ROWS, QUERY_ROWS), 0)
        column = lax.broadcasted_iota(jnp.int32, (QUERY_ROWS, QUERY_ROWS), 1)
        scaled = query_ref[start:end, :] * jnp.asarray(scale, BF)
        rest = jnp.where(lane == half * (1 - head), one, zero)
        scores = dot(jnp.where((lane // half) == head, scaled, rest), keys[head][:end], 1, 1)
        last = jnp.where(column <= row, scores[:, start:], EXCLUDED)
        return jnp.concatenate([scores[:, :start], last], axis=1) if start else last

    def mix(item, scores):
        start, head = item
        end = start + QUERY_ROWS
        other = half * (1 - head)
        ones = jnp.where(lane == other, one, zero)
        value = jnp.where((lane // half) == head, value_ref[:end, :], ones)
        top = jnp.max(scores, axis=1, keepdims=True)
        out = dot(jnp.exp(scores - top).astype(BF), value)
        total = out[:, other : other + 1]
        done[item] = (out / total, top + jnp.log(total))
        if head == 1:
            low, high = done[start, 0], done[start, 1]
            mixed_ref[start:end, :] = jnp.where(lane < half, low[0], high[0]).astype(BF)
            other = jnp.where(place == first + 1, high[1], total_ref[start:end, :])
            total_ref[start:end, :] = jnp.where(place == first, low[1], other)

    starts = range(0, rows, QUERY_ROWS)
    staggered([(start, head) for start in starts for head in range(2)], scores_of, mix, 2)


def pair_specs(rows, wide, pairs, thirds):
    return [pl.BlockSpec((rows, wide), lambda i, l, o=o: (0, i + o * pairs)) for o in range(thirds)]


def attend(length, projected):
    rows, width = projected.shape[0], projected.shape[1] // 3
    size = width // HEADS
    pairs = HEADS // 2
    one = pl.BlockSpec((rows, 2 * size), lambda i, l: (0, i))
    return pl.pallas_call(
        functools.partial(attend_kernel, scale=size**-0.5, half=size),
        out_shape=[
            jax.ShapeDtypeStruct((rows, width), BF),
            jax.ShapeDtypeStruct((rows, 128), F32),
        ],
        grid_spec=pltpu.PrefetchScalarGridSpec(
            num_scalar_prefetch=1,
            grid=(pairs,),
            in_specs=pair_specs(rows, 2 * size, pairs, 3),
            out_specs=[one, pl.BlockSpec((rows, 128), lambda i, l: (0, 0))],
        ),
        compiler_params=params(16),
        cost_estimate=cost(
            16 * rows * rows * width, 12 * rows * width, HEADS * rows * rows // 2
        ),
        name="attend",
    )(length, projected, projected, projected)


def attend_back_kernel(
    length_ref,
    query_ref,
    key_ref,
    value_ref,
    mixed_ref,
    total_ref,
    incoming_ref,
    out_ref,
    key_sum,
    value_sum,
    *,
    scale,
    half,
):
    lane = lax.broadcasted_iota(jnp.int32, (1, 2 * half), 1)
    bias = length_bias(query_ref.shape[0], length_ref[0])
    zero, one = jnp.zeros((), BF), jnp.ones((), BF)
    key_sum[...] = jnp.zeros_like(key_sum)
    value_sum[...] = jnp.zeros_like(value_sum)
    parts = {}

    def products(item):
        start, head = item
        end = start + QUERY_ROWS
        mine = (lane // half) == head
        other = half * (1 - head)
        ones = jnp.where((lane >= other) & (lane < other + 3), one, zero)

        def extend(base, column, spare):
            a, b, c = split_three(-column)
            rest = jnp.where(lane == other + 2, c, jnp.where(lane == other + 3, spare, zero))
            rest = jnp.where(lane == other + 1, b, rest)
            return jnp.where(mine, base, jnp.where(lane == other, a, rest))

        row = lax.broadcasted_iota(jnp.int32, (QUERY_ROWS, QUERY_ROWS), 0)
        column = lax.broadcasted_iota(jnp.int32, (QUERY_ROWS, QUERY_ROWS), 1)
        incoming = incoming_ref[start:end, :]
        product = incoming.astype(F32) * mixed_ref[start:end, :].astype(F32)
        query = jnp.where(mine, query_ref[start:end, :] * jnp.asarray(scale, BF), zero)
        grad = jnp.where(mine, incoming, zero)
        inner = jnp.sum(jnp.where(mine, product, 0.0), axis=1, keepdims=True)
        number = 2 * pl.program_id(0) + head
        at = lax.broadcasted_iota(jnp.int32, (1, 128), 1) == number
        total = jnp.sum(jnp.where(at, total_ref[start:end, :], 0.0), axis=1, keepdims=True)
        spare = jnp.where(lane == other + 3, bias[:end], ones)
        key = jnp.where(mine, key_ref[:end, :], spare)
        scores = dot(key, extend(query, total, one), 1, 1)
        last = jnp.where(row <= column, scores[start:, :], EXCLUDED)
        scores = jnp.concatenate([scores[:start, :], last], axis=0) if start else last
        value = jnp.where(mine, value_ref[:end, :], ones)
        return scores, dot(value, extend(grad, inner, zero), 1, 1), query, grad

    def gradients(item, values):
        start, head = item
        scores, centred, query, grad = values
        end = start + QUERY_ROWS
        probs = jnp.exp(scores)
        score_gradient = (probs * centred).astype(BF)
        value_sum[:end, :] += dot(probs.astype(BF), grad)
        key_sum[:end, :] += dot(score_gradient, query)
        key = jnp.where((lane // half) == head, key_ref[:end, :], zero)
        parts[item] = dot(score_gradient, key, 0, 0)
        if head == 1:
            total = parts[start, 0] + parts[start, 1]
            out_ref[0, start:end, :] = (total * scale).astype(BF)

    starts = range(0, query_ref.shape[0], QUERY_ROWS)
    staggered([(start, head) for start in starts for head in range(2)], products, gradients)
    out_ref[1] = key_sum[...].astype(BF)
    out_ref[2] = value_sum[...].astype(BF)


def attend_back(length, projected, mixed, total, incoming):
    rows, width = projected.shape[0], projected.shape[1] // 3
    size = width // HEADS
    pairs = HEADS // 2
    one = pl.BlockSpec((rows, 2 * size), lambda i, l: (0, i))
    return pl.pallas_call(
        functools.partial(attend_back_kernel, scale=size**-0.5, half=size),
        out_shape=jax.ShapeDtypeStruct((3, rows, width), BF),
        grid_spec=pltpu.PrefetchScalarGridSpec(
            num_scalar_prefetch=1,
            grid=(pairs,),
            in_specs=pair_specs(rows, 2 * size, pairs, 3)
            + [one, pl.BlockSpec((rows, 128), lambda i, l: (0, 0)), one],
            out_specs=pl.BlockSpec((3, rows, 2 * size), lambda i, l: (0, 0, i)),
            scratch_shapes=[pltpu.VMEM((rows, 2 * size), F32)] * 2,
        ),
        compiler_params=params(60),
        cost_estimate=cost(
            30 * rows * rows * width, 20 * rows * width
        ),
        name="attend_back",
    )(length, projected, projected, projected, mixed, total, incoming)


def picked_rows(target, centroids_ref, capacity):
    experts, width = centroids_ref.shape
    pieces = [piece.astype(F32) for piece in split_three(centroids_ref[...])]
    rest = jnp.zeros((128 - 3 * experts, width), F32)
    table = jnp.concatenate(pieces + [rest], axis=0).astype(BF)
    lane = lax.broadcasted_iota(jnp.int32, (1, 128), 1)
    low = jnp.where(lane < 3 * experts, (lane % experts) * capacity, 1 << 20)
    onehot = jnp.where((target >= low) & (target < low + capacity), 1.0, 0.0).astype(BF)
    return dot(onehot, table)


def present_rows(block_index, count, length):
    row = lax.broadcasted_iota(jnp.int32, (count, 1), 0) + block_index * count
    return jnp.where(row < length, 1.0, 0.0)


def hidden_kernel(
    length_ref,
    mixed_ref,
    tokens_ref,
    weight_ref,
    norms_ref,
    centroids_ref,
    row_ref,
    column_ref,
    residual_ref,
    gate_ref,
    out_ref,
    hidden_low,
):
    rows = row_ref.shape[1]
    count = 256

    def branch_of(number):
        return dot(mixed_ref[number * count : (number + 1) * count, :], weight_ref[...])

    def finish(number, branch):
        at = slice(number * count, (number + 1) * count)
        mask = present_rows(number, count, length_ref[0])
        residual = tokens_ref[at, :].astype(F32) + mask * branch
        residual_ref[at, :] = residual
        normal, _ = normalise(residual)
        hidden = normal * norms_ref[2:3, :] + norms_ref[3:4, :]
        picked = picked_rows(column_ref[at, :], centroids_ref, rows // centroids_ref.shape[0])
        gate = jax.nn.sigmoid(jnp.sum(hidden * picked, axis=-1, keepdims=True))
        gate_ref[at, :] = jnp.broadcast_to(gate, (count, 128))
        hidden_low[at, :] = hidden.astype(BF)

    staggered(range(rows // count), branch_of, finish)
    for first in range(0, rows, count):
        chosen = selection(row_ref[0:1, :], first, count)
        out_ref[first : first + count, :] = dot(chosen, hidden_low[...]).astype(BF)


def hidden_rows(length, mixed, tokens, weight, norms, centroids, target_row, target_column):
    rows, width = tokens.shape
    experts = centroids.shape[0]
    whole = lambda *shape: pl.BlockSpec(shape, lambda i, l: (0,) * len(shape))
    return pl.pallas_call(
        hidden_kernel,
        out_shape=[
            jax.ShapeDtypeStruct((rows, width), F32),
            jax.ShapeDtypeStruct((rows, 128), F32),
            jax.ShapeDtypeStruct((rows, width), BF),
        ],
        grid_spec=pltpu.PrefetchScalarGridSpec(
            num_scalar_prefetch=1,
            grid=(1,),
            in_specs=[
                whole(rows, width),
                whole(rows, width),
                whole(width, width),
                whole(4, width),
                whole(experts, width),
                whole(8, rows),
                whole(rows, 128),
            ],
            out_specs=[whole(rows, width), whole(rows, 128), whole(rows, width)],
            scratch_shapes=[pltpu.VMEM((rows, width), BF)],
        ),
        compiler_params=params(HIDDEN_MIB),
        cost_estimate=cost(2 * rows * (rows + width) * width, 12 * rows * width),
        name="hidden_rows",
    )(length, mixed, tokens, weight, norms, centroids, target_row, target_column)


LINE = 4
MIDDLE = 2


def far_first(number, place, shares):
    return jnp.where(place < shares // 2, shares - 1 - number, number)


def expert_kernel(
    me_ref,
    place_ref,
    rows_ref,
    cotangent_ref,
    centroids_ref,
    up_ref,
    down_ref,
    produced_ref,
    back_ref,
    *refs,
    shares,
    together,
):
    outs, scratch = refs[:-8], refs[-8:]
    produced_sum, back_sum, transposed, gradient, gates, downs, ups, sems = scratch
    step = pl.program_id(0)
    count, width = rows_ref.shape
    share = width // shares

    @pl.when(step == 0)
    def _():
        hidden = rows_ref[...].astype(F32)
        centroid = centroids_ref[pl.ds(me_ref[0], 1), :]
        gate = jax.nn.sigmoid(jnp.sum(hidden * centroid, axis=-1, keepdims=True))
        gradient[...] = (gate * cotangent_ref[...].astype(F32)).astype(BF)
        gates[...] = jnp.broadcast_to(gate, gates.shape)
        produced_sum[...] = jnp.zeros_like(produced_sum)
        back_sum[...] = jnp.zeros_like(back_sum)
        values = rows_ref[...].T
        for number in range(shares):
            to = pl.multiple_of(far_first(number, place_ref[0], shares) * share, 16)
            transposed[pl.ds(to, share), :] = values[number * share : (number + 1) * share]

    upper = dot(rows_ref[...], up_ref[...])
    part = 0.5 + 0.5 * lax.erf(upper * (0.5**0.5))
    density = jnp.exp(upper * upper * -0.5) * 0.3989422804014327
    active = (upper * part).astype(BF)
    slope = part + upper * density
    active_gradient = dot(gradient[...], down_ref[...], 1, 1)
    upper_gradient = (active_gradient * slope).astype(BF)
    produced_sum[...] += dot(active, down_ref[...])
    down = dot(active, gradient[...], 0, 0).astype(BF)
    back_sum[...] += dot(upper_gradient, up_ref[...], 1, 1)
    up = dot(transposed[...], upper_gradient).astype(BF)
    real = far_first(step, place_ref[0], shares)
    slot = lax.rem(step, 2)
    pieces = down.shape[0] // share
    places = out_places(shares, pieces, together)

    def down_copy(number, slot):
        target = outs[places[number][0][0]].at[pl.ds(0, pieces)]
        return pltpu.make_async_copy(downs.at[slot], target, sems.at[slot, shares])

    def up_copy(number, slot, piece):
        array, first = places[number][1]
        target = outs[array].at[first + piece]
        return pltpu.make_async_copy(ups.at[slot, number], target, sems.at[slot, number])

    def wait(slot):
        down_copy(0, slot).wait()
        for number in range(shares):
            up_copy(number, slot, 0).wait()

    @pl.when(step >= 2)
    def _():
        wait(slot)

    for piece in range(pieces):
        downs[slot, piece] = down[piece * share : (piece + 1) * share]
    for number in range(shares):
        ups[slot, number] = up[number * share : (number + 1) * share]
        up_copy(number, slot, real).start()

        @pl.when(step == number)
        def _(number=number):
            down_copy(number, slot).start()

    @pl.when(step == pl.num_programs(0) - 1)
    def _():
        centroid = centroids_ref[pl.ds(me_ref[0], 1), :]

        @pl.loop(0, count // 256)
        def _(number):
            at = pl.ds(pl.multiple_of(number * 256, 256), 256)
            produced = produced_sum[at, :].astype(BF)
            produced_ref[at, :] = produced
            gate = gates[at, 0:1]
            cotangent = cotangent_ref[at, :].astype(F32)
            along = jnp.sum(cotangent * produced.astype(F32), axis=-1, keepdims=True)
            logit_gradient = along * gate * (1.0 - gate)
            back_ref[at, :] = (back_sum[at, :] + logit_gradient * centroid).astype(BF)
        wait(1 - slot)
        wait(slot)


def out_places(shares, pieces, together):
    places, count = [], 0
    for number in range(shares):
        if together and number != MIDDLE:
            places.append(((count, 0), (count, pieces)))
            count += 1
        else:
            places.append(((count, 0), (count + 1, 0)))
            count += 2
    return places


def expert(me, place, hidden, cotangent, centroids, up, down, shares):
    count, width = hidden.shape
    inner = up.shape[1]
    chunk, share = inner // shares, width // shares
    together = shares == LINE and chunk == width
    still = lambda c, m, p: (0, 0)
    once = pl.Buffered(1)
    whole = pl.BlockSpec((count, width), still, pipeline_mode=once)
    real = lambda c, p: far_first(c, p[0], shares)
    pieces = chunk // share
    places = out_places(shares, pieces, together)
    shapes = []
    for number in range(shares):
        if together and number != MIDDLE:
            shapes.append((pieces + shares, share, width))
        else:
            shapes += [(pieces, share, width), (shares, share, chunk)]
    outs = pl.pallas_call(
        functools.partial(expert_kernel, shares=shares, together=together),
        out_shape=[jax.ShapeDtypeStruct((count, width), BF)] * 2
        + [jax.ShapeDtypeStruct(shape, BF) for shape in shapes],
        grid_spec=pltpu.PrefetchScalarGridSpec(
            num_scalar_prefetch=2,
            grid=(shares,),
            in_specs=[
                whole,
                whole,
                pl.BlockSpec(centroids.shape, still, pipeline_mode=once),
                pl.BlockSpec((width, chunk), lambda c, m, p: (0, real(c, p))),
                pl.BlockSpec((chunk, width), lambda c, m, p: (real(c, p), 0)),
            ],
            out_specs=[whole, whole] + [pl.BlockSpec(memory_space=pl.ANY)] * len(shapes),
            scratch_shapes=[
                pltpu.VMEM((count, width), F32),
                pltpu.VMEM((count, width), F32),
                pltpu.VMEM((width, count), BF),
                pltpu.VMEM((count, width), BF),
                pltpu.VMEM((count, 128), F32),
                pltpu.VMEM((2, pieces, share, width), BF),
                pltpu.VMEM((2, shares, share, chunk), BF),
                pltpu.SemaphoreType.DMA((2, shares + 1)),
            ],
        ),
        compiler_params=params(EXPERT_MIB),
        cost_estimate=cost(12 * count * width * inner, 8 * inner * width, 2 * count * inner),
        name="expert",
    )(me, place, hidden, cotangent, centroids, up, down)
    arrays = outs[2:]
    pairs = [[(arrays[number], first) for number, first in pair] for pair in places]
    return outs[0], outs[1], pairs


def combine_kernel(
    length_ref,
    returned_ref,
    column_ref,
    cotangent_ref,
    residual_ref,
    norms_ref,
    mixed_ref,
    weight_ref,
    residual_grad_ref,
    mixed_grad_ref,
    weight_grad_ref,
    gains_ref,
    weight_sum,
):
    step = pl.program_id(0)
    count = cotangent_ref.shape[0]

    @pl.when(step == 0)
    def _():
        weight_sum[...] = jnp.zeros_like(weight_sum)
        gains_ref[...] = jnp.zeros_like(gains_ref)

    hidden_gradient = gathered_rows(column_ref, returned_ref)
    mask = present_rows(step, count, length_ref[0])
    normal, inverse = normalise(residual_ref[...])
    gains_ref[0:1, :] += jnp.sum(hidden_gradient * normal, axis=0, keepdims=True)
    gains_ref[1:2, :] += jnp.sum(hidden_gradient, axis=0, keepdims=True)
    residual_gradient = cotangent_ref[...].astype(F32) + norm_backward(
        normal, inverse, norms_ref[2:3, :], hidden_gradient
    )
    residual_grad_ref[...] = residual_gradient
    branch_gradient = (mask * residual_gradient).astype(BF)
    mixed_grad_ref[...] = dot(branch_gradient, weight_ref[...], 1, 1).astype(BF)
    weight_sum[...] += dot(mixed_ref[...], branch_gradient, 0, 0)

    @pl.when(step == pl.num_programs(0) - 1)
    def _():
        weight_grad_ref[...] = weight_sum[...].astype(BF)


def gathered_rows(column_ref, slots_ref):
    place = lax.broadcasted_iota(jnp.int32, (column_ref.shape[0], slots_ref.shape[0]), 1)
    chosen = jnp.where(place == column_ref[:, 0:1], 1.0, 0.0).astype(BF)
    return dot(chosen, slots_ref[...])


def combine(length, returned, target_column, cotangent, residual, norms, mixed, weight):
    rows, width = cotangent.shape
    block = 256
    part = pl.BlockSpec((block, width), lambda i, l: (i, 0))
    thin = pl.BlockSpec((block, 128), lambda i, l: (i, 0))
    still = lambda i, l: (0, 0)
    return pl.pallas_call(
        combine_kernel,
        out_shape=[
            jax.ShapeDtypeStruct((rows, width), F32),
            jax.ShapeDtypeStruct((rows, width), BF),
            jax.ShapeDtypeStruct((width, width), BF),
            jax.ShapeDtypeStruct((8, width), F32),
        ],
        grid_spec=pltpu.PrefetchScalarGridSpec(
            num_scalar_prefetch=1,
            grid=(rows // block,),
            in_specs=[
                pl.BlockSpec((rows, width), still),
                thin,
                part,
                part,
                pl.BlockSpec((4, width), still),
                part,
                pl.BlockSpec((width, width), still),
            ],
            out_specs=[
                part,
                part,
                pl.BlockSpec((width, width), still),
                pl.BlockSpec((8, width), still),
            ],
            scratch_shapes=[pltpu.VMEM((width, width), F32)],
        ),
        compiler_params=params(60),
        cost_estimate=cost(4 * rows * (rows + width) * width, 24 * rows * width),
        name="combine",
    )(length, returned, target_column, cotangent, residual, norms, mixed, weight)


def layer_kernel(length_ref, returned_ref, column_ref, residual_ref, gate_ref, out_ref):
    term = gathered_rows(column_ref, returned_ref)
    mask = present_rows(pl.program_id(0), column_ref.shape[0], length_ref[0])
    out_ref[...] = (residual_ref[...] + mask * gate_ref[:, 0:1] * term).astype(BF)


def layer(length, returned, target_column, residual, gate):
    rows, width = residual.shape
    block = 256
    part = pl.BlockSpec((block, width), lambda i, l: (i, 0))
    thin = pl.BlockSpec((block, 128), lambda i, l: (i, 0))
    return pl.pallas_call(
        layer_kernel,
        out_shape=jax.ShapeDtypeStruct((rows, width), BF),
        grid_spec=pltpu.PrefetchScalarGridSpec(
            num_scalar_prefetch=1,
            grid=(rows // block,),
            in_specs=[pl.BlockSpec((rows, width), lambda i, l: (0, 0)), thin, part, thin],
            out_specs=part,
        ),
        compiler_params=params(60),
        cost_estimate=cost(2 * rows * rows * width, 10 * rows * width),
        name="layer",
    )(length, returned, target_column, residual, gate)


def packed_rows(share, devices):
    unit = 16 * max(1, devices // 2)
    units = -(-(4 * share + 5) // unit)
    return [-(-units // 2) * unit, units // 2 * unit]


def pack_kernel(
    me_ref,
    grads_ref,
    tokens_ref,
    norms_ref,
    output_grad_ref,
    second_ref,
    *refs,
    shares,
):
    keeps, sends, (normed, sums, product) = refs[0:2], refs[2:4], refs[4:]
    step = pl.program_id(0)
    width = tokens_ref.shape[1]
    share = width // shares
    half = width // 2
    upper = (me_ref[0] & 1) != 0

    def put(number, first, values):
        border = keeps[0].shape[1]
        low, high = values[:, :half], values[:, half:]
        keep = jnp.where(upper, high, low).astype(BF)
        send = jnp.where(upper, low, high).astype(BF)
        for stream, (begin, end) in enumerate(((0, border), (border, 1 << 30))):
            a, b = max(first, begin), min(first + values.shape[0], end)
            if a < b:
                keeps[stream][number, a - begin : b - begin, :] = keep[a - first : b - first]
                sends[stream][number, a - begin : b - begin, :] = send[a - first : b - first]

    @pl.when(step == 0)
    def _():

        @pl.loop(0, tokens_ref.shape[0] // 256)
        def _(number):
            at = pl.ds(pl.multiple_of(number * 256, 256), 256)
            normal, _ = normalise(tokens_ref[at, :].astype(F32))
            low = (normal * norms_ref[0:1, :] + norms_ref[1:2, :]).astype(BF)
            normed[:, at] = low.T

    product[...] = dot(normed[...], grads_ref[...])
    sums[pl.ds(step, 1), :] = jnp.sum(grads_ref[...].astype(F32), axis=0, keepdims=True)
    for third in range(3):

        @pl.when(step == third)
        def _(third=third):
            @pl.loop(0, shares)
            def _(number):
                first = pl.multiple_of(number * share, 16)
                put(number, third * share, product[pl.ds(first, share), :])

    @pl.when(step == pl.num_programs(0) - 1)
    def _():
        total_rows = keeps[0].shape[1] + keeps[1].shape[1]
        rest = jnp.zeros((total_rows - 4 * share - 5, width), F32)
        tail = jnp.concatenate([sums[0:3, :], second_ref[0:2, :], rest], axis=0)

        @pl.loop(0, shares)
        def _(number):
            first = pl.multiple_of(number * share, 16)
            put(number, 3 * share, output_grad_ref[pl.ds(first, share), :].astype(F32))
            put(number, 4 * share, tail)


def pack(me, grads, tokens, norms, output_grad, second, shares, devices):
    rows, width = tokens.shape
    shapes = [(shares, count, width // 2) for count in packed_rows(width // shares, devices)] * 2
    whole = lambda shape: pl.BlockSpec(shape, lambda i, m: (0,) * len(shape))
    outs = pl.pallas_call(
        functools.partial(pack_kernel, shares=shares),
        out_shape=[jax.ShapeDtypeStruct(shape, BF) for shape in shapes],
        grid_spec=pltpu.PrefetchScalarGridSpec(
            num_scalar_prefetch=1,
            grid=(3,),
            in_specs=[
                pl.BlockSpec((None, rows, width), lambda i, m: (i, 0, 0)),
                whole((rows, width)),
                whole((4, width)),
                whole((width, width)),
                whole((8, width)),
            ],
            out_specs=[whole(shape) for shape in shapes],
            scratch_shapes=[
                pltpu.VMEM((width, rows), BF),
                pltpu.VMEM((8, width), F32),
                pltpu.VMEM((width, width), F32),
            ],
        ),
        compiler_params=params(40),
        cost_estimate=cost(6 * rows * width * width, 20 * rows * width),
        name="pack",
    )(me, grads, tokens, norms, output_grad, second)
    return outs[:2], outs[2:]


def project_back_kernel(
    grads_ref, tokens_ref, residual_grad_ref, weight_ref, norms_ref, out_ref
):
    width = tokens_ref.shape[1]
    gradient = None
    for number in range(3):
        columns = slice(number * width, (number + 1) * width)
        part = dot(grads_ref[number], weight_ref[:, columns], 1, 1)
        gradient = part if gradient is None else gradient + part
    normal, inverse = normalise(tokens_ref[...].astype(F32))
    input_part = norm_backward(normal, inverse, norms_ref[0:1, :], gradient)
    out_ref[...] = (residual_grad_ref[...] + input_part).astype(BF)


def project_back(grads, tokens, residual_grad, weight, norms):
    rows, width = tokens.shape
    block = 256
    part = pl.BlockSpec((block, width), lambda i: (i, 0))
    return pl.pallas_call(
        project_back_kernel,
        out_shape=jax.ShapeDtypeStruct((rows, width), BF),
        grid=(rows // block,),
        in_specs=[pl.BlockSpec((3, block, width), lambda i: (0, i, 0)), part, part]
        + [pl.BlockSpec(weight.shape, lambda i: (0, 0)), pl.BlockSpec((4, width), lambda i: (0, 0))],
        out_specs=part,
        compiler_params=params(24),
        cost_estimate=cost(18 * rows * width * width, 60 * rows * width),
        name="project_back",
    )(grads, tokens, residual_grad, weight, norms)


def add_kernel(left_ref, right_ref, out_ref):
    out_ref[...] = (left_ref[...].astype(F32) + right_ref[...].astype(F32)).astype(BF)


def add(left, right, pieces):
    (left, i), (right, j) = left, right
    _, rows, columns = left.shape
    half = pieces // 2
    spec = lambda first: pl.BlockSpec((half, rows, columns), lambda a: (first // half + a, 0, 0))
    size = pieces * rows * columns
    return pl.pallas_call(
        add_kernel,
        out_shape=jax.ShapeDtypeStruct((pieces, rows, columns), BF),
        grid=(2,),
        in_specs=[spec(i), spec(j)],
        out_specs=spec(0),
        compiler_params=params(10),
        cost_estimate=cost(0, 0),
        name="add",
    )(left, right)


def total_kernel(place_ref, middle_ref, end_ref, *refs, across):
    arrived, out_ref = refs[:-1], refs[-1]
    end = (place_ref[0] == 0) | (place_ref[0] == LINE - 1)
    rows, columns = middle_ref.shape[1:]
    for piece in range(middle_ref.shape[0]):
        total = jnp.where(end, end_ref[piece].astype(F32), middle_ref[piece].astype(F32))
        for ref in arrived:
            total = total + ref[piece].astype(F32)
        if across:
            out_ref[:, piece * columns : (piece + 1) * columns] = total
        else:
            out_ref[piece * rows : (piece + 1) * rows, :] = total


def line_total(place, middle, end, arrived, across):
    ins = [middle, end, *arrived]
    pieces, rows, columns = middle[0].shape
    shape = (rows, pieces * columns) if across else (pieces * rows, columns)
    half = pieces // 2
    block = (rows, half * columns) if across else (half * rows, columns)
    spec = lambda first: pl.BlockSpec((half, rows, columns), lambda a, p: (first // half + a, 0, 0))
    return pl.pallas_call(
        functools.partial(total_kernel, across=across),
        out_shape=jax.ShapeDtypeStruct(shape, F32),
        grid_spec=pltpu.PrefetchScalarGridSpec(
            num_scalar_prefetch=1,
            grid=(2,),
            in_specs=[spec(first) for _, first in ins],
            out_specs=pl.BlockSpec(block, lambda a, p: (0, a) if across else (a, 0)),
        ),
        compiler_params=params(60),
        cost_estimate=cost(0, 0),
        name="line_total",
    )(place, *[array for array, _ in ins])


class LineSum:
    def __init__(self, pairs, axis, place):
        self.axis, self.place = axis, place
        self.shares = lax.axis_size(axis)
        self.pairs = pairs
        self.line = self.shares == LINE and pairs[0][0][0] is pairs[0][1][0]
        self.got = {}

    def send(self, name, matrix=None):
        if not self.line:
            return
        ends = [(0, 1), (3, 2)]
        middles = [(1, 2), (2, 1)]
        out = [(2, 3), (1, 0)]

        def plus(number, before):
            if matrix is None:
                own = (self.pairs[number][0][0], 0)
                return add(own, (self.got[before], 0), own[0].shape[0])
            own = self.pairs[number][matrix]
            return add(own, (self.got[before], own[1]), self.pairs[MIDDLE][matrix][0].shape[0])

        values, route = {
            "far": lambda: (self.pairs[0][0][0], ends),
            "near": lambda: (self.pairs[1][0][0], ends),
            "own": lambda: (self.pairs[MIDDLE][matrix][0], ends),
            "far_on": lambda: (plus(0, "far"), middles),
            "near_on": lambda: (plus(1, "near"), middles),
            "far_out": lambda: (plus(3, "far_on"), out),
        }[name]()
        key = name if matrix is None else (name, matrix)
        self.got[key] = lax.ppermute(values, self.axis, route)

    def hold(self, name, values):
        if not self.line:
            return values
        self.got[name], values = lax.optimization_barrier((self.got[name], values))
        return values

    def totals(self):
        if self.line:
            sums = []
            for matrix in range(2):
                arrived = [(self.got[name, matrix], 0) for name in ("own", "near_on", "far_out")]
                ins = self.pairs[2][matrix], self.pairs[3][matrix]
                sums.append(line_total(self.place, *ins, arrived, across=matrix == 1))
            return sums
        sums = []
        for matrix in range(2):
            stacked = jnp.stack([pair[matrix][0] for pair in self.pairs])
            total = lax.psum_scatter(stacked, self.axis, scatter_dimension=0).astype(F32)
            pieces, rows, columns = total.shape
            if matrix:
                sums.append(total.swapaxes(0, 1).reshape(rows, pieces * columns))
            else:
                sums.append(total.reshape(pieces * rows, columns))
        return sums


def partner_pairs(axis, bit):
    return [(i, i ^ bit) for i in range(lax.axis_size(axis))]


def halves_kernel(me_ref, *refs, edges, bits):
    streams = len(bits)
    ins, outs = refs[: len(refs) - 2 * streams], refs[len(refs) - 2 * streams :]
    for stream, (first, last) in enumerate(edges):
        keep, got = ins[:2] if len(ins) == 2 else ins[2 * stream : 2 * stream + 2]
        kept, sent = outs[2 * stream : 2 * stream + 2]
        size = (last - first) // 2
        upper = (me_ref[0] // bits[stream]) % 2
        mine = pl.multiple_of(first + upper * size, 16)
        other = pl.multiple_of(first + (1 - upper) * size, 16)
        for at, out in ((mine, kept), (other, sent)):
            total = keep[:, pl.ds(at, size), :].astype(F32) + got[:, pl.ds(at, size), :].astype(F32)
            out[...] = total.astype(BF)


def halves(me, bits, edges, pairs, level):
    shares = pairs[0][0].shape[0]
    spec = lambda rows, columns: pl.BlockSpec((1, rows, columns), lambda z, m: (z, 0, 0))
    in_specs, out_specs, out_shape = [], [], []
    for keep, _ in pairs:
        in_specs += [spec(*keep.shape[1:])] * 2
    columns = pairs[0][0].shape[2]
    for first, last in edges:
        rows = (last - first) // 2
        out_specs += [spec(rows, columns)] * 2
        out_shape += [jax.ShapeDtypeStruct((shares, rows, columns), BF)] * 2
    size = sum(keep.size for keep, _ in pairs)
    outs = pl.pallas_call(
        functools.partial(halves_kernel, edges=edges, bits=bits),
        out_shape=out_shape,
        grid_spec=pltpu.PrefetchScalarGridSpec(
            num_scalar_prefetch=1, grid=(shares,), in_specs=in_specs, out_specs=out_specs
        ),
        compiler_params=params(20),
        cost_estimate=cost(0, 0 * size * level),
        name="halves",
    )(me, *[array for pair in pairs for array in pair])
    return [(outs[2 * i], outs[2 * i + 1]) for i in range(len(bits))]


def join_kernel(*refs):
    ins, out_ref = refs[:-1], refs[-1]
    first = 0
    for keep, got in zip(ins[::2], ins[1::2]):
        last = first + keep.shape[1]
        total = keep[...].astype(F32) + got[...].astype(F32)
        out_ref[:, first:last, :] = total.astype(BF)
        first = last


def join(pairs):
    shares, _, columns = pairs[0][0].shape
    rows = sum(keep.shape[1] for keep, _ in pairs)
    size = shares * rows * columns
    return pl.pallas_call(
        join_kernel,
        out_shape=jax.ShapeDtypeStruct((shares, rows, columns), BF),
        compiler_params=params(12),
        cost_estimate=cost(0, 0),
        name="join",
    )(*[array for pair in pairs for array in pair])


def spread_kernel(parts_ref, out_ref):
    total = jnp.sum(parts_ref[...].astype(F32), axis=0).astype(BF)
    for number in range(out_ref.shape[0]):
        out_ref[number] = total


def spread(parts, devices):
    _, rows, columns = parts.shape
    size = parts.size + devices * rows * columns
    return pl.pallas_call(
        spread_kernel,
        out_shape=jax.ShapeDtypeStruct((devices, rows, columns), BF),
        compiler_params=params(12),
        cost_estimate=cost(0, 0),
        name="spread",
    )(parts)


def assemble_kernel(
    place_ref,
    gathered_ref,
    weight_ref,
    norms_ref,
    input_ref,
    output_ref,
    column_ref,
    tail_ref,
    summed,
    *,
    sources,
):
    half = gathered_ref.shape[2]
    share, width = output_ref.shape
    for device, first, count, to, side in sources:
        values = gathered_ref[device, first : first + count, :].astype(F32)
        summed[to : to + count, side * half : (side + 1) * half] = values
    shift_sum = gain_sum = 0.0
    for third in range(3):
        columns = slice(third * width, (third + 1) * width)
        values = summed[third * share : (third + 1) * share, :]
        input_ref[:, columns] = values
        weight = weight_ref[:, columns].astype(F32)
        line = summed[4 * share + third : 4 * share + third + 1, :]
        shift_sum = shift_sum + jnp.sum(weight * line, axis=1, keepdims=True)
        gain_sum = gain_sum + jnp.sum(weight * values, axis=1, keepdims=True)
    output_ref[...] = summed[3 * share : 4 * share, :]
    lane = lax.broadcasted_iota(jnp.int32, (1, 128), 1)
    column_ref[...] = jnp.where(lane == 0, gain_sum, shift_sum)
    tail_ref[...] = summed[4 * share : 4 * share + 8, :]


def assemble(place, gathered, weight, norms, share, orders, streams):
    devices, _, half = gathered.shape
    width = 2 * half
    levels = len(orders[0])
    sources = []
    for side in range(2):
        first, to = 0, 0
        for count, order in zip(streams, orders):
            for number in range(2**levels):
                digits = [(number >> (levels - 1 - level)) & 1 for level in range(levels)]
                device = side + sum(digit * bit for digit, bit in zip(digits, order))
                sources.append((device, first, count, to, side))
                to += count
            first += count
    total = sum(streams) * 2**levels
    whole = lambda shape: pl.BlockSpec(shape, lambda i, p: (0,) * len(shape))
    return pl.pallas_call(
        functools.partial(assemble_kernel, sources=sources),
        out_shape=[
            jax.ShapeDtypeStruct((share, 3 * width), F32),
            jax.ShapeDtypeStruct((share, width), F32),
            jax.ShapeDtypeStruct((share, 128), F32),
            jax.ShapeDtypeStruct((8, width), F32),
        ],
        grid_spec=pltpu.PrefetchScalarGridSpec(
            num_scalar_prefetch=1,
            grid=(1,),
            in_specs=[
                whole(gathered.shape),
                pl.BlockSpec((share, 3 * width), lambda i, p: (p[0], 0)),
                whole(norms.shape),
            ],
            out_specs=[
                whole((share, 3 * width)),
                whole((share, width)),
                whole((share, 128)),
                whole((8, width)),
            ],
            scratch_shapes=[pltpu.VMEM((total, width), F32)],
        ),
        compiler_params=params(24),
        cost_estimate=cost(0, 0),
        name="assemble",
    )(place, gathered, weight, norms)


def on_device(
    tokens,
    lengths,
    expert_index,
    centroids,
    input_weight,
    output_weight,
    first_gain,
    first_shift,
    second_gain,
    second_shift,
    up_weight,
    down_weight,
    cotangent,
):
    rows, width = tokens.shape
    experts = centroids.shape[0]
    capacity = rows // experts
    shares = lax.axis_size("dp")
    share = width // shares
    me = lax.axis_index("expert").reshape(1).astype(jnp.int32)
    place = lax.axis_index("dp").reshape(1).astype(jnp.int32)
    norms = jnp.stack([first_gain, first_shift, second_gain, second_shift])

    def exchange(values, axis="expert"):
        return lax.all_to_all(values, axis, split_axis=0, concat_axis=0, tiled=True)

    def dispatch(values):
        return exchange(values.reshape(experts, capacity, -1)).reshape(rows, -1)

    outgoing_cotangent, target_row, target_column = route(
        lengths, expert_index, cotangent, experts
    )
    arrived_cotangent = dispatch(outgoing_cotangent)
    held_tokens, target_row = lax.optimization_barrier((tokens, target_row))
    projected = project(held_tokens, input_weight, norms)
    mixed, total = attend(lengths, projected)
    mixed, arrived_cotangent = lax.optimization_barrier((mixed, arrived_cotangent))
    residual, gate, outgoing = hidden_rows(
        lengths, mixed, tokens, output_weight, norms, centroids, target_row, target_column
    )
    arrived = dispatch(outgoing)
    order = place if shares == LINE else jnp.full_like(place, shares)
    produced, back, pairs = expert(
        me, order, arrived, arrived_cotangent, centroids, up_weight[0], down_weight[0], shares
    )
    line = LineSum(pairs, "dp", place)
    line.send("far")
    line.send("near")
    produced, returned = lax.optimization_barrier((produced, dispatch(back)))
    residual_grad, mixed_grad, output_grad, second_gains = combine(
        lengths, returned, target_column, cotangent, residual, norms, mixed, output_weight
    )
    produced, mixed_grad = lax.optimization_barrier((produced, mixed_grad))
    returned = dispatch(produced)
    mixed_grad = line.hold("far", mixed_grad)
    line.send("far_on")
    grads = attend_back(lengths, projected, mixed, total, mixed_grad)
    grads, returned = lax.optimization_barrier((grads, returned))
    keeps, sends = pack(
        me, grads, tokens, norms, output_grad, second_gains, shares, experts
    )
    swap = lambda values, bit: lax.ppermute(values, "expert", partner_pairs("expert", bit))
    pairs = [(keep, swap(send, 1)) for keep, send in zip(keeps, sends)]
    bits = [2**i for i in range(1, (experts - 1).bit_length())]
    orders = [bits, bits[::-1]]
    for level, now in enumerate(zip(*orders)):
        made = halves(me, now, [(0, keep.shape[1]) for keep, _ in pairs], pairs, level)
        pairs = [(kept, swap(sent, bit)) for (kept, sent), bit in zip(made, now)]
        if level == 0:
            kept, got = pairs[0]
            kept = line.hold("near", kept)
            line.send("own", 0)
            line.send("near_on", 0)
            kept = line.hold("far_on", kept)
            line.send("far_out", 0)
            pairs[0] = (kept, got)
    input_gradient = project_back(grads, tokens, residual_grad, input_weight, norms)
    input_gradient, pairs = lax.optimization_barrier((input_gradient, pairs))
    for name in ("far_out", "near_on", "own"):
        pairs = line.hold((name, 0), pairs)
    streams = [keep.shape[1] for keep, _ in pairs]
    joined = join(pairs)
    joined, returned = lax.optimization_barrier((joined, returned))
    over_line = exchange(joined, "dp")
    layer_output = layer(lengths, returned, target_column, residual, gate)
    for name in ("far_out", "near_on", "own"):
        line.send(name, 1)
    gathered = exchange(spread(over_line, experts))
    input_share, output_share, sums, tail = assemble(
        place, gathered, input_weight, norms, share, orders, streams
    )
    for name in ("far_out", "near_on", "own"):
        sums = line.hold((name, 1), sums)
    begin = lax.axis_index("dp") * share
    mine = lambda vector: lax.dynamic_slice_in_dim(vector, begin, share, vector.ndim - 1)
    shift_sum = sums[:, 1]
    gain_sum = (sums[:, 0] - mine(first_shift) * shift_sum) / mine(first_gain)
    second = mine(tail[3:5])
    down_share, up_share = line.totals()
    return (
        layer_output,
        input_gradient,
        input_share,
        output_share,
        gain_sum,
        shift_sum,
        second[0],
        second[1],
        up_share[None],
        down_share[None],
    )


def solution(mesh):
    both = P(("dp", "expert"))
    rows = P(("dp", "expert"), None)
    weights = P("expert", None, None)
    return jax.shard_map(
        on_device,
        mesh=mesh,
        in_specs=(rows, both, both, P(), P(), P(), P(), P(), P(), P(), weights, weights, rows),
        out_specs=(
            rows,
            rows,
            P("dp", None),
            P("dp", None),
            P("dp"),
            P("dp"),
            P("dp"),
            P("dp"),
            P("expert", "dp", None),
            P("expert", "dp", None),
        ),
        check_vma=False,
    )
```

```python
import functools

import jax
import jax.numpy as jnp
from jax import lax
from jax.experimental import pallas as pl
from jax.experimental.pallas import tpu as pltpu
from jax.sharding import PartitionSpec as P

HEADS = 12
EPS = 1e-05
EXCLUDED = -1e30
BF = jnp.bfloat16
F32 = jnp.float32
QUERY_ROWS = 256
SEEN = 1
EXPERT_MIB = 54
HIDDEN_MIB = 60


def dot(left, right, left_axis=1, right_axis=0):
    return lax.dot_general(
        left,
        right,
        (((left_axis,), (right_axis,)), ((), ())),
        preferred_element_type=F32,
    )


def params(limit=60):
    return pltpu.CompilerParams(vmem_limit_bytes=limit << 20)


def cost(flops, bytes_accessed, transcendentals=0):
    return pl.CostEstimate(
        flops=int(flops * SEEN),
        bytes_accessed=int(bytes_accessed * SEEN),
        transcendentals=int(transcendentals * SEEN),
    )


def split_three(values):
    high = values.astype(BF)
    rest = values - high.astype(F32)
    middle = rest.astype(BF)
    return high, middle, (rest - middle.astype(F32)).astype(BF)


def normalise(values):
    average = jnp.mean(values, axis=-1, keepdims=True)
    centred = values - average
    variance = jnp.mean(centred * centred, axis=-1, keepdims=True)
    inverse = lax.rsqrt(variance + EPS)
    return centred * inverse, inverse


def norm_backward(normal, inverse, gain, gradient):
    scaled = gain * gradient
    first = jnp.mean(scaled, axis=-1, keepdims=True)
    second = jnp.mean(scaled * normal, axis=-1, keepdims=True)
    return (scaled - first - normal * second) * inverse


def selection(target, first, count):
    rows = lax.broadcasted_iota(jnp.int32, (count, target.shape[1]), 0) + first
    return jnp.where(rows == target, 1.0, 0.0).astype(BF)


def route_kernel(length_ref, expert_ref, cotangent_ref, out_ref, row_ref, column_ref, *, experts):
    step = pl.program_id(0)
    rows = cotangent_ref.shape[0]
    block = out_ref.shape[0]

    @pl.when(step == 0)
    def _():
        length = length_ref[0]
        position = lax.broadcasted_iota(jnp.int32, (1, rows), 1)
        named = jnp.where(position < length, expert_ref[...], -1)
        number = lax.broadcasted_iota(jnp.int32, (experts, rows), 0)
        onehot = jnp.where(number == named, 1.0, 0.0)
        before = lax.broadcasted_iota(jnp.int32, (rows, rows), 0)
        after = lax.broadcasted_iota(jnp.int32, (rows, rows), 1)
        earlier = jnp.where(before < after, 1.0, 0.0).astype(BF)
        counts = dot(onehot.astype(BF), earlier)
        slot = jnp.sum(onehot * counts, axis=0, keepdims=True).astype(jnp.int32)
        target = jnp.where(named >= 0, named * (rows // experts) + slot, -1)
        row_ref[...] = jnp.broadcast_to(target, row_ref.shape)
        wide = jnp.broadcast_to(target.astype(F32), (128, rows))
        column_ref[...] = wide.T.astype(jnp.int32)

    chosen = selection(row_ref[0:1, :], step * block, block)
    out_ref[...] = dot(chosen, cotangent_ref[...]).astype(BF)


def route(length, expert_index, cotangent, experts):
    rows, width = cotangent.shape
    block = 512
    return pl.pallas_call(
        functools.partial(route_kernel, experts=experts),
        out_shape=[
            jax.ShapeDtypeStruct((rows, width), BF),
            jax.ShapeDtypeStruct((8, rows), jnp.int32),
            jax.ShapeDtypeStruct((rows, 128), jnp.int32),
        ],
        grid_spec=pltpu.PrefetchScalarGridSpec(
            num_scalar_prefetch=1,
            grid=(rows // block,),
            in_specs=[
                pl.BlockSpec((1, rows), lambda i, l: (0, 0)),
                pl.BlockSpec((rows, width), lambda i, l: (0, 0)),
            ],
            out_specs=[
                pl.BlockSpec((block, width), lambda i, l: (i, 0)),
                pl.BlockSpec((8, rows), lambda i, l: (0, 0)),
                pl.BlockSpec((rows, 128), lambda i, l: (0, 0)),
            ],
        ),
        compiler_params=params(60),
        cost_estimate=cost(2 * rows * rows * width, 4 * rows * width),
        name="route",
    )(length, expert_index.reshape(1, rows), cotangent)


def project_kernel(tokens_ref, weight_ref, norms_ref, out_ref):
    normal, _ = normalise(tokens_ref[...].astype(F32))
    normed = (normal * norms_ref[0:1, :] + norms_ref[1:2, :]).astype(BF)
    out_ref[...] = dot(normed, weight_ref[...]).astype(BF)


def project(tokens, weight, norms):
    rows, width = tokens.shape
    columns = weight.shape[1]
    block = 256
    return pl.pallas_call(
        project_kernel,
        out_shape=jax.ShapeDtypeStruct((rows, columns), BF),
        grid=(rows // block,),
        in_specs=[
            pl.BlockSpec((block, width), lambda i: (i, 0)),
            pl.BlockSpec((width, columns), lambda i: (0, 0)),
            pl.BlockSpec((4, width), lambda i: (0, 0)),
        ],
        out_specs=pl.BlockSpec((block, columns), lambda i: (i, 0)),
        compiler_params=params(24),
        cost_estimate=cost(2 * rows * width * columns, 2 * (rows + width) * columns),
        name="project",
    )(tokens, weight, norms)


def staggered(items, begin, finish, ahead=1):
    waiting = []
    for item in items:
        waiting.append((item, begin(item)))
        if len(waiting) > ahead:
            finish(*waiting.pop(0))
    for item, values in waiting:
        finish(item, values)


def length_bias(rows, length):
    row = lax.broadcasted_iota(jnp.int32, (rows, 1), 0)
    return jnp.where(row < length, 0.0, EXCLUDED).astype(BF)


def attend_kernel(length_ref, query_ref, key_ref, value_ref, mixed_ref, total_ref, *, scale, half):
    rows = query_ref.shape[0]
    lane = lax.broadcasted_iota(jnp.int32, (1, 2 * half), 1)
    zero, one = jnp.zeros((), BF), jnp.ones((), BF)
    bias = length_bias(rows, length_ref[0])
    done = {}
    place = lax.broadcasted_iota(jnp.int32, (1, 128), 1)
    first = 2 * pl.program_id(0)
    keys = [jnp.where(lane == half * (1 - head), bias, key_ref[...]) for head in range(2)]

    def scores_of(item):
        start, head = item
        end = start + QUERY_ROWS
        row = lax.broadcasted_iota(jnp.int32, (QUERY_ROWS, QUERY_ROWS), 0)
        column = lax.broadcasted_iota(jnp.int32, (QUERY_ROWS, QUERY_ROWS), 1)
        scaled = query_ref[start:end, :] * jnp.asarray(scale, BF)
        rest = jnp.where(lane == half * (1 - head), one, zero)
        scores = dot(jnp.where((lane // half) == head, scaled, rest), keys[head][:end], 1, 1)
        last = jnp.where(column <= row, scores[:, start:], EXCLUDED)
        return jnp.concatenate([scores[:, :start], last], axis=1) if start else last

    def mix(item, scores):
        start, head = item
        end = start + QUERY_ROWS
        other = half * (1 - head)
        ones = jnp.where(lane == other, one, zero)
        value = jnp.where((lane // half) == head, value_ref[:end, :], ones)
        top = jnp.max(scores, axis=1, keepdims=True)
        out = dot(jnp.exp(scores - top).astype(BF), value)
        total = out[:, other : other + 1]
        done[item] = (out / total, top + jnp.log(total))
        if head == 1:
            low, high = done[start, 0], done[start, 1]
            mixed_ref[start:end, :] = jnp.where(lane < half, low[0], high[0]).astype(BF)
            other = jnp.where(place == first + 1, high[1], total_ref[start:end, :])
            total_ref[start:end, :] = jnp.where(place == first, low[1], other)

    starts = range(0, rows, QUERY_ROWS)
    staggered([(start, head) for start in starts for head in range(2)], scores_of, mix, 2)


def pair_specs(rows, wide, pairs, thirds):
    return [pl.BlockSpec((rows, wide), lambda i, l, o=o: (0, i + o * pairs)) for o in range(thirds)]


def attend(length, projected):
    rows, width = projected.shape[0], projected.shape[1] // 3
    size = width // HEADS
    pairs = HEADS // 2
    one = pl.BlockSpec((rows, 2 * size), lambda i, l: (0, i))
    return pl.pallas_call(
        functools.partial(attend_kernel, scale=size**-0.5, half=size),
        out_shape=[
            jax.ShapeDtypeStruct((rows, width), BF),
            jax.ShapeDtypeStruct((rows, 128), F32),
        ],
        grid_spec=pltpu.PrefetchScalarGridSpec(
            num_scalar_prefetch=1,
            grid=(pairs,),
            in_specs=pair_specs(rows, 2 * size, pairs, 3),
            out_specs=[one, pl.BlockSpec((rows, 128), lambda i, l: (0, 0))],
        ),
        compiler_params=params(16),
        cost_estimate=cost(
            16 * rows * rows * width, 12 * rows * width, HEADS * rows * rows // 2
        ),
        name="attend",
    )(length, projected, projected, projected)


def attend_back_kernel(
    length_ref,
    query_ref,
    key_ref,
    value_ref,
    mixed_ref,
    total_ref,
    incoming_ref,
    out_ref,
    key_sum,
    value_sum,
    *,
    scale,
    half,
):
    lane = lax.broadcasted_iota(jnp.int32, (1, 2 * half), 1)
    bias = length_bias(query_ref.shape[0], length_ref[0])
    zero, one = jnp.zeros((), BF), jnp.ones((), BF)
    key_sum[...] = jnp.zeros_like(key_sum)
    value_sum[...] = jnp.zeros_like(value_sum)
    parts = {}

    def products(item):
        start, head = item
        end = start + QUERY_ROWS
        mine = (lane // half) == head
        other = half * (1 - head)
        ones = jnp.where((lane >= other) & (lane < other + 3), one, zero)

        def extend(base, column, spare):
            a, b, c = split_three(-column)
            rest = jnp.where(lane == other + 2, c, jnp.where(lane == other + 3, spare, zero))
            rest = jnp.where(lane == other + 1, b, rest)
            return jnp.where(mine, base, jnp.where(lane == other, a, rest))

        row = lax.broadcasted_iota(jnp.int32, (QUERY_ROWS, QUERY_ROWS), 0)
        column = lax.broadcasted_iota(jnp.int32, (QUERY_ROWS, QUERY_ROWS), 1)
        incoming = incoming_ref[start:end, :]
        product = incoming.astype(F32) * mixed_ref[start:end, :].astype(F32)
        query = jnp.where(mine, query_ref[start:end, :] * jnp.asarray(scale, BF), zero)
        grad = jnp.where(mine, incoming, zero)
        inner = jnp.sum(jnp.where(mine, product, 0.0), axis=1, keepdims=True)
        number = 2 * pl.program_id(0) + head
        at = lax.broadcasted_iota(jnp.int32, (1, 128), 1) == number
        total = jnp.sum(jnp.where(at, total_ref[start:end, :], 0.0), axis=1, keepdims=True)
        spare = jnp.where(lane == other + 3, bias[:end], ones)
        key = jnp.where(mine, key_ref[:end, :], spare)
        scores = dot(key, extend(query, total, one), 1, 1)
        last = jnp.where(row <= column, scores[start:, :], EXCLUDED)
        scores = jnp.concatenate([scores[:start, :], last], axis=0) if start else last
        value = jnp.where(mine, value_ref[:end, :], ones)
        return scores, dot(value, extend(grad, inner, zero), 1, 1), query, grad

    def gradients(item, values):
        start, head = item
        scores, centred, query, grad = values
        end = start + QUERY_ROWS
        probs = jnp.exp(scores)
        score_gradient = (probs * centred).astype(BF)
        value_sum[:end, :] += dot(probs.astype(BF), grad)
        key_sum[:end, :] += dot(score_gradient, query)
        key = jnp.where((lane // half) == head, key_ref[:end, :], zero)
        parts[item] = dot(score_gradient, key, 0, 0)
        if head == 1:
            total = parts[start, 0] + parts[start, 1]
            out_ref[0, start:end, :] = (total * scale).astype(BF)

    starts = range(0, query_ref.shape[0], QUERY_ROWS)
    staggered([(start, head) for start in starts for head in range(2)], products, gradients)
    out_ref[1] = key_sum[...].astype(BF)
    out_ref[2] = value_sum[...].astype(BF)


def attend_back(length, projected, mixed, total, incoming):
    rows, width = projected.shape[0], projected.shape[1] // 3
    size = width // HEADS
    pairs = HEADS // 2
    one = pl.BlockSpec((rows, 2 * size), lambda i, l: (0, i))
    return pl.pallas_call(
        functools.partial(attend_back_kernel, scale=size**-0.5, half=size),
        out_shape=jax.ShapeDtypeStruct((3, rows, width), BF),
        grid_spec=pltpu.PrefetchScalarGridSpec(
            num_scalar_prefetch=1,
            grid=(pairs,),
            in_specs=pair_specs(rows, 2 * size, pairs, 3)
            + [one, pl.BlockSpec((rows, 128), lambda i, l: (0, 0)), one],
            out_specs=pl.BlockSpec((3, rows, 2 * size), lambda i, l: (0, 0, i)),
            scratch_shapes=[pltpu.VMEM((rows, 2 * size), F32)] * 2,
        ),
        compiler_params=params(60),
        cost_estimate=cost(
            30 * rows * rows * width, 20 * rows * width
        ),
        name="attend_back",
    )(length, projected, projected, projected, mixed, total, incoming)


def picked_rows(target, centroids_ref, capacity):
    experts, width = centroids_ref.shape
    pieces = [piece.astype(F32) for piece in split_three(centroids_ref[...])]
    rest = jnp.zeros((128 - 3 * experts, width), F32)
    table = jnp.concatenate(pieces + [rest], axis=0).astype(BF)
    lane = lax.broadcasted_iota(jnp.int32, (1, 128), 1)
    low = jnp.where(lane < 3 * experts, (lane % experts) * capacity, 1 << 20)
    onehot = jnp.where((target >= low) & (target < low + capacity), 1.0, 0.0).astype(BF)
    return dot(onehot, table)


def present_rows(block_index, count, length):
    row = lax.broadcasted_iota(jnp.int32, (count, 1), 0) + block_index * count
    return jnp.where(row < length, 1.0, 0.0)


def hidden_kernel(
    length_ref,
    mixed_ref,
    tokens_ref,
    weight_ref,
    norms_ref,
    centroids_ref,
    row_ref,
    column_ref,
    residual_ref,
    gate_ref,
    out_ref,
    hidden_low,
):
    rows = row_ref.shape[1]
    count = 256

    def branch_of(number):
        return dot(mixed_ref[number * count : (number + 1) * count, :], weight_ref[...])

    def finish(number, branch):
        at = slice(number * count, (number + 1) * count)
        mask = present_rows(number, count, length_ref[0])
        residual = tokens_ref[at, :].astype(F32) + mask * branch
        residual_ref[at, :] = residual
        normal, _ = normalise(residual)
        hidden = normal * norms_ref[2:3, :] + norms_ref[3:4, :]
        picked = picked_rows(column_ref[at, :], centroids_ref, rows // centroids_ref.shape[0])
        gate = jax.nn.sigmoid(jnp.sum(hidden * picked, axis=-1, keepdims=True))
        gate_ref[at, :] = jnp.broadcast_to(gate, (count, 128))
        hidden_low[at, :] = hidden.astype(BF)

    staggered(range(rows // count), branch_of, finish)
    for first in range(0, rows, count):
        chosen = selection(row_ref[0:1, :], first, count)
        out_ref[first : first + count, :] = dot(chosen, hidden_low[...]).astype(BF)


def hidden_rows(length, mixed, tokens, weight, norms, centroids, target_row, target_column):
    rows, width = tokens.shape
    experts = centroids.shape[0]
    whole = lambda *shape: pl.BlockSpec(shape, lambda i, l: (0,) * len(shape))
    return pl.pallas_call(
        hidden_kernel,
        out_shape=[
            jax.ShapeDtypeStruct((rows, width), F32),
            jax.ShapeDtypeStruct((rows, 128), F32),
            jax.ShapeDtypeStruct((rows, width), BF),
        ],
        grid_spec=pltpu.PrefetchScalarGridSpec(
            num_scalar_prefetch=1,
            grid=(1,),
            in_specs=[
                whole(rows, width),
                whole(rows, width),
                whole(width, width),
                whole(4, width),
                whole(experts, width),
                whole(8, rows),
                whole(rows, 128),
            ],
            out_specs=[whole(rows, width), whole(rows, 128), whole(rows, width)],
            scratch_shapes=[pltpu.VMEM((rows, width), BF)],
        ),
        compiler_params=params(HIDDEN_MIB),
        cost_estimate=cost(2 * rows * (rows + width) * width, 12 * rows * width),
        name="hidden_rows",
    )(length, mixed, tokens, weight, norms, centroids, target_row, target_column)


LINE = 4
MIDDLE = 2


def far_first(number, place, shares):
    return jnp.where(place < shares // 2, shares - 1 - number, number)


def expert_kernel(
    me_ref,
    place_ref,
    rows_ref,
    cotangent_ref,
    centroids_ref,
    up_ref,
    down_ref,
    produced_ref,
    back_ref,
    *refs,
    shares,
    together,
):
    outs, scratch = refs[:-8], refs[-8:]
    produced_sum, back_sum, transposed, gradient, gates, downs, ups, sems = scratch
    step = pl.program_id(0)
    count, width = rows_ref.shape
    share = width // shares

    @pl.when(step == 0)
    def _():
        hidden = rows_ref[...].astype(F32)
        centroid = centroids_ref[pl.ds(me_ref[0], 1), :]
        gate = jax.nn.sigmoid(jnp.sum(hidden * centroid, axis=-1, keepdims=True))
        gradient[...] = (gate * cotangent_ref[...].astype(F32)).astype(BF)
        gates[...] = jnp.broadcast_to(gate, gates.shape)
        produced_sum[...] = jnp.zeros_like(produced_sum)
        back_sum[...] = jnp.zeros_like(back_sum)
        values = rows_ref[...].T
        for number in range(shares):
            to = pl.multiple_of(far_first(number, place_ref[0], shares) * share, 16)
            transposed[pl.ds(to, share), :] = values[number * share : (number + 1) * share]

    upper = dot(rows_ref[...], up_ref[...])
    part = 0.5 + 0.5 * lax.erf(upper * (0.5**0.5))
    density = jnp.exp(upper * upper * -0.5) * 0.3989422804014327
    active = (upper * part).astype(BF)
    slope = part + upper * density
    active_gradient = dot(gradient[...], down_ref[...], 1, 1)
    upper_gradient = (active_gradient * slope).astype(BF)
    produced_sum[...] += dot(active, down_ref[...])
    down = dot(active, gradient[...], 0, 0).astype(BF)
    back_sum[...] += dot(upper_gradient, up_ref[...], 1, 1)
    up = dot(transposed[...], upper_gradient).astype(BF)
    real = far_first(step, place_ref[0], shares)
    slot = lax.rem(step, 2)
    pieces = down.shape[0] // share
    places = out_places(shares, pieces, together)

    def down_copy(number, slot):
        target = outs[places[number][0][0]].at[pl.ds(0, pieces)]
        return pltpu.make_async_copy(downs.at[slot], target, sems.at[slot, shares])

    def up_copy(number, slot, piece):
        array, first = places[number][1]
        target = outs[array].at[first + piece]
        return pltpu.make_async_copy(ups.at[slot, number], target, sems.at[slot, number])

    def wait(slot):
        down_copy(0, slot).wait()
        for number in range(shares):
            up_copy(number, slot, 0).wait()

    @pl.when(step >= 2)
    def _():
        wait(slot)

    for piece in range(pieces):
        downs[slot, piece] = down[piece * share : (piece + 1) * share]
    for number in range(shares):
        ups[slot, number] = up[number * share : (number + 1) * share]
        up_copy(number, slot, real).start()

        @pl.when(step == number)
        def _(number=number):
            down_copy(number, slot).start()

    @pl.when(step == pl.num_programs(0) - 1)
    def _():
        centroid = centroids_ref[pl.ds(me_ref[0], 1), :]

        @pl.loop(0, count // 256)
        def _(number):
            at = pl.ds(pl.multiple_of(number * 256, 256), 256)
            produced = produced_sum[at, :].astype(BF)
            produced_ref[at, :] = produced
            gate = gates[at, 0:1]
            cotangent = cotangent_ref[at, :].astype(F32)
            along = jnp.sum(cotangent * produced.astype(F32), axis=-1, keepdims=True)
            logit_gradient = along * gate * (1.0 - gate)
            back_ref[at, :] = (back_sum[at, :] + logit_gradient * centroid).astype(BF)
        wait(1 - slot)
        wait(slot)


def out_places(shares, pieces, together):
    places, count = [], 0
    for number in range(shares):
        if together and number != MIDDLE:
            places.append(((count, 0), (count, pieces)))
            count += 1
        else:
            places.append(((count, 0), (count + 1, 0)))
            count += 2
    return places


def expert(me, place, hidden, cotangent, centroids, up, down, shares):
    count, width = hidden.shape
    inner = up.shape[1]
    chunk, share = inner // shares, width // shares
    together = shares == LINE and chunk == width
    still = lambda c, m, p: (0, 0)
    once = pl.Buffered(1)
    whole = pl.BlockSpec((count, width), still, pipeline_mode=once)
    real = lambda c, p: far_first(c, p[0], shares)
    pieces = chunk // share
    places = out_places(shares, pieces, together)
    shapes = []
    for number in range(shares):
        if together and number != MIDDLE:
            shapes.append((pieces + shares, share, width))
        else:
            shapes += [(pieces, share, width), (shares, share, chunk)]
    outs = pl.pallas_call(
        functools.partial(expert_kernel, shares=shares, together=together),
        out_shape=[jax.ShapeDtypeStruct((count, width), BF)] * 2
        + [jax.ShapeDtypeStruct(shape, BF) for shape in shapes],
        grid_spec=pltpu.PrefetchScalarGridSpec(
            num_scalar_prefetch=2,
            grid=(shares,),
            in_specs=[
                whole,
                whole,
                pl.BlockSpec(centroids.shape, still, pipeline_mode=once),
                pl.BlockSpec((width, chunk), lambda c, m, p: (0, real(c, p))),
                pl.BlockSpec((chunk, width), lambda c, m, p: (real(c, p), 0)),
            ],
            out_specs=[whole, whole] + [pl.BlockSpec(memory_space=pl.ANY)] * len(shapes),
            scratch_shapes=[
                pltpu.VMEM((count, width), F32),
                pltpu.VMEM((count, width), F32),
                pltpu.VMEM((width, count), BF),
                pltpu.VMEM((count, width), BF),
                pltpu.VMEM((count, 128), F32),
                pltpu.VMEM((2, pieces, share, width), BF),
                pltpu.VMEM((2, shares, share, chunk), BF),
                pltpu.SemaphoreType.DMA((2, shares + 1)),
            ],
        ),
        compiler_params=params(EXPERT_MIB),
        cost_estimate=cost(12 * count * width * inner, 8 * inner * width, 2 * count * inner),
        name="expert",
    )(me, place, hidden, cotangent, centroids, up, down)
    arrays = outs[2:]
    pairs = [[(arrays[number], first) for number, first in pair] for pair in places]
    return outs[0], outs[1], pairs


def combine_kernel(
    length_ref,
    returned_ref,
    column_ref,
    cotangent_ref,
    residual_ref,
    norms_ref,
    mixed_ref,
    weight_ref,
    residual_grad_ref,
    mixed_grad_ref,
    weight_grad_ref,
    gains_ref,
    weight_sum,
):
    step = pl.program_id(0)
    count = cotangent_ref.shape[0]

    @pl.when(step == 0)
    def _():
        weight_sum[...] = jnp.zeros_like(weight_sum)
        gains_ref[...] = jnp.zeros_like(gains_ref)

    hidden_gradient = gathered_rows(column_ref, returned_ref)
    mask = present_rows(step, count, length_ref[0])
    normal, inverse = normalise(residual_ref[...])
    gains_ref[0:1, :] += jnp.sum(hidden_gradient * normal, axis=0, keepdims=True)
    gains_ref[1:2, :] += jnp.sum(hidden_gradient, axis=0, keepdims=True)
    residual_gradient = cotangent_ref[...].astype(F32) + norm_backward(
        normal, inverse, norms_ref[2:3, :], hidden_gradient
    )
    residual_grad_ref[...] = residual_gradient
    branch_gradient = (mask * residual_gradient).astype(BF)
    mixed_grad_ref[...] = dot(branch_gradient, weight_ref[...], 1, 1).astype(BF)
    weight_sum[...] += dot(mixed_ref[...], branch_gradient, 0, 0)

    @pl.when(step == pl.num_programs(0) - 1)
    def _():
        weight_grad_ref[...] = weight_sum[...].astype(BF)


def gathered_rows(column_ref, slots_ref):
    place = lax.broadcasted_iota(jnp.int32, (column_ref.shape[0], slots_ref.shape[0]), 1)
    chosen = jnp.where(place == column_ref[:, 0:1], 1.0, 0.0).astype(BF)
    return dot(chosen, slots_ref[...])


def combine(length, returned, target_column, cotangent, residual, norms, mixed, weight):
    rows, width = cotangent.shape
    block = 256
    part = pl.BlockSpec((block, width), lambda i, l: (i, 0))
    thin = pl.BlockSpec((block, 128), lambda i, l: (i, 0))
    still = lambda i, l: (0, 0)
    return pl.pallas_call(
        combine_kernel,
        out_shape=[
            jax.ShapeDtypeStruct((rows, width), F32),
            jax.ShapeDtypeStruct((rows, width), BF),
            jax.ShapeDtypeStruct((width, width), BF),
            jax.ShapeDtypeStruct((8, width), F32),
        ],
        grid_spec=pltpu.PrefetchScalarGridSpec(
            num_scalar_prefetch=1,
            grid=(rows // block,),
            in_specs=[
                pl.BlockSpec((rows, width), still),
                thin,
                part,
                part,
                pl.BlockSpec((4, width), still),
                part,
                pl.BlockSpec((width, width), still),
            ],
            out_specs=[
                part,
                part,
                pl.BlockSpec((width, width), still),
                pl.BlockSpec((8, width), still),
            ],
            scratch_shapes=[pltpu.VMEM((width, width), F32)],
        ),
        compiler_params=params(60),
        cost_estimate=cost(4 * rows * (rows + width) * width, 24 * rows * width),
        name="combine",
    )(length, returned, target_column, cotangent, residual, norms, mixed, weight)


def layer_kernel(length_ref, returned_ref, column_ref, residual_ref, gate_ref, out_ref):
    term = gathered_rows(column_ref, returned_ref)
    mask = present_rows(pl.program_id(0), column_ref.shape[0], length_ref[0])
    out_ref[...] = (residual_ref[...] + mask * gate_ref[:, 0:1] * term).astype(BF)


def layer(length, returned, target_column, residual, gate):
    rows, width = residual.shape
    block = 256
    part = pl.BlockSpec((block, width), lambda i, l: (i, 0))
    thin = pl.BlockSpec((block, 128), lambda i, l: (i, 0))
    return pl.pallas_call(
        layer_kernel,
        out_shape=jax.ShapeDtypeStruct((rows, width), BF),
        grid_spec=pltpu.PrefetchScalarGridSpec(
            num_scalar_prefetch=1,
            grid=(rows // block,),
            in_specs=[pl.BlockSpec((rows, width), lambda i, l: (0, 0)), thin, part, thin],
            out_specs=part,
        ),
        compiler_params=params(60),
        cost_estimate=cost(2 * rows * rows * width, 10 * rows * width),
        name="layer",
    )(length, returned, target_column, residual, gate)


def packed_rows(share, devices):
    unit = 16 * max(1, devices // 2)
    units = -(-(4 * share + 5) // unit)
    return [-(-units // 2) * unit, units // 2 * unit]


def pack_kernel(
    me_ref,
    grads_ref,
    tokens_ref,
    norms_ref,
    output_grad_ref,
    second_ref,
    *refs,
    shares,
):
    keeps, sends, (normed, sums, product) = refs[0:2], refs[2:4], refs[4:]
    step = pl.program_id(0)
    width = tokens_ref.shape[1]
    share = width // shares
    half = width // 2
    upper = (me_ref[0] & 1) != 0

    def put(number, first, values):
        border = keeps[0].shape[1]
        low, high = values[:, :half], values[:, half:]
        keep = jnp.where(upper, high, low).astype(BF)
        send = jnp.where(upper, low, high).astype(BF)
        for stream, (begin, end) in enumerate(((0, border), (border, 1 << 30))):
            a, b = max(first, begin), min(first + values.shape[0], end)
            if a < b:
                keeps[stream][number, a - begin : b - begin, :] = keep[a - first : b - first]
                sends[stream][number, a - begin : b - begin, :] = send[a - first : b - first]

    @pl.when(step == 0)
    def _():

        @pl.loop(0, tokens_ref.shape[0] // 256)
        def _(number):
            at = pl.ds(pl.multiple_of(number * 256, 256), 256)
            normal, _ = normalise(tokens_ref[at, :].astype(F32))
            low = (normal * norms_ref[0:1, :] + norms_ref[1:2, :]).astype(BF)
            normed[:, at] = low.T

    product[...] = dot(normed[...], grads_ref[...])
    sums[pl.ds(step, 1), :] = jnp.sum(grads_ref[...].astype(F32), axis=0, keepdims=True)
    for third in range(3):

        @pl.when(step == third)
        def _(third=third):
            @pl.loop(0, shares)
            def _(number):
                first = pl.multiple_of(number * share, 16)
                put(number, third * share, product[pl.ds(first, share), :])

    @pl.when(step == pl.num_programs(0) - 1)
    def _():
        total_rows = keeps[0].shape[1] + keeps[1].shape[1]
        rest = jnp.zeros((total_rows - 4 * share - 5, width), F32)
        tail = jnp.concatenate([sums[0:3, :], second_ref[0:2, :], rest], axis=0)

        @pl.loop(0, shares)
        def _(number):
            first = pl.multiple_of(number * share, 16)
            put(number, 3 * share, output_grad_ref[pl.ds(first, share), :].astype(F32))
            put(number, 4 * share, tail)


def pack(me, grads, tokens, norms, output_grad, second, shares, devices):
    rows, width = tokens.shape
    shapes = [(shares, count, width // 2) for count in packed_rows(width // shares, devices)] * 2
    whole = lambda shape: pl.BlockSpec(shape, lambda i, m: (0,) * len(shape))
    outs = pl.pallas_call(
        functools.partial(pack_kernel, shares=shares),
        out_shape=[jax.ShapeDtypeStruct(shape, BF) for shape in shapes],
        grid_spec=pltpu.PrefetchScalarGridSpec(
            num_scalar_prefetch=1,
            grid=(3,),
            in_specs=[
                pl.BlockSpec((None, rows, width), lambda i, m: (i, 0, 0)),
                whole((rows, width)),
                whole((4, width)),
                whole((width, width)),
                whole((8, width)),
            ],
            out_specs=[whole(shape) for shape in shapes],
            scratch_shapes=[
                pltpu.VMEM((width, rows), BF),
                pltpu.VMEM((8, width), F32),
                pltpu.VMEM((width, width), F32),
            ],
        ),
        compiler_params=params(40),
        cost_estimate=cost(6 * rows * width * width, 20 * rows * width),
        name="pack",
    )(me, grads, tokens, norms, output_grad, second)
    return outs[:2], outs[2:]


def project_back_kernel(
    grads_ref, tokens_ref, residual_grad_ref, weight_ref, norms_ref, out_ref
):
    width = tokens_ref.shape[1]
    gradient = None
    for number in range(3):
        columns = slice(number * width, (number + 1) * width)
        part = dot(grads_ref[number], weight_ref[:, columns], 1, 1)
        gradient = part if gradient is None else gradient + part
    normal, inverse = normalise(tokens_ref[...].astype(F32))
    input_part = norm_backward(normal, inverse, norms_ref[0:1, :], gradient)
    out_ref[...] = (residual_grad_ref[...] + input_part).astype(BF)


def project_back(grads, tokens, residual_grad, weight, norms):
    rows, width = tokens.shape
    block = 256
    part = pl.BlockSpec((block, width), lambda i: (i, 0))
    return pl.pallas_call(
        project_back_kernel,
        out_shape=jax.ShapeDtypeStruct((rows, width), BF),
        grid=(rows // block,),
        in_specs=[pl.BlockSpec((3, block, width), lambda i: (0, i, 0)), part, part]
        + [pl.BlockSpec(weight.shape, lambda i: (0, 0)), pl.BlockSpec((4, width), lambda i: (0, 0))],
        out_specs=part,
        compiler_params=params(24),
        cost_estimate=cost(18 * rows * width * width, 60 * rows * width),
        name="project_back",
    )(grads, tokens, residual_grad, weight, norms)


def add_kernel(left_ref, right_ref, out_ref):
    out_ref[...] = (left_ref[...].astype(F32) + right_ref[...].astype(F32)).astype(BF)


def add(left, right, pieces):
    (left, i), (right, j) = left, right
    _, rows, columns = left.shape
    half = pieces // 2
    spec = lambda first: pl.BlockSpec((half, rows, columns), lambda a: (first // half + a, 0, 0))
    size = pieces * rows * columns
    return pl.pallas_call(
        add_kernel,
        out_shape=jax.ShapeDtypeStruct((pieces, rows, columns), BF),
        grid=(2,),
        in_specs=[spec(i), spec(j)],
        out_specs=spec(0),
        compiler_params=params(10),
        cost_estimate=cost(0, 0),
        name="add",
    )(left, right)


def total_kernel(place_ref, middle_ref, end_ref, *refs, across):
    arrived, out_ref = refs[:-1], refs[-1]
    end = (place_ref[0] == 0) | (place_ref[0] == LINE - 1)
    rows, columns = middle_ref.shape[1:]
    for piece in range(middle_ref.shape[0]):
        total = jnp.where(end, end_ref[piece].astype(F32), middle_ref[piece].astype(F32))
        for ref in arrived:
            total = total + ref[piece].astype(F32)
        if across:
            out_ref[:, piece * columns : (piece + 1) * columns] = total
        else:
            out_ref[piece * rows : (piece + 1) * rows, :] = total


def line_total(place, middle, end, arrived, across):
    ins = [middle, end, *arrived]
    pieces, rows, columns = middle[0].shape
    shape = (rows, pieces * columns) if across else (pieces * rows, columns)
    half = pieces // 2
    block = (rows, half * columns) if across else (half * rows, columns)
    spec = lambda first: pl.BlockSpec((half, rows, columns), lambda a, p: (first // half + a, 0, 0))
    return pl.pallas_call(
        functools.partial(total_kernel, across=across),
        out_shape=jax.ShapeDtypeStruct(shape, F32),
        grid_spec=pltpu.PrefetchScalarGridSpec(
            num_scalar_prefetch=1,
            grid=(2,),
            in_specs=[spec(first) for _, first in ins],
            out_specs=pl.BlockSpec(block, lambda a, p: (0, a) if across else (a, 0)),
        ),
        compiler_params=params(60),
        cost_estimate=cost(0, 0),
        name="line_total",
    )(place, *[array for array, _ in ins])


class LineSum:
    def __init__(self, pairs, axis, place):
        self.axis, self.place = axis, place
        self.shares = lax.axis_size(axis)
        self.pairs = pairs
        self.line = self.shares == LINE and pairs[0][0][0] is pairs[0][1][0]
        self.got = {}

    def send(self, name, matrix=None):
        if not self.line:
            return
        ends = [(0, 1), (3, 2)]
        middles = [(1, 2), (2, 1)]
        out = [(2, 3), (1, 0)]

        def plus(number, before):
            if matrix is None:
                own = (self.pairs[number][0][0], 0)
                return add(own, (self.got[before], 0), own[0].shape[0])
            own = self.pairs[number][matrix]
            return add(own, (self.got[before], own[1]), self.pairs[MIDDLE][matrix][0].shape[0])

        values, route = {
            "far": lambda: (self.pairs[0][0][0], ends),
            "near": lambda: (self.pairs[1][0][0], ends),
            "own": lambda: (self.pairs[MIDDLE][matrix][0], ends),
            "far_on": lambda: (plus(0, "far"), middles),
            "near_on": lambda: (plus(1, "near"), middles),
            "far_out": lambda: (plus(3, "far_on"), out),
        }[name]()
        key = name if matrix is None else (name, matrix)
        self.got[key] = lax.ppermute(values, self.axis, route)

    def hold(self, name, values):
        if not self.line:
            return values
        self.got[name], values = lax.optimization_barrier((self.got[name], values))
        return values

    def totals(self):
        if self.line:
            sums = []
            for matrix in range(2):
                arrived = [(self.got[name, matrix], 0) for name in ("own", "near_on", "far_out")]
                ins = self.pairs[2][matrix], self.pairs[3][matrix]
                sums.append(line_total(self.place, *ins, arrived, across=matrix == 1))
            return sums
        sums = []
        for matrix in range(2):
            stacked = jnp.stack([pair[matrix][0] for pair in self.pairs])
            total = lax.psum_scatter(stacked, self.axis, scatter_dimension=0).astype(F32)
            pieces, rows, columns = total.shape
            if matrix:
                sums.append(total.swapaxes(0, 1).reshape(rows, pieces * columns))
            else:
                sums.append(total.reshape(pieces * rows, columns))
        return sums


def partner_pairs(axis, bit):
    return [(i, i ^ bit) for i in range(lax.axis_size(axis))]


def halves_kernel(me_ref, *refs, edges, bits):
    streams = len(bits)
    ins, outs = refs[: len(refs) - 2 * streams], refs[len(refs) - 2 * streams :]
    for stream, (first, last) in enumerate(edges):
        keep, got = ins[:2] if len(ins) == 2 else ins[2 * stream : 2 * stream + 2]
        kept, sent = outs[2 * stream : 2 * stream + 2]
        size = (last - first) // 2
        upper = (me_ref[0] // bits[stream]) % 2
        mine = pl.multiple_of(first + upper * size, 16)
        other = pl.multiple_of(first + (1 - upper) * size, 16)
        for at, out in ((mine, kept), (other, sent)):
            total = keep[:, pl.ds(at, size), :].astype(F32) + got[:, pl.ds(at, size), :].astype(F32)
            out[...] = total.astype(BF)


def halves(me, bits, edges, pairs, level):
    shares = pairs[0][0].shape[0]
    spec = lambda rows, columns: pl.BlockSpec((1, rows, columns), lambda z, m: (z, 0, 0))
    in_specs, out_specs, out_shape = [], [], []
    for keep, _ in pairs:
        in_specs += [spec(*keep.shape[1:])] * 2
    columns = pairs[0][0].shape[2]
    for first, last in edges:
        rows = (last - first) // 2
        out_specs += [spec(rows, columns)] * 2
        out_shape += [jax.ShapeDtypeStruct((shares, rows, columns), BF)] * 2
    size = sum(keep.size for keep, _ in pairs)
    outs = pl.pallas_call(
        functools.partial(halves_kernel, edges=edges, bits=bits),
        out_shape=out_shape,
        grid_spec=pltpu.PrefetchScalarGridSpec(
            num_scalar_prefetch=1, grid=(shares,), in_specs=in_specs, out_specs=out_specs
        ),
        compiler_params=params(20),
        cost_estimate=cost(0, 0 * size * level),
        name="halves",
    )(me, *[array for pair in pairs for array in pair])
    return [(outs[2 * i], outs[2 * i + 1]) for i in range(len(bits))]


def join_kernel(*refs):
    ins, out_ref = refs[:-1], refs[-1]
    first = 0
    for keep, got in zip(ins[::2], ins[1::2]):
        last = first + keep.shape[1]
        total = keep[...].astype(F32) + got[...].astype(F32)
        out_ref[:, first:last, :] = total.astype(BF)
        first = last


def join(pairs):
    shares, _, columns = pairs[0][0].shape
    rows = sum(keep.shape[1] for keep, _ in pairs)
    size = shares * rows * columns
    return pl.pallas_call(
        join_kernel,
        out_shape=jax.ShapeDtypeStruct((shares, rows, columns), BF),
        compiler_params=params(12),
        cost_estimate=cost(0, 0),
        name="join",
    )(*[array for pair in pairs for array in pair])


def spread_kernel(parts_ref, out_ref):
    total = jnp.sum(parts_ref[...].astype(F32), axis=0).astype(BF)
    for number in range(out_ref.shape[0]):
        out_ref[number] = total


def spread(parts, devices):
    _, rows, columns = parts.shape
    size = parts.size + devices * rows * columns
    return pl.pallas_call(
        spread_kernel,
        out_shape=jax.ShapeDtypeStruct((devices, rows, columns), BF),
        compiler_params=params(12),
        cost_estimate=cost(0, 0),
        name="spread",
    )(parts)


def assemble_kernel(
    place_ref,
    gathered_ref,
    weight_ref,
    norms_ref,
    input_ref,
    output_ref,
    column_ref,
    tail_ref,
    summed,
    *,
    sources,
):
    half = gathered_ref.shape[2]
    share, width = output_ref.shape
    for device, first, count, to, side in sources:
        values = gathered_ref[device, first : first + count, :].astype(F32)
        summed[to : to + count, side * half : (side + 1) * half] = values
    shift_sum = gain_sum = 0.0
    for third in range(3):
        columns = slice(third * width, (third + 1) * width)
        values = summed[third * share : (third + 1) * share, :]
        input_ref[:, columns] = values
        weight = weight_ref[:, columns].astype(F32)
        line = summed[4 * share + third : 4 * share + third + 1, :]
        shift_sum = shift_sum + jnp.sum(weight * line, axis=1, keepdims=True)
        gain_sum = gain_sum + jnp.sum(weight * values, axis=1, keepdims=True)
    output_ref[...] = summed[3 * share : 4 * share, :]
    lane = lax.broadcasted_iota(jnp.int32, (1, 128), 1)
    column_ref[...] = jnp.where(lane == 0, gain_sum, shift_sum)
    tail_ref[...] = summed[4 * share : 4 * share + 8, :]


def assemble(place, gathered, weight, norms, share, orders, streams):
    devices, _, half = gathered.shape
    width = 2 * half
    levels = len(orders[0])
    sources = []
    for side in range(2):
        first, to = 0, 0
        for count, order in zip(streams, orders):
            for number in range(2**levels):
                digits = [(number >> (levels - 1 - level)) & 1 for level in range(levels)]
                device = side + sum(digit * bit for digit, bit in zip(digits, order))
                sources.append((device, first, count, to, side))
                to += count
            first += count
    total = sum(streams) * 2**levels
    whole = lambda shape: pl.BlockSpec(shape, lambda i, p: (0,) * len(shape))
    return pl.pallas_call(
        functools.partial(assemble_kernel, sources=sources),
        out_shape=[
            jax.ShapeDtypeStruct((share, 3 * width), F32),
            jax.ShapeDtypeStruct((share, width), F32),
            jax.ShapeDtypeStruct((share, 128), F32),
            jax.ShapeDtypeStruct((8, width), F32),
        ],
        grid_spec=pltpu.PrefetchScalarGridSpec(
            num_scalar_prefetch=1,
            grid=(1,),
            in_specs=[
                whole(gathered.shape),
                pl.BlockSpec((share, 3 * width), lambda i, p: (p[0], 0)),
                whole(norms.shape),
            ],
            out_specs=[
                whole((share, 3 * width)),
                whole((share, width)),
                whole((share, 128)),
                whole((8, width)),
            ],
            scratch_shapes=[pltpu.VMEM((total, width), F32)],
        ),
        compiler_params=params(24),
        cost_estimate=cost(0, 0),
        name="assemble",
    )(place, gathered, weight, norms)


def on_device(
    tokens,
    lengths,
    expert_index,
    centroids,
    input_weight,
    output_weight,
    first_gain,
    first_shift,
    second_gain,
    second_shift,
    up_weight,
    down_weight,
    cotangent,
):
    rows, width = tokens.shape
    experts = centroids.shape[0]
    capacity = rows // experts
    shares = lax.axis_size("dp")
    share = width // shares
    me = lax.axis_index("expert").reshape(1).astype(jnp.int32)
    place = lax.axis_index("dp").reshape(1).astype(jnp.int32)
    norms = jnp.stack([first_gain, first_shift, second_gain, second_shift])

    def exchange(values, axis="expert"):
        return lax.all_to_all(values, axis, split_axis=0, concat_axis=0, tiled=True)

    def dispatch(values):
        return exchange(values.reshape(experts, capacity, -1)).reshape(rows, -1)

    outgoing_cotangent, target_row, target_column = route(
        lengths, expert_index, cotangent, experts
    )
    arrived_cotangent = dispatch(outgoing_cotangent)
    held_tokens, target_row = lax.optimization_barrier((tokens, target_row))
    projected = project(held_tokens, input_weight, norms)
    mixed, total = attend(lengths, projected)
    mixed, arrived_cotangent = lax.optimization_barrier((mixed, arrived_cotangent))
    residual, gate, outgoing = hidden_rows(
        lengths, mixed, tokens, output_weight, norms, centroids, target_row, target_column
    )
    arrived = dispatch(outgoing)
    order = place if shares == LINE else jnp.full_like(place, shares)
    produced, back, pairs = expert(
        me, order, arrived, arrived_cotangent, centroids, up_weight[0], down_weight[0], shares
    )
    line = LineSum(pairs, "dp", place)
    line.send("far")
    line.send("near")
    produced, returned = lax.optimization_barrier((produced, dispatch(back)))
    residual_grad, mixed_grad, output_grad, second_gains = combine(
        lengths, returned, target_column, cotangent, residual, norms, mixed, output_weight
    )
    produced, mixed_grad = lax.optimization_barrier((produced, mixed_grad))
    returned = dispatch(produced)
    mixed_grad = line.hold("far", mixed_grad)
    line.send("far_on")
    grads = attend_back(lengths, projected, mixed, total, mixed_grad)
    grads, returned = lax.optimization_barrier((grads, returned))
    keeps, sends = pack(
        me, grads, tokens, norms, output_grad, second_gains, shares, experts
    )
    swap = lambda values, bit: lax.ppermute(values, "expert", partner_pairs("expert", bit))
    pairs = [(keep, swap(send, 1)) for keep, send in zip(keeps, sends)]
    bits = [2**i for i in range(1, (experts - 1).bit_length())]
    orders = [bits, bits[::-1]]
    for level, now in enumerate(zip(*orders)):
        made = halves(me, now, [(0, keep.shape[1]) for keep, _ in pairs], pairs, level)
        pairs = [(kept, swap(sent, bit)) for (kept, sent), bit in zip(made, now)]
        if level == 0:
            kept, got = pairs[0]
            kept = line.hold("near", kept)
            line.send("own", 0)
            line.send("near_on", 0)
            kept = line.hold("far_on", kept)
            line.send("far_out", 0)
            pairs[0] = (kept, got)
    input_gradient = project_back(grads, tokens, residual_grad, input_weight, norms)
    input_gradient, pairs = lax.optimization_barrier((input_gradient, pairs))
    for name in ("far_out", "near_on", "own"):
        pairs = line.hold((name, 0), pairs)
    streams = [keep.shape[1] for keep, _ in pairs]
    joined = join(pairs)
    joined, returned = lax.optimization_barrier((joined, returned))
    over_line = exchange(joined, "dp")
    layer_output = layer(lengths, returned, target_column, residual, gate)
    for name in ("far_out", "near_on", "own"):
        line.send(name, 1)
    gathered = exchange(spread(over_line, experts))
    input_share, output_share, sums, tail = assemble(
        place, gathered, input_weight, norms, share, orders, streams
    )
    for name in ("far_out", "near_on", "own"):
        sums = line.hold((name, 1), sums)
    begin = lax.axis_index("dp") * share
    mine = lambda vector: lax.dynamic_slice_in_dim(vector, begin, share, vector.ndim - 1)
    shift_sum = sums[:, 1]
    gain_sum = (sums[:, 0] - mine(first_shift) * shift_sum) / mine(first_gain)
    second = mine(tail[3:5])
    down_share, up_share = line.totals()
    return (
        layer_output,
        input_gradient,
        input_share,
        output_share,
        gain_sum,
        shift_sum,
        second[0],
        second[1],
        up_share[None],
        down_share[None],
    )


def solution(mesh):
    both = P(("dp", "expert"))
    rows = P(("dp", "expert"), None)
    weights = P("expert", None, None)
    return jax.shard_map(
        on_device,
        mesh=mesh,
        in_specs=(rows, both, both, P(), P(), P(), P(), P(), P(), P(), weights, weights, rows),
        out_specs=(
            rows,
            rows,
            P("dp", None),
            P("dp", None),
            P("dp"),
            P("dp"),
            P("dp"),
            P("dp"),
            P("expert", "dp", None),
            P("expert", "dp", None),
        ),
        check_vma=False,
    )
```
